32 devices in a mesh: freq: 2 (over y), facet: 16 (over z, x, core).
Axes of the slice: x: 2, y: 2, z: 4, core: 2. Of those that a mesh axis runs over, the one named last changes fastest.
Arguments:
- sky_image: float32 [1024, 2048], P('facet'), may hold values from -6 to 6
- primary_beam: float32 [2, 1024, 2048], P('freq', 'facet'), may hold values from 0.1 to 1
- observed: bfloat16 [8192, 512], P(('freq', 'facet')), may hold values from -6 to 6
- facet_of: int32 [8192], P(('freq', 'facet')), may hold values from 0 to 15, as said below
- tile_slot: int32 [8192], P(('freq', 'facet')), may hold values from 0 to 511
- conv_first: float32 [32, 3, 3], replicated, may hold values from -2 to 2
- bias_first: float32 [32], replicated, may hold values from -3 to 3
- conv_second: float32 [32, 3, 3], replicated, may hold values from -0.375 to 0.375
Outputs:
- residual_tiles: bfloat16 [8192, 512], P(('freq', 'facet'))
- image_next: float32 [1024, 2048], P('facet', 'freq')
The draws below stay inside these ranges and needn't reach their ends.
Inputs may be any that keep to these rules, and one draw needn't show every extreme that they name: `facet_of`: at most 32 of one device's tiles name one facet; in every frequency group some facet is named by exactly 32 tiles of every device of the group.
All inputs are finite; a program needn't handle non-finite values.
Results may differ from the reference program's by a relative error of at most 0.002.
Values may be sent and summed in bfloat16 or wider, within the bound.
No kernel may reach another device: no remote copies, remote signals or barrier semaphores. Data moves between devices by JAX's collectives and lax.ppermute only.
A program may use at most 64 MiB of HBM per device.

```python
import math
import jax
import jax.numpy as jnp
from jax import lax

FR = 64
FC = 2048
S = 16
HID = 32
TILE_DEV = 256
CHANNELS = 2
FACETS = 16
IMG_ROWS = 1024
SLOTS = 512
CAP = 32
TILES = 8192
N_FREQ = 2
N_FACET = 16


def draw_facet_of(key, part):
    devices = TILES // TILE_DEV
    groups = devices // FACETS
    key_hot, key_pref, key_rest = jax.random.split(key, 3)
    hottest = jax.random.randint(key_hot, (groups,), 0, FACETS)
    preference = jax.random.randint(key_pref, (groups, FACETS), 0, 4)
    entries = jnp.arange(FACETS * CAP, dtype=jnp.int32)
    owners = entries // CAP

    def one_device(device_index):
        group_index = device_index // FACETS
        device_key = jax.random.fold_in(key_rest, device_index)
        key_score, key_perm = jax.random.split(device_key)
        jitter = jax.random.randint(key_score, (FACETS * CAP,), 0, 4096)
        scores = preference[group_index][owners] * 16777216 + jitter * 2048 + entries
        scores = jnp.where(owners == hottest[group_index], 1073741824 + entries, scores)
        ranking = jnp.argsort(-scores, stable=True)
        chosen = owners[ranking[:TILE_DEV]]
        return jax.random.permutation(key_perm, chosen)
    return jax.vmap(one_device)(jnp.arange(devices, dtype=jnp.int32)).reshape(TILES)


def place_ends(array, stream_key, low, high):
    dims = array.shape
    index_at = [jax.random.randint(jax.random.fold_in(stream_key, axis), (), 0, dims[axis]) for axis in range(len(dims))]
    array = array.at[tuple(index_at)].set(low)
    longest = dims.index(max(dims))
    index_at[longest] = (index_at[longest] + 1) % dims[longest]
    return array.at[tuple(index_at)].set(high)


def shard_levels(stream_key, shape, cuts, low, largest):
    gain = 1.0
    for dim, shards_of in cuts:
        draws = jax.random.uniform(jax.random.fold_in(jax.random.fold_in(stream_key, 6), dim), (shards_of,), jnp.float32, low / len(cuts), largest / len(cuts))
        gain = gain * jnp.repeat(jnp.exp(draws), shape[dim] // shards_of).reshape((-1,) + (1,) * (len(shape) - 1 - dim))
    return gain


def normal_values(own_key, shape, spread, most, cuts=(), kind=jnp.bfloat16):
    drawn = jax.random.normal(own_key, shape, jnp.float32) * spread
    if len(cuts) > 0:
        drawn = shard_levels(own_key, shape, cuts, -0.22, 0.18) * drawn
    return jnp.clip(drawn, min=-most, max=most).astype(kind)


def setup_inputs(seed: int = 0) -> dict:
    key_list = jax.random.split(jax.random.key(seed), 9)
    return {
        "sky_image": normal_values(key_list[0], (IMG_ROWS, FC), 1.0, 6.0, ((0, 16),), jnp.float32),
        "primary_beam": jnp.clip(jnp.exp(math.log(1.0) - 2.3025851 * jax.random.uniform(key_list[1], (CHANNELS, IMG_ROWS, FC), jnp.float32) ** shard_levels(key_list[1], (CHANNELS, IMG_ROWS, FC), ((0, 2), (1, 16)), -0.2, 0.2)), 0.1, 1.0),
        "observed": normal_values(key_list[2], (TILES, 2 * S * S), 1.0, 6.0, ((0, 32),)),
        "facet_of": draw_facet_of(jax.random.fold_in(key_list[8], 71), 0),
        "tile_slot": place_ends(jax.random.randint(key_list[4], (TILES,), 0, SLOTS), jax.random.fold_in(key_list[4], 1), 0, SLOTS - 1).astype(jnp.int32),
        "conv_first": normal_values(key_list[5], (HID, 3, 3), 9 ** -0.5, 2.0, (), jnp.float32),
        "bias_first": normal_values(key_list[6], (HID,), 0.5, 3.0, (), jnp.float32),
        "conv_second": normal_values(key_list[7], (HID, 3, 3), (HID * 9) ** -0.5, 0.375, (), jnp.float32),
    }


step_size = 0.5


def to_tiles(real_part, imag_part):
    leading = real_part.shape[:-2]
    row_count, col_count = real_part.shape[-2:]
    lead_len = len(leading)
    stacked = jnp.stack([real_part, imag_part], axis=-3)
    stacked = stacked.reshape(leading + (2, row_count // S, S, col_count // S, S))
    stacked = jnp.transpose(stacked, tuple(range(lead_len)) + (lead_len + 1, lead_len + 3, lead_len, lead_len + 2, lead_len + 4))
    return stacked.reshape(leading + ((row_count // S) * (col_count // S), 2 * S * S))


def from_tiles(tiles, row_count, col_count):
    leading = tiles.shape[:-2]
    lead_len = len(leading)
    stacked = tiles.reshape(leading + (row_count // S, col_count // S, 2, S, S))
    stacked = jnp.transpose(stacked, tuple(range(lead_len)) + (lead_len + 2, lead_len, lead_len + 3, lead_len + 1, lead_len + 4))
    stacked = stacked.reshape(leading + (2, row_count, col_count))
    return stacked[..., 0, :, :], stacked[..., 1, :, :]


def prior_global(shifted, conv_first, bias_first, conv_second):
    row_count, col_count = shifted.shape
    padded = jnp.pad(shifted, 2)
    inside = jnp.pad(jnp.ones(shifted.shape, shifted.dtype), 1)

    def add_channel(summed, weights):
        first_w, bias_w, second_w = weights
        hidden = jnp.zeros((row_count + 2, col_count + 2), shifted.dtype)
        for row_off in range(3):
            for col_off in range(3):
                hidden = hidden + first_w[row_off, col_off] * padded[row_off:row_off + row_count + 2, col_off:col_off + col_count + 2]
        hidden = jax.nn.relu(hidden + bias_w) * inside
        for row_off in range(3):
            for col_off in range(3):
                summed = summed + second_w[row_off, col_off] * hidden[row_off:row_off + row_count, col_off:col_off + col_count]
        return summed, None

    summed, unused = lax.scan(add_channel, jnp.zeros_like(shifted), (conv_first, bias_first, conv_second))
    return shifted + summed


def reference(sky_image, primary_beam, observed, facet_of, tile_slot, conv_first, bias_first, conv_second):
    per_group = TILE_DEV * N_FACET
    gradient = jnp.zeros((IMG_ROWS, FC), jnp.float32)
    residual_parts = []
    image_blocks = sky_image.reshape(N_FACET, FR, FC)
    for channel in range(N_FREQ):
        beam_blocks = primary_beam[channel].reshape(N_FACET, FR, FC)
        spectrum = jnp.fft.fft2(beam_blocks * image_blocks, norm="ortho")
        model_tiles = to_tiles(jnp.real(spectrum), jnp.imag(spectrum))
        facet_ids = facet_of[channel * per_group:(channel + 1) * per_group]
        slot_ids = tile_slot[channel * per_group:(channel + 1) * per_group]
        predicted = model_tiles[facet_ids, slot_ids]
        seen = observed[channel * per_group:(channel + 1) * per_group].astype(jnp.float32)
        residual = (predicted - seen).astype(jnp.bfloat16)
        gridded = jnp.zeros(model_tiles.shape, jnp.float32).at[facet_ids, slot_ids].add(residual.astype(jnp.float32))
        grid_real, grid_imag = from_tiles(gridded, FR, FC)
        back_real = jnp.real(jnp.fft.ifft2(grid_real + 1j * grid_imag, norm="ortho"))
        gradient = gradient + (beam_blocks * back_real).reshape(IMG_ROWS, FC)
        residual_parts.append(residual)
    shifted = sky_image - step_size * gradient
    image_next = prior_global(shifted, conv_first, bias_first, conv_second)
    return jnp.concatenate(residual_parts, axis=0), image_next
```

```python
import functools
import math

import jax
import jax.numpy as jnp
import numpy as np
from jax import lax
from jax.experimental import pallas as pl
from jax.experimental.pallas import tpu as pltpu
from jax.sharding import PartitionSpec as P

S = 16
LANES = 128
BAND = 22
STEP = 0.5
F32 = jnp.float32
BF16 = jnp.bfloat16


def iota(shape, dim):
    return lax.broadcasted_iota(jnp.int32, shape, dim)


def mm(a, b, dims=((1,), (0,))):
    return lax.dot_general(a, b, (dims, ((), ())), preferred_element_type=F32)


def one_hot(cond):
    return jnp.where(cond, 1.0, 0.0).astype(BF16)


def split(x):
    high = x.astype(BF16)
    return high, (x - high.astype(F32)).astype(BF16)


def np_split(x):
    x = np.asarray(x, np.float32)
    high = x.astype(BF16)
    return high, (x - high.astype(np.float32)).astype(BF16)


def tables(rows, cols, sign):
    outer = cols // LANES
    scale = 1.0 / math.sqrt(rows * cols)
    k = np.arange(rows)
    angle = sign * 2.0 * np.pi * ((k[:, None] * k[None, :]) % rows) / rows
    cos_r, sin_r = np.cos(angle) * scale, np.sin(angle) * scale
    if sign < 0:
        row_high, row_low = np_split(np.concatenate([cos_r, sin_r], 0))
        row = np.concatenate([row_high, row_high, row_low], 1)
    else:
        row_high, row_low = np_split(np.concatenate([cos_r, -sin_r], 1))
        row = np.concatenate([row_high, row_high, row_low], 1)
    i2 = np.arange(LANES)
    w = np.arange(outer)
    twist = sign * 2.0 * np.pi * ((w[:, None] * i2[None, :]) % cols) / cols
    inner = sign * 2.0 * np.pi * ((i2[:, None] * i2[None, :]) % LANES) / LANES
    c, s = np.cos(inner), np.sin(inner)
    mat_high, mat_low = np_split(np.block([[c, s], [-s, c]]))
    return (
        row,
        np.stack([np.cos(twist), np.sin(twist)]).astype(np.float32),
        np.stack([mat_high, mat_low]),
    )


def times_i(z, sign):
    re, im = z
    return (-im, re) if sign > 0 else (im, -re)


def add(a, b):
    return (a[0] + b[0], a[1] + b[1])


def sub(a, b):
    return (a[0] - b[0], a[1] - b[1])


def dft4(x, sign):
    s0, s1 = add(x[0], x[2]), sub(x[0], x[2])
    s2, s3 = add(x[1], x[3]), times_i(sub(x[1], x[3]), sign)
    return [add(s0, s2), add(s1, s3), sub(s0, s2), sub(s1, s3)]


def dft16(x, sign):
    mid = [dft4([x[4 * a + b] for a in range(4)], sign) for b in range(4)]
    out = [None] * 16
    for c in range(4):
        turned = []
        for b in range(4):
            re, im = mid[b][c]
            phase = (b * c) % 16
            if phase == 0:
                turned.append((re, im))
            elif phase == 4:
                turned.append(times_i((re, im), sign))
            else:
                wr = math.cos(2.0 * math.pi * phase / 16)
                wi = sign * math.sin(2.0 * math.pi * phase / 16)
                turned.append((re * wr - im * wi, re * wi + im * wr))
        for d, value in enumerate(dft4(turned, sign)):
            out[c + 4 * d] = value
    return out


def swap_matrix(size):
    src = iota((1, size), 1)
    swapped = (src & -256) | ((src & 15) << 4) | ((src >> 4) & 15)
    return one_hot(iota((size, size), 0) == swapped)


def pack_kernel(facets, cap, facet_ref, slot_ref, seen_ref, send_ref, dest_ref):
    tiles, width = seen_ref.shape
    total = facets * cap
    facet = facet_ref[...]
    member = iota((facets, tiles), 0) == facet
    member_f = jnp.where(member, 1.0, 0.0)
    before = one_hot(iota((tiles, tiles), 0) < iota((tiles, tiles), 1))
    ranks = mm(member_f.astype(BF16), before)
    rank = jnp.sum(member_f * ranks, axis=0, keepdims=True).astype(jnp.int32)
    dest = facet * cap + rank
    dest_ref[...] = dest
    placing = one_hot(iota((total, tiles), 0) == dest)
    turned = mm(seen_ref[...], swap_matrix(width)).astype(BF16)
    packed = mm(placing, turned).astype(BF16)
    code = slot_ref[...] + 1
    lane = iota((LANES, tiles), 0)
    slots = mm(
        (member_f * (code >> 4).astype(F32)).astype(BF16), one_hot(lane == rank), ((1,), (1,))
    ) + mm(
        (member_f * (code & 15).astype(F32)).astype(BF16),
        one_hot(lane - LANES // 2 == rank),
        ((1,), (1,)),
    )
    parts = width // LANES
    for d in range(facets):
        for part in range(parts):
            send_ref[d, part * cap : (part + 1) * cap, :] = packed[
                d * cap : (d + 1) * cap, part * LANES : (part + 1) * LANES
            ]
        send_ref[d, parts * cap : parts * cap + 8, :] = jnp.broadcast_to(
            slots[d : d + 1, :], (8, LANES)
        ).astype(BF16)


def forward_kernel(sky_ref, beam_ref, row_ref, twist_ref, mat_ref, high_ref, low_ref):
    rows, cols = sky_ref.shape
    outer = cols // LANES
    weighted = sky_ref[...] * beam_ref[...]
    w_high, w_low = split(weighted)
    mid = mm(row_ref[...], jnp.concatenate([w_high, w_low, w_high], axis=0))
    lines = [
        (
            mid[:rows, i * LANES : (i + 1) * LANES],
            mid[rows:, i * LANES : (i + 1) * LANES],
        )
        for i in range(outer)
    ]
    spread = dft16(lines, -1)
    blocks = []
    for w in range(outer):
        re, im = spread[w]
        tr, ti = twist_ref[0, w : w + 1, :], twist_ref[1, w : w + 1, :]
        blocks.append(jnp.concatenate([re * tr - im * ti, re * ti + im * tr], axis=1))
    high, low = split(jnp.concatenate(blocks, axis=0))
    mat_high, mat_low = mat_ref[0], mat_ref[1]
    model = mm(high, mat_high) + mm(low, mat_high) + mm(high, mat_low)
    for w in range(outer):
        for r in range(rows // S):
            for e in range(2):
                piece = model[
                    w * rows + r * S : w * rows + (r + 1) * S, e * LANES : (e + 1) * LANES
                ]
                piece_high, piece_low = split(piece)
                at = (pl.ds(e * 256 + w * S, S), pl.ds(r * LANES, LANES))
                high_ref[at] = piece_high
                low_ref[at] = piece_low


def residual_kernel(facets, cap, got_ref, high_ref, low_ref, res_ref, sel_ref):
    total = facets * cap
    slots = high_ref.shape[1]
    parts = high_ref.shape[0] // LANES
    code = got_ref[:, parts * cap : parts * cap + 8, :].astype(F32).reshape(facets * 8, LANES)
    source = iota((total, facets * 8), 0) // cap
    spread = mm(one_hot(iota((total, facets * 8), 1) == source * 8), code.astype(BF16))
    lane = iota((total, LANES), 1)
    rank = iota((total, LANES), 0) % cap
    kept = jnp.where((lane & (LANES // 2 - 1)) == rank, spread, 0.0).astype(BF16)
    digit = jnp.where(iota((LANES, slots), 0) < LANES // 2, 16.0, 1.0).astype(BF16)
    code_all = mm(kept, digit)
    sel = one_hot(code_all.astype(jnp.int32) == iota((total, slots), 1) + 1)
    sel_ref[...] = sel
    contract = ((1,), (1,))
    predicted = mm(sel, high_ref[...], contract) + mm(sel, low_ref[...], contract)
    for part in range(parts):
        cols = slice(part * LANES, (part + 1) * LANES)
        seen = got_ref[:, part * cap : (part + 1) * cap, :].astype(F32).reshape(total, LANES)
        res_ref[:, cols] = (predicted[:, cols] - seen).astype(BF16)


def window(index, count, cols):
    part = cols // count
    width = min(cols, part + (LANES if count == 2 else 2 * LANES))
    return jnp.clip(index * part - LANES, 0, cols - width), width


def inverse_kernel(count, res_ref, sel_ref, sky_ref, beam_ref, row_ref, twist_ref, mat_ref, keep_ref, *out_refs):
    rows, cols = sky_ref.shape
    outer = cols // LANES
    send_refs = out_refs[: count - 1]
    up_refs = out_refs[count - 1 : 2 * count - 1]
    down_refs = out_refs[2 * count - 1 : 3 * count - 1]
    shift_ref, rim_ref = out_refs[3 * count - 1 :]
    grid = mm(res_ref[...], sel_ref[...], ((0,), (0,)))
    blocks = []
    for w in range(outer):
        blocks.append(
            jnp.concatenate(
                [
                    jnp.concatenate(
                        [
                            grid[
                                e * 256 + w * S : e * 256 + (w + 1) * S,
                                r * LANES : (r + 1) * LANES,
                            ]
                            for e in range(2)
                        ],
                        axis=1,
                    )
                    for r in range(rows // S)
                ],
                axis=0,
            )
        )
    high, low = split(jnp.concatenate(blocks, axis=0))
    mat_high, mat_low = mat_ref[0], mat_ref[1]
    mid = mm(high, mat_high) + mm(low, mat_high) + mm(high, mat_low)
    lines = []
    for w in range(outer):
        re = mid[w * rows : (w + 1) * rows, :LANES]
        im = mid[w * rows : (w + 1) * rows, LANES:]
        tr, ti = twist_ref[0, w : w + 1, :], twist_ref[1, w : w + 1, :]
        lines.append((re * tr - im * ti, re * ti + im * tr))
    spread = dft16(lines, 1)
    stacked = jnp.concatenate(
        [
            jnp.concatenate([z[0] for z in spread], axis=1),
            jnp.concatenate([z[1] for z in spread], axis=1),
        ],
        axis=0,
    )
    high, low = split(stacked)
    back = mm(row_ref[...], jnp.concatenate([high, low, high], axis=0))
    shift = back * beam_ref[...] * (-STEP)
    me = lax.axis_index("freq")
    shift_ref[...] = shift
    rim_ref[...] = shift + sky_ref[...] * jnp.where(me == 0, 1.0, 0.0)
    for d in range(count):
        start, width = window(lax.rem(me + d, count), count, cols)
        at = pl.ds(pl.multiple_of(start, LANES), width)
        if d == 0:
            keep_ref[...] = shift_ref[:, at] + sky_ref[:, at]
        else:
            send_refs[d - 1][...] = shift_ref[:, at].astype(BF16)
        up_refs[d][...] = rim_ref[0:2, at]
        down_refs[d][...] = rim_ref[rows - 2 : rows, at]


def prepare_kernel(first_ref, bias_ref, second_ref, one_ref, two_ref):
    hidden = first_ref.shape[0]
    taps = first_ref.shape[1]
    height = one_ref.shape[0]
    depth = one_ref.shape[1]
    bands, out_rows, _ = two_ref.shape
    rows = out_rows // 3
    high, low = split(first_ref[...])
    bias_high, bias_low = split(bias_ref[...])
    pick = one_hot((iota((height, hidden), 0) & (hidden - 1)) == iota((height, hidden), 1))
    y = iota((height, depth), 0) // hidden
    lane = iota((height, depth), 1)
    yin = lane - (lane * 2731 >> 16) * (BAND + 2)
    full = (BAND + 2) * 9
    table = jnp.zeros((height, depth), F32)
    row_high = mm(pick, high).astype(BF16)
    row_low = mm(pick, low).astype(BF16)
    tap = iota((taps, depth), 0)
    group = iota((taps, depth), 1) * 2731 >> 16
    term = group * 86 >> 8
    col = group - term * 3
    for a in range(3):
        match = tap == a * 3 + col
        value = mm(row_high, one_hot(match & (term < 2))) + mm(row_low, one_hot(match & (term == 2)))
        table = table + jnp.where((yin - y == a) & (lane < full), value, 0.0)
    ones = jnp.zeros((hidden, depth), BF16)
    bias_lane = iota((hidden, depth), 1)
    spread_high = jnp.where(bias_lane == full, bias_high.astype(F32), 0.0)
    spread_low = jnp.where(bias_lane == full + 1, bias_low.astype(F32), 0.0)
    table = table + mm(pick, (spread_high + spread_low).astype(BF16))
    one_ref[...] = table.astype(BF16)

    place = lax.axis_index("facet")
    last = lax.axis_size("facet") - 1
    wide = two_ref.shape[2]
    expand = one_hot(iota((hidden, wide), 0) == (iota((hidden, wide), 1) & (hidden - 1)))
    second = second_ref[...].astype(BF16)
    tapped = mm(second, expand, ((0,), (0,))).astype(BF16)
    out_tap = iota((out_rows, taps), 1)
    out_col = iota((out_rows, taps), 0) // rows
    values = [mm(one_hot(out_tap == a * 3 + out_col), tapped) for a in range(3)]
    y_out = iota((out_rows, wide), 0) & (rows - 1)
    y_band = iota((out_rows, wide), 1) // hidden
    for k in range(bands):
        y_hid = y_band + k * BAND
        outside = ((y_hid == 0) & (place == 0)) | ((y_hid == rows + 1) & (place == last))
        total = jnp.zeros((out_rows, wide), F32)
        for a in range(3):
            total = total + jnp.where(y_hid - y_out == a, values[a], 0.0)
        two_ref[k] = jnp.where(outside, 0.0, total).astype(BF16)


def prior_kernel(count, part, keep_ref, *refs):
    got_refs = refs[: count - 1]
    top_refs = refs[count - 1 : 2 * count - 1]
    bottom_refs = refs[2 * count - 1 : 3 * count - 1]
    one_ref, two_ref, out_ref, base_ref = refs[3 * count - 1 :]
    rows, width = keep_ref.shape
    main = keep_ref[...]
    for ref in got_refs:
        main = main + ref[...].astype(F32)
    top, bottom = top_refs[0][...], bottom_refs[0][...]
    for ref in top_refs[1:]:
        top = top + ref[...]
    for ref in bottom_refs[1:]:
        bottom = bottom + ref[...]
    base_ref[0:8, :] = jnp.zeros((8, width), F32)
    base_ref[rows + 8 : rows + 16, :] = jnp.zeros((8, width), F32)
    base_ref[8 : rows + 8, :] = main
    base_ref[6:8, :] = top
    base_ref[rows + 8 : rows + 10, :] = bottom
    tall = BAND + 2
    lane = iota((tall, width), 1)
    ones = jnp.where(iota((8, width), 0) < 2, 1.0, 0.0)
    bands = two_ref.shape[0]
    total = None
    for k in range(bands):
        band = base_ref[k * BAND + 6 : k * BAND + 6 + tall, :]
        high = band.astype(BF16).astype(F32)
        low = band - high
        shifted = []
        for value in (high, low):
            shifted.append(
                [
                    jnp.where(lane == 0, 0.0, pltpu.roll(value, 1, 1)),
                    value,
                    jnp.where(lane == width - 1, 0.0, pltpu.roll(value, width - 1, 1)),
                ]
            )
        stack = jnp.concatenate(shifted[0] + shifted[1] + shifted[0] + [ones], axis=0).astype(BF16)
        hidden = jnp.maximum(mm(one_ref[...], stack), 0.0).astype(BF16)
        term = mm(two_ref[k], hidden)
        total = term if total is None else total + term
    edge = iota((rows, width), 1)
    left = jnp.where(edge == 0, 0.0, pltpu.roll(total[:rows], 1, 1))
    right = jnp.where(edge == width - 1, 0.0, pltpu.roll(total[2 * rows :], width - 1, 1))
    base_ref[0:rows, :] = main + total[rows : 2 * rows] + left + right
    me = lax.axis_index("freq")
    start, _ = window(me, count, part * count)
    out_ref[...] = base_ref[0:rows, pl.ds(pl.multiple_of(me * part - start, LANES), part)]


def unpack_kernel(dest_ref, back_ref, out_ref):
    tiles = dest_ref.shape[1]
    total, width = back_ref.shape
    placing = one_hot(iota((total, tiles), 0) == dest_ref[...])
    mine = mm(placing, back_ref[...], ((0,), (0,))).astype(BF16)
    out_ref[...] = mm(mine, swap_matrix(width)).astype(BF16)


def shape(dims, dtype):
    return jax.ShapeDtypeStruct(dims, dtype)


def call(kernel, out_shape, flops, scratch=(), name=None):
    return pl.pallas_call(
        kernel,
        out_shape=out_shape,
        scratch_shapes=scratch,
        name=name,
        cost_estimate=pl.CostEstimate(flops=flops, bytes_accessed=4 << 20, transcendentals=0),
    )


def on_device(sky, beam, observed, facet_of, tile_slot, conv_first, bias_first, conv_second):
    rows, cols = sky.shape
    beam = beam.reshape(rows, cols)
    facets = lax.axis_size("facet")
    count = lax.axis_size("freq")
    tiles, width = observed.shape
    cap = 2 * tiles // facets
    total = facets * cap
    slots = (rows // S) * (cols // S)
    hidden = conv_first.shape[0]
    row_f, twist_f, mat_f = tables(rows, cols, -1)
    row_b, twist_b, mat_b = tables(rows, cols, 1)

    deep = (width // LANES) * cap + 8
    send, dest = call(
        functools.partial(pack_kernel, facets, cap),
        [shape((facets, deep, LANES), BF16), shape((1, tiles), jnp.int32)],
        1 << 28,
        name="pack",
    )(facet_of.reshape(1, tiles), tile_slot.reshape(1, tiles), observed)
    got = lax.all_to_all(send, "facet", split_axis=0, concat_axis=0, tiled=True)

    bands = (rows + 2) // BAND
    first, second = call(
        prepare_kernel,
        [
            shape((hidden * BAND, 9 * (BAND + 2) + 8), BF16),
            shape((bands, 3 * rows, hidden * BAND), BF16),
        ],
        1 << 28,
        name="prepare",
    )(conv_first.reshape(hidden, 9), bias_first.reshape(hidden, 1), conv_second.reshape(hidden, 9))
    high, low = call(
        forward_kernel, [shape((width, slots), BF16)] * 2, 1 << 30, name="forward"
    )(sky, beam, row_f, twist_f, mat_f)

    residual, select = call(
        functools.partial(residual_kernel, facets, cap),
        [shape((total, width), BF16), shape((total, slots), BF16)],
        1 << 30,
        name="residual",
    )(got, high, low)
    returned = lax.all_to_all(
        residual.reshape(facets, cap, width), "facet", split_axis=0, concat_axis=0, tiled=True
    ).reshape(total, width)

    _, wide = window(0, count, cols)
    outs = call(
        functools.partial(inverse_kernel, count),
        [shape((rows, wide), F32)]
        + [shape((rows, wide), BF16)] * (count - 1)
        + [shape((2, wide), F32)] * (2 * count),
        1 << 30,
        scratch=[pltpu.VMEM((rows, cols), F32), pltpu.VMEM((rows, cols), F32)],
        name="inverse",
    )(residual, select, sky, beam, row_b, twist_b, mat_b)
    keep, sends = outs[0], outs[1:count]
    ups, downs = outs[count : 2 * count], outs[2 * count :]
    both = ("freq", "facet")

    def hop(value, d, step):
        pairs = [
            (f * facets + p, (f + d) % count * facets + p + step)
            for f in range(count)
            for p in range(facets)
            if 0 <= p + step < facets
        ]
        return lax.ppermute(value, both, pairs)

    gots = [hop(value, d + 1, 0) for d, value in enumerate(sends)]
    bottoms = [hop(value, d, -1) for d, value in enumerate(ups)]
    tops = [hop(value, d, 1) for d, value in enumerate(downs)]
    image = call(
        functools.partial(prior_kernel, count, cols // count),
        shape((rows, cols // count), F32),
        1 << 31,
        scratch=[pltpu.VMEM((rows + 16, wide), F32)],
        name="prior",
    )(keep, *gots, *tops, *bottoms, first, second)

    tiles_out = call(unpack_kernel, shape((tiles, width), BF16), 1 << 28, name="unpack")(
        dest, returned
    )
    return tiles_out, image


def solution(mesh):
    placed = (
        P("facet", None),
        P("freq", "facet", None),
        P(("freq", "facet"), None),
        P(("freq", "facet")),
        P(("freq", "facet")),
        P(),
        P(),
        P(),
    )
    return jax.shard_map(
        on_device,
        mesh=mesh,
        in_specs=placed,
        out_specs=(P(("freq", "facet"), None), P("facet", "freq")),
        check_vma=False,
    )
```

```python
import functools
import math

import jax
import jax.numpy as jnp
import numpy as np
from jax import lax
from jax.experimental import pallas as pl
from jax.experimental.pallas import tpu as pltpu
from jax.sharding import PartitionSpec as P

S = 16
LANES = 128
BAND = 22
STEP = 0.5
F32 = jnp.float32
BF16 = jnp.bfloat16


def iota(shape, dim):
    return lax.broadcasted_iota(jnp.int32, shape, dim)


def mm(a, b, dims=((1,), (0,))):
    return lax.dot_general(a, b, (dims, ((), ())), preferred_element_type=F32)


def one_hot(cond):
    return jnp.where(cond, 1.0, 0.0).astype(BF16)


def split(x):
    high = x.astype(BF16)
    return high, (x - high.astype(F32)).astype(BF16)


def np_split(x):
    x = np.asarray(x, np.float32)
    high = x.astype(BF16)
    return high, (x - high.astype(np.float32)).astype(BF16)


def tables(rows, cols, sign):
    outer = cols // LANES
    scale = 1.0 / math.sqrt(rows * cols)
    k = np.arange(rows)
    angle = sign * 2.0 * np.pi * ((k[:, None] * k[None, :]) % rows) / rows
    cos_r, sin_r = np.cos(angle) * scale, np.sin(angle) * scale
    if sign < 0:
        row_high, row_low = np_split(np.concatenate([cos_r, sin_r], 0))
        row = np.concatenate([row_high, row_high, row_low], 1)
    else:
        row_high, row_low = np_split(np.concatenate([cos_r, -sin_r], 1))
        row = np.concatenate([row_high, row_high, row_low], 1)
    i2 = np.arange(LANES)
    w = np.arange(outer)
    twist = sign * 2.0 * np.pi * ((w[:, None] * i2[None, :]) % cols) / cols
    inner = sign * 2.0 * np.pi * ((i2[:, None] * i2[None, :]) % LANES) / LANES
    c, s = np.cos(inner), np.sin(inner)
    mat_high, mat_low = np_split(np.block([[c, s], [-s, c]]))
    return (
        row,
        np.stack([np.cos(twist), np.sin(twist)]).astype(np.float32),
        np.stack([mat_high, mat_low]),
    )


def times_i(z, sign):
    re, im = z
    return (-im, re) if sign > 0 else (im, -re)


def add(a, b):
    return (a[0] + b[0], a[1] + b[1])


def sub(a, b):
    return (a[0] - b[0], a[1] - b[1])


def dft4(x, sign):
    s0, s1 = add(x[0], x[2]), sub(x[0], x[2])
    s2, s3 = add(x[1], x[3]), times_i(sub(x[1], x[3]), sign)
    return [add(s0, s2), add(s1, s3), sub(s0, s2), sub(s1, s3)]


def dft16(x, sign):
    mid = [dft4([x[4 * a + b] for a in range(4)], sign) for b in range(4)]
    out = [None] * 16
    for c in range(4):
        turned = []
        for b in range(4):
            re, im = mid[b][c]
            phase = (b * c) % 16
            if phase == 0:
                turned.append((re, im))
            elif phase == 4:
                turned.append(times_i((re, im), sign))
            else:
                wr = math.cos(2.0 * math.pi * phase / 16)
                wi = sign * math.sin(2.0 * math.pi * phase / 16)
                turned.append((re * wr - im * wi, re * wi + im * wr))
        for d, value in enumerate(dft4(turned, sign)):
            out[c + 4 * d] = value
    return out


def swap_matrix(size):
    src = iota((1, size), 1)
    swapped = (src & -256) | ((src & 15) << 4) | ((src >> 4) & 15)
    return one_hot(iota((size, size), 0) == swapped)


def pack_kernel(facets, cap, facet_hbm, slot_hbm, seen_hbm, send_ref, dest_ref, facet_ref, slot_ref, seen_ref, sems):
    tiles, width = seen_ref.shape
    total = facets * cap
    loads = [
        pltpu.make_async_copy(src, dst, sems.at[i])
        for i, (src, dst) in enumerate(
            ((facet_hbm, facet_ref), (slot_hbm, slot_ref), (seen_hbm, seen_ref))
        )
    ]
    for load in loads:
        load.start()
    swap = swap_matrix(width)
    loads[0].wait()
    facet = facet_ref[...]
    member = iota((facets, tiles), 0) == facet
    member_f = jnp.where(member, 1.0, 0.0)
    before = one_hot(iota((tiles, tiles), 0) < iota((tiles, tiles), 1))
    ranks = mm(member_f.astype(BF16), before)
    rank = jnp.sum(member_f * ranks, axis=0, keepdims=True).astype(jnp.int32)
    dest = facet * cap + rank
    dest_ref[...] = dest
    placing = one_hot(iota((total, tiles), 0) == dest)
    loads[2].wait()
    turned = mm(seen_ref[...], swap).astype(BF16)
    packed = mm(placing, turned).astype(BF16)
    loads[1].wait()
    code = slot_ref[...] + 1
    lane = iota((LANES, tiles), 0)
    slots = mm(
        (member_f * (code >> 4).astype(F32)).astype(BF16), one_hot(lane == rank), ((1,), (1,))
    ) + mm(
        (member_f * (code & 15).astype(F32)).astype(BF16),
        one_hot(lane - LANES // 2 == rank),
        ((1,), (1,)),
    )
    parts = width // LANES
    for d in range(facets):
        for part in range(parts):
            send_ref[d, part * cap : (part + 1) * cap, :] = packed[
                d * cap : (d + 1) * cap, part * LANES : (part + 1) * LANES
            ]
        send_ref[d, parts * cap : parts * cap + 8, :] = jnp.broadcast_to(
            slots[d : d + 1, :], (8, LANES)
        ).astype(BF16)


def forward_kernel(
    sky_ref,
    beam_ref,
    row_ref,
    twist_ref,
    mat_ref,
    first_ref,
    bias_ref,
    second_ref,
    high_ref,
    low_ref,
    one_ref,
    two_ref,
):
    prepare(first_ref, bias_ref, second_ref, one_ref, two_ref)
    rows, cols = sky_ref.shape
    outer = cols // LANES
    weighted = sky_ref[...] * beam_ref[...]
    w_high, w_low = split(weighted)
    mid = mm(row_ref[...], jnp.concatenate([w_high, w_low, w_high], axis=0))
    lines = [
        (
            mid[:rows, i * LANES : (i + 1) * LANES],
            mid[rows:, i * LANES : (i + 1) * LANES],
        )
        for i in range(outer)
    ]
    spread = dft16(lines, -1)
    blocks = []
    for w in range(outer):
        re, im = spread[w]
        tr, ti = twist_ref[0, w : w + 1, :], twist_ref[1, w : w + 1, :]
        blocks.append(jnp.concatenate([re * tr - im * ti, re * ti + im * tr], axis=1))
    high, low = split(jnp.concatenate(blocks, axis=0))
    mat_high, mat_low = mat_ref[0], mat_ref[1]
    model = mm(high, mat_high) + mm(low, mat_high) + mm(high, mat_low)
    for w in range(outer):
        for r in range(rows // S):
            for e in range(2):
                piece = model[
                    w * rows + r * S : w * rows + (r + 1) * S, e * LANES : (e + 1) * LANES
                ]
                piece_high, piece_low = split(piece)
                at = (pl.ds(e * 256 + w * S, S), pl.ds(r * LANES, LANES))
                high_ref[at] = piece_high
                low_ref[at] = piece_low


def residual_kernel(facets, cap, got_ref, high_ref, low_ref, res_hbm, sel_ref, own_ref, sems):
    total = facets * cap
    slots = high_ref.shape[1]
    parts = high_ref.shape[0] // LANES
    code = got_ref[:, parts * cap : parts * cap + 8, :].astype(F32).reshape(facets * 8, LANES)
    source = iota((total, facets * 8), 0) // cap
    spread = mm(one_hot(iota((total, facets * 8), 1) == source * 8), code.astype(BF16))
    lane = iota((total, LANES), 1)
    rank = iota((total, LANES), 0) % cap
    kept = jnp.where((lane & (LANES // 2 - 1)) == rank, spread, 0.0).astype(BF16)
    digit = jnp.where(iota((LANES, slots), 0) < LANES // 2, 16.0, 1.0).astype(BF16)
    code_all = mm(kept, digit)
    sel = one_hot(code_all.astype(jnp.int32) == iota((total, slots), 1) + 1)
    sel_ref[...] = sel
    contract = ((1,), (1,))
    predicted = mm(sel, high_ref[...], contract) + mm(sel, low_ref[...], contract)
    saves = []
    pieces = sems.shape[0]
    for i in range(pieces):
        here = facets // pieces
        at = slice(i * here * cap, (i + 1) * here * cap)
        for part in range(parts):
            cols = slice(part * LANES, (part + 1) * LANES)
            seen = got_ref[i * here : (i + 1) * here, part * cap : (part + 1) * cap, :]
            seen = seen.astype(F32).reshape(here * cap, LANES)
            own_ref[at, cols] = (predicted[at, cols] - seen).astype(BF16)
        save = pltpu.make_async_copy(own_ref.at[at, :], res_hbm.at[at, :], sems.at[i])
        save.start()
        saves.append(save)
    for save in saves:
        save.wait()


def window(index, count, cols):
    part = cols // count
    width = min(cols, part + (LANES if count == 2 else 2 * LANES))
    return jnp.clip(index * part - LANES, 0, cols - width), width


def inverse_kernel(
    count,
    res_ref,
    sel_ref,
    row_ref,
    twist_ref,
    mat_ref,
    sky_hbm,
    beam_hbm,
    keep_ref,
    *rest,
):
    send_refs = rest[: count - 1]
    sky_ref, beam_ref, lines_ref, shift_ref, sems = rest[count - 1 :]
    rows, cols = beam_ref.shape
    outer = cols // LANES
    me = lax.axis_index("freq")
    start, width = window(me, count, cols)
    sky_part = sky_hbm.at[:, pl.ds(pl.multiple_of(start, LANES), width)]
    loads = [
        pltpu.make_async_copy(beam_hbm, beam_ref, sems.at[0]),
        pltpu.make_async_copy(sky_part, sky_ref, sems.at[1]),
    ]
    for load in loads:
        load.start()
    grid = mm(res_ref[...], sel_ref[...], ((0,), (0,)))
    blocks = []
    for w in range(outer):
        blocks.append(
            jnp.concatenate(
                [
                    jnp.concatenate(
                        [
                            grid[
                                e * 256 + w * S : e * 256 + (w + 1) * S,
                                r * LANES : (r + 1) * LANES,
                            ]
                            for e in range(2)
                        ],
                        axis=1,
                    )
                    for r in range(rows // S)
                ],
                axis=0,
            )
        )
    high, low = split(jnp.concatenate(blocks, axis=0))
    mat_high, mat_low = mat_ref[0], mat_ref[1]
    mid = mm(high, mat_high) + mm(low, mat_high) + mm(high, mat_low)
    lines = []
    for w in range(outer):
        re = mid[w * rows : (w + 1) * rows, :LANES]
        im = mid[w * rows : (w + 1) * rows, LANES:]
        tr, ti = twist_ref[0, w : w + 1, :], twist_ref[1, w : w + 1, :]
        lines.append((re * tr - im * ti, re * ti + im * tr))
    spread = dft16(lines, 1)
    for i, pair in enumerate(spread):
        for e in range(2):
            high, low = split(pair[e])
            lines_ref[e * rows : (e + 1) * rows, i * LANES : (i + 1) * LANES] = high
            lines_ref[(2 + e) * rows : (3 + e) * rows, i * LANES : (i + 1) * LANES] = low
    back = mm(row_ref[:, : 4 * rows], lines_ref[...]) + mm(
        row_ref[:, 4 * rows :], lines_ref[: 2 * rows, :]
    )
    for load in loads:
        load.wait()
    shift_ref[...] = back * beam_ref[...] * (-STEP)
    for d in range(count):
        start, width = window(lax.rem(me + d, count), count, cols)
        at = pl.ds(pl.multiple_of(start, LANES), width)
        if d == 0:
            keep_ref[...] = shift_ref[:, at] + sky_ref[...]
        else:
            send_refs[d - 1][...] = shift_ref[:, at].astype(BF16)


def sum_kernel(keep_ref, *refs):
    main_ref, near_ref, far_ref = refs[-3:]
    rows = keep_ref.shape[0]
    main = keep_ref[...]
    for ref in refs[:-3]:
        main = main + ref[...].astype(F32)
    main_ref[...] = main
    even = (lax.axis_index("facet") & 1) == 0
    top, bottom = main[0:2], main[rows - 2 : rows]
    near_ref[...] = jnp.where(even, bottom, top)
    far_ref[...] = jnp.where(even, top, bottom)


def prepare(first_ref, bias_ref, second_ref, one_ref, two_ref):
    hidden = first_ref.shape[2]
    depth = one_ref.shape[1]
    full = (BAND + 2) * 9
    bias_high, bias_low = split(bias_ref[...])
    line = iota((8, depth), 0)
    lane = iota((8, depth), 1)
    group = lane * 2731 >> 16
    term = group * 86 >> 8
    col = group - term * 3
    taps = one_hot(((line == col) & (term < 2)) | ((line - 3 == col) & (term == 2)))
    ends = one_hot(((line == 6) & (lane == full)) | ((line == 7) & (lane == full + 1)))
    values = []
    for a in range(3):
        high, low = split(first_ref[a])
        pieces = [high, low, bias_high, bias_low]
        weights = jnp.concatenate([p.astype(F32) for p in pieces], axis=0).astype(BF16)
        values.append(mm(weights, taps, ((0,), (0,))))
        if a == 0:
            offset = mm(weights, ends, ((0,), (0,)))
    lane = iota((hidden, depth), 1)
    yin = lane - (lane * 2731 >> 16) * (BAND + 2)
    for y in range(BAND):
        block = offset
        for a in range(3):
            block = block + jnp.where(yin == y + a, values[a], 0.0)
        one_ref[y * hidden : (y + 1) * hidden, :] = block.astype(BF16)

    wide = two_ref.shape[1]
    tall = BAND + 2
    expand = one_hot(iota((hidden, wide), 0) == (iota((hidden, wide), 1) & (hidden - 1)))
    pieces = [split(second_ref[a]) for a in range(3)]
    gap = iota((tall, wide), 1) // hidden + 2 - iota((tall, wide), 0)
    blocks = []
    for half in range(2):
        lines = [mm(pieces[a][half], expand) for a in range(3)]
        for b in range(3):
            total = jnp.zeros((tall, wide), F32)
            for a in range(3):
                total = jnp.where(gap == a, lines[a][b : b + 1, :], total)
            blocks.append(total)
    two_ref[...] = jnp.concatenate(blocks, axis=0).astype(BF16)


def prior_kernel(count, part, main_ref, near_ref, far_ref, one_ref, two_ref, out_ref, base_ref, sum_ref):
    rows, width = main_ref.shape
    me = lax.axis_index("freq")
    start, _ = window(me, count, part * count)
    main = main_ref[...]
    near, far = near_ref[...], far_ref[...]
    even = (lax.axis_index("facet") & 1) == 0
    top, bottom = jnp.where(even, far, near), jnp.where(even, near, far)
    base_ref[0:8, :] = jnp.zeros((8, width), F32)
    base_ref[rows + 8 : rows + 16, :] = jnp.zeros((8, width), F32)
    base_ref[8 : rows + 8, :] = main
    base_ref[6:8, :] = top
    base_ref[rows + 8 : rows + 10, :] = bottom
    tall = BAND + 2
    lane = iota((tall, width), 1)
    ones = jnp.where(iota((8, width), 0) < 2, 1.0, 0.0)
    bands = (rows + 2) // BAND
    place = lax.axis_index("facet")
    last = lax.axis_size("facet") - 1
    inner = one_ref.shape[0] // BAND
    sum_ref[0:8, :] = jnp.zeros((8, width), F32)
    sum_ref[8 : rows + 8, :] = main
    sum_ref[rows + 8 :, :] = jnp.zeros((8, width), F32)
    for k in range(bands):
        band = base_ref[k * BAND + 6 : k * BAND + 6 + tall, :]
        high = band.astype(BF16).astype(F32)
        low = band - high
        shifted = []
        for value in (high, low):
            shifted.append(
                [
                    jnp.where(lane == 0, 0.0, pltpu.roll(value, 1, 1)),
                    value,
                    jnp.where(lane == width - 1, 0.0, pltpu.roll(value, width - 1, 1)),
                ]
            )
        stack = jnp.concatenate(shifted[0] + shifted[1] + shifted[0] + [ones], axis=0).astype(BF16)
        hidden = jnp.maximum(mm(one_ref[...], stack), 0.0)
        if k == 0:
            edge = jnp.where(place == 0, 0.0, hidden[:inner])
            hidden = jnp.concatenate([edge, hidden[inner:]], axis=0)
        if k == bands - 1:
            edge = jnp.where(place == last, 0.0, hidden[-inner:])
            hidden = jnp.concatenate([hidden[:-inner], edge], axis=0)
        taps = mm(two_ref[...], hidden.astype(BF16))
        left, middle, right = (
            taps[b * tall : (b + 1) * tall] + taps[(3 + b) * tall : (4 + b) * tall]
            for b in range(3)
        )
        left = jnp.where(lane == 0, 0.0, pltpu.roll(left, 1, 1))
        right = jnp.where(lane == width - 1, 0.0, pltpu.roll(right, width - 1, 1))
        at = slice(k * BAND + 6, k * BAND + 6 + tall)
        sum_ref[at, :] = sum_ref[at, :] + (middle + left + right)
    out_ref[...] = sum_ref[8 : rows + 8, pl.ds(pl.multiple_of(me * part - start, LANES), part)]


def unpack_kernel(dest_ref, back_ref, out_ref):
    tiles = dest_ref.shape[1]
    total, width = back_ref.shape
    placing = one_hot(iota((total, tiles), 0) == dest_ref[...])
    mine = mm(placing, back_ref[...], ((0,), (0,))).astype(BF16)
    out_ref[...] = mm(mine, swap_matrix(width)).astype(BF16)


def shape(dims, dtype):
    return jax.ShapeDtypeStruct(dims, dtype)


def call(kernel, out_shape, flops, scratch=(), name=None, loaded=(), saved=(), limit=16):
    near = pl.BlockSpec(memory_space=pltpu.VMEM)
    far = pl.BlockSpec(memory_space=pltpu.HBM)

    def run(*args):
        return pl.pallas_call(
            kernel,
            out_shape=out_shape,
            in_specs=[far if i in loaded else near for i in range(len(args))],
            out_specs=[far if i in saved else near for i in range(len(out_shape))]
            if isinstance(out_shape, list)
            else near,
            scratch_shapes=scratch,
            name=name,
            compiler_params=pltpu.CompilerParams(vmem_limit_bytes=limit << 20),
            cost_estimate=pl.CostEstimate(flops=flops, bytes_accessed=4 << 20, transcendentals=0),
        )(*args)

    return run


def on_device(sky, beam, observed, facet_of, tile_slot, conv_first, bias_first, conv_second):
    rows, cols = sky.shape
    beam = beam.reshape(rows, cols)
    facets = lax.axis_size("facet")
    count = lax.axis_size("freq")
    tiles, width = observed.shape
    cap = 2 * tiles // facets
    total = facets * cap
    slots = (rows // S) * (cols // S)
    hidden = conv_first.shape[0]
    row_f, twist_f, mat_f = tables(rows, cols, -1)
    row_b, twist_b, mat_b = tables(rows, cols, 1)

    deep = (width // LANES) * cap + 8
    send, dest = call(
        functools.partial(pack_kernel, facets, cap),
        [shape((facets, deep, LANES), BF16), shape((1, tiles), jnp.int32)],
        1 << 28,
        scratch=[
            pltpu.VMEM((1, tiles), jnp.int32),
            pltpu.VMEM((1, tiles), jnp.int32),
            pltpu.VMEM((tiles, width), BF16),
            pltpu.SemaphoreType.DMA((3,)),
        ],
        name="pack",
        loaded=(0, 1, 2),
    )(
        *(
            pltpu.with_memory_space_constraint(value, pltpu.HBM)
            for value in (facet_of.reshape(1, tiles), tile_slot.reshape(1, tiles), observed)
        )
    )
    got = lax.all_to_all(send, "facet", split_axis=0, concat_axis=0, tiled=True)

    high, low, first, second = call(
        forward_kernel,
        [
            shape((width, slots), BF16),
            shape((width, slots), BF16),
            shape((hidden * BAND, 9 * (BAND + 2) + 8), BF16),
            shape((6 * (BAND + 2), hidden * BAND), BF16),
        ],
        1 << 30,
        name="forward",
    )(
        sky,
        beam,
        row_f,
        twist_f,
        mat_f,
        conv_first.transpose(1, 2, 0),
        bias_first.reshape(1, hidden),
        conv_second.transpose(1, 2, 0),
    )

    residual, select, own = call(
        functools.partial(residual_kernel, facets, cap),
        [shape((total, width), BF16), shape((total, slots), BF16), shape((total, width), BF16)],
        1 << 30,
        scratch=[pltpu.SemaphoreType.DMA((4,))],
        name="residual",
        saved=(0,),
    )(got, *(pltpu.with_memory_space_constraint(value, pltpu.VMEM) for value in (high, low)))
    returned = lax.all_to_all(
        residual.reshape(facets, cap, width), "facet", split_axis=0, concat_axis=0, tiled=True
    ).reshape(total, width)

    _, wide = window(0, count, cols)
    keep, *sends = call(
        functools.partial(inverse_kernel, count),
        [shape((rows, wide), F32)] + [shape((rows, wide), BF16)] * (count - 1),
        1 << 30,
        scratch=[
            pltpu.VMEM((rows, wide), F32),
            pltpu.VMEM((rows, cols), F32),
            pltpu.VMEM((4 * rows, cols), BF16),
            pltpu.VMEM((rows, cols), F32),
            pltpu.SemaphoreType.DMA((2,)),
        ],
        name="inverse",
        loaded=(5, 6),
    )(
        own,
        select,
        row_b,
        twist_b,
        mat_b,
        *(pltpu.with_memory_space_constraint(value, pltpu.HBM) for value in (sky, beam)),
    )

    def beside(value, to):
        pairs = [(p, to(p)) for p in range(facets) if 0 <= to(p) < facets]
        return lax.ppermute(value, "facet", pairs)

    gots = [
        lax.ppermute(value, "freq", [(f, (f + d + 1) % count) for f in range(count)])
        for d, value in enumerate(sends)
    ]
    main, near, far = call(
        sum_kernel,
        [shape((rows, wide), F32), shape((2, wide), F32), shape((2, wide), F32)],
        1 << 24,
        name="total",
    )(keep, *gots)
    far = beside(far, lambda p: p + 1 if p & 1 else p - 1)
    near = beside(near, lambda p: p ^ 1)
    image = call(
        functools.partial(prior_kernel, count, cols // count),
        shape((rows, cols // count), F32),
        1 << 31,
        scratch=[pltpu.VMEM((rows + 16, wide), F32)] * 2,
        name="prior",
    )(main, near, far, first, second)

    tiles_out = call(unpack_kernel, shape((tiles, width), BF16), 1 << 28, name="unpack")(
        dest, returned
    )
    return tiles_out, image


def solution(mesh):
    placed = (
        P("facet", None),
        P("freq", "facet", None),
        P(("freq", "facet"), None),
        P(("freq", "facet")),
        P(("freq", "facet")),
        P(),
        P(),
        P(),
    )
    return jax.shard_map(
        on_device,
        mesh=mesh,
        in_specs=placed,
        out_specs=(P(("freq", "facet"), None), P("facet", "freq")),
        check_vma=False,
    )
```

```python
import functools
import math

import jax
import jax.numpy as jnp
import numpy as np
from jax import lax
from jax.experimental import pallas as pl
from jax.experimental.pallas import tpu as pltpu
from jax.sharding import PartitionSpec as P


S = 16
LANES = 128
BAND = 22
STEP = 0.5
F32 = jnp.float32
BF16 = jnp.bfloat16


def iota(shape, dim):
    return lax.broadcasted_iota(jnp.int32, shape, dim)


def mm(a, b, dims=((1,), (0,))):
    return lax.dot_general(a, b, (dims, ((), ())), preferred_element_type=F32)


def one_hot(cond):
    return jnp.where(cond, 1.0, 0.0).astype(BF16)


def split(x):
    high = x.astype(BF16)
    return high, (x - high.astype(F32)).astype(BF16)


def np_split(x):
    x = np.asarray(x, np.float32)
    high = x.astype(BF16)
    return high, (x - high.astype(np.float32)).astype(BF16)


def tables(rows, cols, sign):
    outer = cols // LANES
    scale = 1.0 / math.sqrt(rows * cols)
    k = np.arange(rows)
    angle = sign * 2.0 * np.pi * ((k[:, None] * k[None, :]) % rows) / rows
    cos_r, sin_r = np.cos(angle) * scale, np.sin(angle) * scale
    if sign < 0:
        row_high, row_low = np_split(np.concatenate([cos_r, sin_r], 0))
        row = np.concatenate([row_high, row_high, row_low], 1)
    else:
        row_high, row_low = np_split(np.concatenate([cos_r, -sin_r], 1))
        row = np.concatenate([row_high, row_high, row_low], 1)
    i2 = np.arange(LANES)
    w = np.arange(outer)
    twist = sign * 2.0 * np.pi * ((w[:, None] * i2[None, :]) % cols) / cols
    inner = sign * 2.0 * np.pi * ((i2[:, None] * i2[None, :]) % LANES) / LANES
    c, s = np.cos(inner), np.sin(inner)
    mat_high, mat_low = np_split(np.block([[c, s], [-s, c]]))
    return (
        row,
        np.stack([np.cos(twist), np.sin(twist)]).astype(np.float32),
        np.stack([mat_high, mat_low]),
    )


def times_i(z, sign):
    re, im = z
    return (-im, re) if sign > 0 else (im, -re)


def add(a, b):
    return (a[0] + b[0], a[1] + b[1])


def sub(a, b):
    return (a[0] - b[0], a[1] - b[1])


def dft4(x, sign):
    s0, s1 = add(x[0], x[2]), sub(x[0], x[2])
    s2, s3 = add(x[1], x[3]), times_i(sub(x[1], x[3]), sign)
    return [add(s0, s2), add(s1, s3), sub(s0, s2), sub(s1, s3)]


def dft16(x, sign):
    mid = [dft4([x[4 * a + b] for a in range(4)], sign) for b in range(4)]
    out = [None] * 16
    for c in range(4):
        turned = []
        for b in range(4):
            re, im = mid[b][c]
            phase = (b * c) % 16
            if phase == 0:
                turned.append((re, im))
            elif phase == 4:
                turned.append(times_i((re, im), sign))
            else:
                wr = math.cos(2.0 * math.pi * phase / 16)
                wi = sign * math.sin(2.0 * math.pi * phase / 16)
                turned.append((re * wr - im * wi, re * wi + im * wr))
        for d, value in enumerate(dft4(turned, sign)):
            out[c + 4 * d] = value
    return out


def swap_matrix(size):
    src = iota((1, size), 1)
    swapped = (src & -256) | ((src & 15) << 4) | ((src >> 4) & 15)
    return one_hot(iota((size, size), 0) == swapped)


def pack_kernel(facets, cap, facet_hbm, slot_hbm, seen_hbm, send_ref, dest_ref, facet_ref, slot_ref, seen_ref, sems):
    tiles, width = seen_ref.shape
    total = facets * cap
    loads = [
        pltpu.make_async_copy(src, dst, sems.at[i])
        for i, (src, dst) in enumerate(
            ((facet_hbm, facet_ref), (slot_hbm, slot_ref), (seen_hbm, seen_ref))
        )
    ]
    for load in loads:
        load.start()
    swap = swap_matrix(width)
    loads[0].wait()
    facet = facet_ref[...]
    member = iota((facets, tiles), 0) == facet
    member_f = jnp.where(member, 1.0, 0.0)
    before = one_hot(iota((tiles, tiles), 0) < iota((tiles, tiles), 1))
    ranks = mm(member_f.astype(BF16), before)
    rank = jnp.sum(member_f * ranks, axis=0, keepdims=True).astype(jnp.int32)
    dest = facet * cap + rank
    dest_ref[...] = dest
    placing = one_hot(iota((total, tiles), 0) == dest)
    loads[2].wait()
    turned = mm(seen_ref[...], swap).astype(BF16)
    packed = mm(placing, turned).astype(BF16)
    loads[1].wait()
    code = slot_ref[...] + 1
    lane = iota((LANES, tiles), 0)
    slots = mm(
        (member_f * (code >> 4).astype(F32)).astype(BF16), one_hot(lane == rank), ((1,), (1,))
    ) + mm(
        (member_f * (code & 15).astype(F32)).astype(BF16),
        one_hot(lane - LANES // 2 == rank),
        ((1,), (1,)),
    )
    parts = width // LANES
    for d in range(facets):
        for part in range(parts):
            send_ref[d, part * cap : (part + 1) * cap, :] = packed[
                d * cap : (d + 1) * cap, part * LANES : (part + 1) * LANES
            ]
        send_ref[d, parts * cap : parts * cap + 8, :] = jnp.broadcast_to(
            slots[d : d + 1, :], (8, LANES)
        ).astype(BF16)


def forward_kernel(
    sky_ref,
    beam_ref,
    row_ref,
    twist_ref,
    mat_ref,
    first_ref,
    bias_ref,
    second_ref,
    high_ref,
    low_ref,
    one_ref,
    two_ref,
):
    prepare(first_ref, bias_ref, second_ref, one_ref, two_ref)
    rows, cols = sky_ref.shape
    outer = cols // LANES
    weighted = sky_ref[...] * beam_ref[...]
    w_high, w_low = split(weighted)
    mid = mm(row_ref[...], jnp.concatenate([w_high, w_low, w_high], axis=0))
    lines = [
        (
            mid[:rows, i * LANES : (i + 1) * LANES],
            mid[rows:, i * LANES : (i + 1) * LANES],
        )
        for i in range(outer)
    ]
    spread = dft16(lines, -1)
    blocks = []
    for w in range(outer):
        re, im = spread[w]
        tr, ti = twist_ref[0, w : w + 1, :], twist_ref[1, w : w + 1, :]
        blocks.append(jnp.concatenate([re * tr - im * ti, re * ti + im * tr], axis=1))
    high, low = split(jnp.concatenate(blocks, axis=0))
    mat_high, mat_low = mat_ref[0], mat_ref[1]
    model = mm(high, mat_high) + mm(low, mat_high) + mm(high, mat_low)
    for w in range(outer):
        for r in range(rows // S):
            for e in range(2):
                piece = model[
                    w * rows + r * S : w * rows + (r + 1) * S, e * LANES : (e + 1) * LANES
                ]
                piece_high, piece_low = split(piece)
                at = (pl.ds(e * 256 + w * S, S), pl.ds(r * LANES, LANES))
                high_ref[at] = piece_high
                low_ref[at] = piece_low


def residual_kernel(facets, cap, got_ref, high_ref, low_ref, res_hbm, sel_ref, own_ref, sems):
    total = facets * cap
    slots = high_ref.shape[1]
    parts = high_ref.shape[0] // LANES
    code = got_ref[:, parts * cap : parts * cap + 8, :].astype(F32).reshape(facets * 8, LANES)
    source = iota((total, facets * 8), 0) // cap
    spread = mm(one_hot(iota((total, facets * 8), 1) == source * 8), code.astype(BF16))
    lane = iota((total, LANES), 1)
    rank = iota((total, LANES), 0) % cap
    kept = jnp.where((lane & (LANES // 2 - 1)) == rank, spread, 0.0).astype(BF16)
    digit = jnp.where(iota((LANES, slots), 0) < LANES // 2, 16.0, 1.0).astype(BF16)
    code_all = mm(kept, digit)
    sel = one_hot(code_all.astype(jnp.int32) == iota((total, slots), 1) + 1)
    sel_ref[...] = sel
    contract = ((1,), (1,))
    predicted = mm(sel, high_ref[...], contract) + mm(sel, low_ref[...], contract)
    saves = []
    pieces = sems.shape[0]
    for i in range(pieces):
        here = facets // pieces
        at = slice(i * here * cap, (i + 1) * here * cap)
        for part in range(parts):
            cols = slice(part * LANES, (part + 1) * LANES)
            seen = got_ref[i * here : (i + 1) * here, part * cap : (part + 1) * cap, :]
            seen = seen.astype(F32).reshape(here * cap, LANES)
            own_ref[at, cols] = (predicted[at, cols] - seen).astype(BF16)
        save = pltpu.make_async_copy(own_ref.at[at, :], res_hbm.at[at, :], sems.at[i])
        save.start()
        saves.append(save)
    for save in saves:
        save.wait()


def window(index, count, cols):
    part = cols // count
    width = min(cols, part + (LANES if count == 2 else 2 * LANES))
    return jnp.clip(index * part - LANES, 0, cols - width), width


def inverse_kernel(
    count,
    res_ref,
    sel_ref,
    row_ref,
    twist_ref,
    mat_ref,
    sky_hbm,
    beam_hbm,
    keep_ref,
    *rest,
):
    send_refs = rest[: count - 1]
    sky_ref, beam_ref, lines_ref, shift_ref, sems = rest[count - 1 :]
    rows, cols = beam_ref.shape
    outer = cols // LANES
    me = lax.axis_index("freq")
    start, width = window(me, count, cols)
    sky_part = sky_hbm.at[:, pl.ds(pl.multiple_of(start, LANES), width)]
    loads = [
        pltpu.make_async_copy(beam_hbm, beam_ref, sems.at[0]),
        pltpu.make_async_copy(sky_part, sky_ref, sems.at[1]),
    ]
    for load in loads:
        load.start()
    grid = mm(res_ref[...], sel_ref[...], ((0,), (0,)))
    blocks = []
    for w in range(outer):
        blocks.append(
            jnp.concatenate(
                [
                    jnp.concatenate(
                        [
                            grid[
                                e * 256 + w * S : e * 256 + (w + 1) * S,
                                r * LANES : (r + 1) * LANES,
                            ]
                            for e in range(2)
                        ],
                        axis=1,
                    )
                    for r in range(rows // S)
                ],
                axis=0,
            )
        )
    high, low = split(jnp.concatenate(blocks, axis=0))
    mat_high, mat_low = mat_ref[0], mat_ref[1]
    mid = mm(high, mat_high) + mm(low, mat_high) + mm(high, mat_low)
    lines = []
    for w in range(outer):
        re = mid[w * rows : (w + 1) * rows, :LANES]
        im = mid[w * rows : (w + 1) * rows, LANES:]
        tr, ti = twist_ref[0, w : w + 1, :], twist_ref[1, w : w + 1, :]
        lines.append((re * tr - im * ti, re * ti + im * tr))
    spread = dft16(lines, 1)
    for i, pair in enumerate(spread):
        for e in range(2):
            high, low = split(pair[e])
            lines_ref[e * rows : (e + 1) * rows, i * LANES : (i + 1) * LANES] = high
            lines_ref[(2 + e) * rows : (3 + e) * rows, i * LANES : (i + 1) * LANES] = low
    back = mm(row_ref[:, : 4 * rows], lines_ref[...]) + mm(
        row_ref[:, 4 * rows :], lines_ref[: 2 * rows, :]
    )
    for load in loads:
        load.wait()
    shift_ref[...] = back * beam_ref[...] * (-STEP)
    for d in range(count):
        start, width = window(lax.rem(me + d, count), count, cols)
        at = pl.ds(pl.multiple_of(start, LANES), width)
        if d == 0:
            keep_ref[...] = shift_ref[:, at] + sky_ref[...]
        else:
            send_refs[d - 1][...] = shift_ref[:, at].astype(BF16)


def sum_kernel(keep_ref, *refs):
    main_ref, near_ref, far_ref = refs[-3:]
    rows = keep_ref.shape[0]
    main = keep_ref[...]
    for ref in refs[:-3]:
        main = main + ref[...].astype(F32)
    main_ref[...] = main
    even = (lax.axis_index("facet") & 1) == 0
    top, bottom = main[0:2], main[rows - 2 : rows]
    near_ref[...] = jnp.where(even, bottom, top)
    far_ref[...] = jnp.where(even, top, bottom)


def prepare(first_ref, bias_ref, second_ref, one_ref, two_ref):
    hidden = first_ref.shape[2]
    depth = one_ref.shape[1]
    full = (BAND + 2) * 9
    bias_high, bias_low = split(bias_ref[...])
    line = iota((8, depth), 0)
    lane = iota((8, depth), 1)
    group = lane * 2731 >> 16
    term = group * 86 >> 8
    col = group - term * 3
    taps = one_hot(((line == col) & (term < 2)) | ((line - 3 == col) & (term == 2)))
    ends = one_hot(((line == 6) & (lane == full)) | ((line == 7) & (lane == full + 1)))
    values = []
    for a in range(3):
        high, low = split(first_ref[a])
        pieces = [high, low, bias_high, bias_low]
        weights = jnp.concatenate([p.astype(F32) for p in pieces], axis=0).astype(BF16)
        values.append(mm(weights, taps, ((0,), (0,))))
        if a == 0:
            offset = mm(weights, ends, ((0,), (0,)))
    lane = iota((hidden, depth), 1)
    yin = lane - (lane * 2731 >> 16) * (BAND + 2)
    for y in range(BAND):
        block = offset
        for a in range(3):
            block = block + jnp.where(yin == y + a, values[a], 0.0)
        one_ref[y * hidden : (y + 1) * hidden, :] = block.astype(BF16)

    wide = two_ref.shape[1]
    tall = BAND + 2
    expand = one_hot(iota((hidden, wide), 0) == (iota((hidden, wide), 1) & (hidden - 1)))
    pieces = [split(second_ref[a]) for a in range(3)]
    gap = iota((tall, wide), 1) // hidden + 2 - iota((tall, wide), 0)
    blocks = []
    for half in range(2):
        lines = [mm(pieces[a][half], expand) for a in range(3)]
        for b in range(3):
            total = jnp.zeros((tall, wide), F32)
            for a in range(3):
                total = jnp.where(gap == a, lines[a][b : b + 1, :], total)
            blocks.append(total)
    two_ref[...] = jnp.concatenate(blocks, axis=0).astype(BF16)


def band_prior(band, one_ref, two_ref, trim=None):
    tall, width = band.shape
    lane = iota((tall, width), 1)
    ones = jnp.where(iota((8, width), 0) < 2, 1.0, 0.0)
    high = band.astype(BF16).astype(F32)
    low = band - high

    def moved(value):
        return (
            jnp.where(lane == 0, 0.0, pltpu.roll(value, 1, 1)),
            jnp.where(lane == width - 1, 0.0, pltpu.roll(value, width - 1, 1)),
        )

    shifted = []
    for value in (high, low):
        left, right = moved(value)
        shifted.append([left, value, right])
    stack = jnp.concatenate(shifted[0] + shifted[1] + shifted[0] + [ones], axis=0).astype(BF16)
    hidden = jnp.maximum(mm(one_ref[...], stack), 0.0)
    if trim is not None:
        inner = one_ref.shape[0] // BAND
        first, last = trim
        hidden = jnp.concatenate(
            [
                jnp.where(first, 0.0, hidden[:inner]),
                hidden[inner:-inner],
                jnp.where(last, 0.0, hidden[-inner:]),
            ],
            axis=0,
        )
    taps = mm(two_ref[...], hidden.astype(BF16))
    parts = [
        taps[b * tall : (b + 1) * tall] + taps[(3 + b) * tall : (4 + b) * tall] for b in range(3)
    ]
    return parts[1] + moved(parts[0])[0] + moved(parts[2])[1]


def prior_kernel(main_ref, near_ref, one_ref, two_ref, sum_ref, base_ref):
    rows, width = main_ref.shape
    tall = BAND + 2
    main, near = main_ref[...], near_ref[...]
    even = (lax.axis_index("facet") & 1) == 0
    base_ref[8 : rows + 8, :] = main
    base_ref[6:8, :] = near
    base_ref[rows + 8 : rows + 10, :] = near
    sum_ref[0:8, :] = jnp.zeros((8, width), F32)
    sum_ref[8 : rows + 8, :] = main
    sum_ref[rows + 8 :, :] = jnp.zeros((8, width), F32)
    spots = [slice(k * BAND + 6, k * BAND + 6 + tall) for k in range((rows + 2) // BAND)]
    for spot in spots[1:-1]:
        share = band_prior(base_ref[spot, :], one_ref, two_ref)
        sum_ref[spot, :] = sum_ref[spot, :] + share
    band = jnp.where(even, base_ref[spots[-1], :], base_ref[spots[0], :])
    share = band_prior(band, one_ref, two_ref)
    sum_ref[spots[0], :] = sum_ref[spots[0], :] + jnp.where(even, 0.0, share)
    sum_ref[spots[-1], :] = sum_ref[spots[-1], :] + jnp.where(even, share, 0.0)


def edge_kernel(count, part, sum_ref, main_ref, far_ref, one_ref, two_ref, out_ref, base_ref, all_ref):
    rows, _ = main_ref.shape
    tall = BAND + 2
    place = lax.axis_index("facet")
    last = lax.axis_size("facet") - 1
    even = (place & 1) == 0
    far = far_ref[...]
    base_ref[0:2, :] = far
    base_ref[2:tall, :] = main_ref[0:BAND, :]
    base_ref[32 : 32 + BAND, :] = main_ref[rows - BAND : rows, :]
    base_ref[32 + BAND : 32 + tall, :] = far
    band = jnp.where(even, base_ref[0:tall, :], base_ref[32 : 32 + tall, :])
    share = band_prior(band, one_ref, two_ref, (place == 0, place == last))
    all_ref[...] = sum_ref[...]
    head, tail = slice(6, 6 + tall), slice(rows + 10 - tall, rows + 10)
    all_ref[head, :] = all_ref[head, :] + jnp.where(even, share, 0.0)
    all_ref[tail, :] = all_ref[tail, :] + jnp.where(even, 0.0, share)
    me = lax.axis_index("freq")
    start, _ = window(me, count, part * count)
    out_ref[...] = all_ref[8 : rows + 8, pl.ds(pl.multiple_of(me * part - start, LANES), part)]


def unpack_kernel(dest_ref, back_ref, out_ref):
    tiles = dest_ref.shape[1]
    total, width = back_ref.shape
    placing = one_hot(iota((total, tiles), 0) == dest_ref[...])
    mine = mm(placing, back_ref[...], ((0,), (0,))).astype(BF16)
    out_ref[...] = mm(mine, swap_matrix(width)).astype(BF16)


def shape(dims, dtype):
    return jax.ShapeDtypeStruct(dims, dtype)


def call(kernel, out_shape, flops, scratch=(), loaded=(), saved=(), limit=16):
    near = pl.BlockSpec(memory_space=pltpu.VMEM)
    far = pl.BlockSpec(memory_space=pltpu.HBM)

    def run(*args):
        return pl.pallas_call(
            kernel,
            out_shape=out_shape,
            in_specs=[far if i in loaded else near for i in range(len(args))],
            out_specs=[far if i in saved else near for i in range(len(out_shape))]
            if isinstance(out_shape, list)
            else near,
            scratch_shapes=scratch,
            compiler_params=pltpu.CompilerParams(vmem_limit_bytes=limit << 20),
            cost_estimate=pl.CostEstimate(flops=flops, bytes_accessed=4 << 20, transcendentals=0),
        )(*args)

    return run


def on_device(sky, beam, observed, facet_of, tile_slot, conv_first, bias_first, conv_second):
    rows, cols = sky.shape
    beam = beam.reshape(rows, cols)
    facets = lax.axis_size("facet")
    count = lax.axis_size("freq")
    tiles, width = observed.shape
    cap = 2 * tiles // facets
    total = facets * cap
    slots = (rows // S) * (cols // S)
    hidden = conv_first.shape[0]
    row_f, twist_f, mat_f = tables(rows, cols, -1)
    row_b, twist_b, mat_b = tables(rows, cols, 1)

    deep = (width // LANES) * cap + 8
    send, dest = call(
        functools.partial(pack_kernel, facets, cap),
        [shape((facets, deep, LANES), BF16), shape((1, tiles), jnp.int32)],
        1 << 28,
        scratch=[
            pltpu.VMEM((1, tiles), jnp.int32),
            pltpu.VMEM((1, tiles), jnp.int32),
            pltpu.VMEM((tiles, width), BF16),
            pltpu.SemaphoreType.DMA((3,)),
        ],
        loaded=(0, 1, 2),
    )(
        *(
            pltpu.with_memory_space_constraint(value, pltpu.HBM)
            for value in (facet_of.reshape(1, tiles), tile_slot.reshape(1, tiles), observed)
        )
    )
    got = lax.all_to_all(send, "facet", split_axis=0, concat_axis=0, tiled=True)

    high, low, first, second = call(
        forward_kernel,
        [
            shape((width, slots), BF16),
            shape((width, slots), BF16),
            shape((hidden * BAND, 9 * (BAND + 2) + 8), BF16),
            shape((6 * (BAND + 2), hidden * BAND), BF16),
        ],
        1 << 30,
    )(
        sky,
        beam,
        row_f,
        twist_f,
        mat_f,
        conv_first.transpose(1, 2, 0),
        bias_first.reshape(1, hidden),
        conv_second.transpose(1, 2, 0),
    )

    residual, select, own = call(
        functools.partial(residual_kernel, facets, cap),
        [shape((total, width), BF16), shape((total, slots), BF16), shape((total, width), BF16)],
        1 << 30,
        scratch=[pltpu.SemaphoreType.DMA((4,))],
        saved=(0,),
    )(got, *(pltpu.with_memory_space_constraint(value, pltpu.VMEM) for value in (high, low)))
    returned = lax.all_to_all(
        residual.reshape(facets, cap, width), "facet", split_axis=0, concat_axis=0, tiled=True
    ).reshape(total, width)

    _, wide = window(0, count, cols)
    keep, *sends = call(
        functools.partial(inverse_kernel, count),
        [shape((rows, wide), F32)] + [shape((rows, wide), BF16)] * (count - 1),
        1 << 30,
        scratch=[
            pltpu.VMEM((rows, wide), F32),
            pltpu.VMEM((rows, cols), F32),
            pltpu.VMEM((4 * rows, cols), BF16),
            pltpu.VMEM((rows, cols), F32),
            pltpu.SemaphoreType.DMA((2,)),
        ],
        loaded=(5, 6),
    )(
        own,
        select,
        row_b,
        twist_b,
        mat_b,
        *(pltpu.with_memory_space_constraint(value, pltpu.HBM) for value in (sky, beam)),
    )

    def beside(value, to):
        pairs = [(p, to(p)) for p in range(facets) if 0 <= to(p) < facets]
        return lax.ppermute(value, "facet", pairs)

    gots = [
        lax.ppermute(value, "freq", [(f, (f + d + 1) % count) for f in range(count)])
        for d, value in enumerate(sends)
    ]
    main, near, far = call(
        sum_kernel,
        [shape((rows, wide), F32), shape((2, wide), F32), shape((2, wide), F32)],
        1 << 24,
    )(keep, *gots)
    far = beside(far, lambda p: p + 1 if p & 1 else p - 1)
    near = beside(near, lambda p: p ^ 1)
    tall_rows = pltpu.VMEM((rows + 16, wide), F32)
    partial = call(
        prior_kernel, shape((rows + 16, wide), F32), 1 << 31, scratch=[tall_rows]
    )(main, near, first, second)
    image = call(
        functools.partial(edge_kernel, count, cols // count),
        shape((rows, cols // count), F32),
        1 << 30,
        scratch=[pltpu.VMEM((64, wide), F32), tall_rows],
    )(partial, main, far, first, second)

    tiles_out = call(unpack_kernel, shape((tiles, width), BF16), 1 << 28)(dest, returned)
    return tiles_out, image


def solution(mesh):
    placed = (
        P("facet", None),
        P("freq", "facet", None),
        P(("freq", "facet"), None),
        P(("freq", "facet")),
        P(("freq", "facet")),
        P(),
        P(),
        P(),
    )

    return jax.shard_map(
        on_device,
        mesh=mesh,
        in_specs=placed,
        out_specs=(P(("freq", "facet"), None), P("facet", "freq")),
        check_vma=False,
    )
```

```python
import functools
import math

import jax
import jax.numpy as jnp
import numpy as np
from jax import lax
from jax.experimental import pallas as pl
from jax.experimental.pallas import tpu as pltpu
from jax.sharding import PartitionSpec as P


S = 16
LANES = 128
BAND = 22
STEP = 0.5
F32 = jnp.float32
BF16 = jnp.bfloat16


def iota(shape, dim):
    return lax.broadcasted_iota(jnp.int32, shape, dim)


def mm(a, b, dims=((1,), (0,))):
    return lax.dot_general(a, b, (dims, ((), ())), preferred_element_type=F32)


def one_hot(cond):
    return jnp.where(cond, 1.0, 0.0).astype(BF16)


def split(x):
    high = x.astype(BF16)
    return high, (x - high.astype(F32)).astype(BF16)


def np_split(x):
    x = np.asarray(x, np.float32)
    high = x.astype(BF16)
    return high, (x - high.astype(np.float32)).astype(BF16)


def tables(rows, cols, sign):
    outer = cols // LANES
    scale = 1.0 / math.sqrt(rows * cols)
    k = np.arange(rows)
    angle = sign * 2.0 * np.pi * ((k[:, None] * k[None, :]) % rows) / rows
    cos_r, sin_r = np.cos(angle) * scale, np.sin(angle) * scale
    if sign < 0:
        row_high, row_low = np_split(np.concatenate([cos_r, sin_r], 0))
        row = np.concatenate([row_high, row_high, row_low], 1)
    else:
        row_high, row_low = np_split(np.concatenate([cos_r, -sin_r], 1))
        row = np.concatenate([row_high, row_high, row_low], 1)
    i2 = np.arange(LANES)
    w = np.arange(outer)
    twist = sign * 2.0 * np.pi * ((w[:, None] * i2[None, :]) % cols) / cols
    inner = sign * 2.0 * np.pi * ((i2[:, None] * i2[None, :]) % LANES) / LANES
    c, s = np.cos(inner), np.sin(inner)
    mat_high, mat_low = np_split(np.block([[c, s], [-s, c]]))
    return (
        row,
        np.stack([np.cos(twist), np.sin(twist)]).astype(np.float32),
        np.stack([mat_high, mat_low]),
    )


def times_i(z, sign):
    re, im = z
    return (-im, re) if sign > 0 else (im, -re)


def add(a, b):
    return (a[0] + b[0], a[1] + b[1])


def sub(a, b):
    return (a[0] - b[0], a[1] - b[1])


def dft4(x, sign):
    s0, s1 = add(x[0], x[2]), sub(x[0], x[2])
    s2, s3 = add(x[1], x[3]), times_i(sub(x[1], x[3]), sign)
    return [add(s0, s2), add(s1, s3), sub(s0, s2), sub(s1, s3)]


def dft16(x, sign):
    mid = [dft4([x[4 * a + b] for a in range(4)], sign) for b in range(4)]
    out = [None] * 16
    for c in range(4):
        turned = []
        for b in range(4):
            re, im = mid[b][c]
            phase = (b * c) % 16
            if phase == 0:
                turned.append((re, im))
            elif phase == 4:
                turned.append(times_i((re, im), sign))
            else:
                wr = math.cos(2.0 * math.pi * phase / 16)
                wi = sign * math.sin(2.0 * math.pi * phase / 16)
                turned.append((re * wr - im * wi, re * wi + im * wr))
        for d, value in enumerate(dft4(turned, sign)):
            out[c + 4 * d] = value
    return out


def swap_matrix(size):
    src = iota((1, size), 1)
    swapped = (src & -256) | ((src & 15) << 4) | ((src >> 4) & 15)
    return one_hot(iota((size, size), 0) == swapped)


def pack_kernel(facets, cap, facet_hbm, slot_hbm, seen_hbm, send_ref, dest_ref, facet_ref, slot_ref, seen_ref, sems):
    tiles, width = seen_ref.shape
    total = facets * cap
    loads = [
        pltpu.make_async_copy(src, dst, sems.at[i])
        for i, (src, dst) in enumerate(
            ((facet_hbm, facet_ref), (slot_hbm, slot_ref), (seen_hbm, seen_ref))
        )
    ]
    for load in loads:
        load.start()
    swap = swap_matrix(width)
    loads[0].wait()
    facet = facet_ref[...]
    member = iota((facets, tiles), 0) == facet
    member_f = jnp.where(member, 1.0, 0.0)
    before = one_hot(iota((tiles, tiles), 0) < iota((tiles, tiles), 1))
    ranks = mm(member_f.astype(BF16), before)
    rank = jnp.sum(member_f * ranks, axis=0, keepdims=True).astype(jnp.int32)
    dest = facet * cap + rank
    dest_ref[...] = dest
    placing = one_hot(iota((total, tiles), 0) == dest)
    loads[2].wait()
    turned = mm(seen_ref[...], swap).astype(BF16)
    packed = mm(placing, turned).astype(BF16)
    loads[1].wait()
    code = slot_ref[...] + 1
    lane = iota((LANES, tiles), 0)
    slots = mm(
        (member_f * (code >> 4).astype(F32)).astype(BF16), one_hot(lane == rank), ((1,), (1,))
    ) + mm(
        (member_f * (code & 15).astype(F32)).astype(BF16),
        one_hot(lane - LANES // 2 == rank),
        ((1,), (1,)),
    )
    parts = width // LANES
    for d in range(facets):
        for part in range(parts):
            send_ref[d, part * cap : (part + 1) * cap, :] = packed[
                d * cap : (d + 1) * cap, part * LANES : (part + 1) * LANES
            ]
        send_ref[d, parts * cap : parts * cap + 8, :] = jnp.broadcast_to(
            slots[d : d + 1, :], (8, LANES)
        ).astype(BF16)


def forward_kernel(
    sky_ref,
    beam_ref,
    row_ref,
    twist_ref,
    mat_ref,
    first_ref,
    bias_ref,
    second_ref,
    high_ref,
    low_ref,
    one_ref,
    two_ref,
):
    prepare(first_ref, bias_ref, second_ref, one_ref, two_ref)
    rows, cols = sky_ref.shape
    outer = cols // LANES
    weighted = sky_ref[...] * beam_ref[...]
    w_high, w_low = split(weighted)
    mid = mm(row_ref[...], jnp.concatenate([w_high, w_low, w_high], axis=0))
    lines = [
        (
            mid[:rows, i * LANES : (i + 1) * LANES],
            mid[rows:, i * LANES : (i + 1) * LANES],
        )
        for i in range(outer)
    ]
    spread = dft16(lines, -1)
    blocks = []
    for w in range(outer):
        re, im = spread[w]
        tr, ti = twist_ref[0, w : w + 1, :], twist_ref[1, w : w + 1, :]
        blocks.append(jnp.concatenate([re * tr - im * ti, re * ti + im * tr], axis=1))
    high, low = split(jnp.concatenate(blocks, axis=0))
    mat_high, mat_low = mat_ref[0], mat_ref[1]
    model = mm(high, mat_high) + mm(low, mat_high) + mm(high, mat_low)
    for w in range(outer):
        for r in range(rows // S):
            for e in range(2):
                piece = model[
                    w * rows + r * S : w * rows + (r + 1) * S, e * LANES : (e + 1) * LANES
                ]
                piece_high, piece_low = split(piece)
                at = (pl.ds(e * 256 + w * S, S), pl.ds(r * LANES, LANES))
                high_ref[at] = piece_high
                low_ref[at] = piece_low


def residual_kernel(facets, cap, got_ref, high_ref, low_ref, res_hbm, sel_ref, own_ref, sems):
    total = facets * cap
    slots = high_ref.shape[1]
    parts = high_ref.shape[0] // LANES
    code = got_ref[:, parts * cap : parts * cap + 8, :].astype(F32).reshape(facets * 8, LANES)
    source = iota((total, facets * 8), 0) // cap
    spread = mm(one_hot(iota((total, facets * 8), 1) == source * 8), code.astype(BF16))
    lane = iota((total, LANES), 1)
    rank = iota((total, LANES), 0) % cap
    kept = jnp.where((lane & (LANES // 2 - 1)) == rank, spread, 0.0).astype(BF16)
    digit = jnp.where(iota((LANES, slots), 0) < LANES // 2, 16.0, 1.0).astype(BF16)
    code_all = mm(kept, digit)
    sel = one_hot(code_all.astype(jnp.int32) == iota((total, slots), 1) + 1)
    sel_ref[...] = sel
    contract = ((1,), (1,))
    predicted = mm(sel, high_ref[...], contract) + mm(sel, low_ref[...], contract)
    saves = []
    pieces = sems.shape[0]
    for i in range(pieces):
        here = facets // pieces
        at = slice(i * here * cap, (i + 1) * here * cap)
        for part in range(parts):
            cols = slice(part * LANES, (part + 1) * LANES)
            seen = got_ref[i * here : (i + 1) * here, part * cap : (part + 1) * cap, :]
            seen = seen.astype(F32).reshape(here * cap, LANES)
            own_ref[at, cols] = (predicted[at, cols] - seen).astype(BF16)
        save = pltpu.make_async_copy(own_ref.at[at, :], res_hbm.at[at, :], sems.at[i])
        save.start()
        saves.append(save)
    for save in saves:
        save.wait()


def window(index, count, cols):
    part = cols // count
    width = min(cols, part + (LANES if count == 2 else 2 * LANES))
    return jnp.clip(index * part - LANES, 0, cols - width), width


def inverse_kernel(
    count,
    res_ref,
    sel_ref,
    row_ref,
    twist_ref,
    mat_ref,
    sky_hbm,
    beam_hbm,
    keep_ref,
    *rest,
):
    send_refs = rest[: count - 1]
    rim_ref, sky_ref, edge_ref, beam_ref, lines_ref, shift_ref, sems = rest[count - 1 :]
    rows, cols = beam_ref.shape
    outer = cols // LANES
    me = lax.axis_index("freq")
    start, width = window(me, count, cols)
    sky_part = sky_hbm.at[:, pl.ds(pl.multiple_of(start, LANES), width)]
    loads = [
        pltpu.make_async_copy(beam_hbm, beam_ref, sems.at[0]),
        pltpu.make_async_copy(sky_part, sky_ref, sems.at[1]),
        pltpu.make_async_copy(sky_hbm.at[0:8, :], edge_ref.at[0:8, :], sems.at[2]),
        pltpu.make_async_copy(sky_hbm.at[rows - 8 : rows, :], edge_ref.at[8:16, :], sems.at[3]),
    ]
    for load in loads:
        load.start()
    grid = mm(res_ref[...], sel_ref[...], ((0,), (0,)))
    blocks = []
    for w in range(outer):
        blocks.append(
            jnp.concatenate(
                [
                    jnp.concatenate(
                        [
                            grid[
                                e * 256 + w * S : e * 256 + (w + 1) * S,
                                r * LANES : (r + 1) * LANES,
                            ]
                            for e in range(2)
                        ],
                        axis=1,
                    )
                    for r in range(rows // S)
                ],
                axis=0,
            )
        )
    high, low = split(jnp.concatenate(blocks, axis=0))
    mat_high, mat_low = mat_ref[0], mat_ref[1]
    mid = mm(high, mat_high) + mm(low, mat_high) + mm(high, mat_low)
    lines = []
    for w in range(outer):
        re = mid[w * rows : (w + 1) * rows, :LANES]
        im = mid[w * rows : (w + 1) * rows, LANES:]
        tr, ti = twist_ref[0, w : w + 1, :], twist_ref[1, w : w + 1, :]
        lines.append((re * tr - im * ti, re * ti + im * tr))
    spread = dft16(lines, 1)
    for i, pair in enumerate(spread):
        for e in range(2):
            high, low = split(pair[e])
            lines_ref[e * rows : (e + 1) * rows, i * LANES : (i + 1) * LANES] = high
            lines_ref[(2 + e) * rows : (3 + e) * rows, i * LANES : (i + 1) * LANES] = low
    back = mm(row_ref[:, : 4 * rows], lines_ref[...]) + mm(
        row_ref[:, 4 * rows :], lines_ref[: 2 * rows, :]
    )
    for load in loads:
        load.wait()
    shift_ref[...] = back * beam_ref[...] * (-STEP)
    even = (lax.axis_index("facet") & 1) == 0
    rim_ref[0:2, :] = jnp.where(even, shift_ref[0:2, :], shift_ref[rows - 2 : rows, :])
    rim_ref[2:4, :] = jnp.where(even, edge_ref[0:2, :], edge_ref[14:16, :])
    for d in range(count):
        start, width = window(lax.rem(me + d, count), count, cols)
        at = pl.ds(pl.multiple_of(start, LANES), width)
        if d == 0:
            keep_ref[...] = shift_ref[:, at] + sky_ref[...]
        else:
            send_refs[d - 1][...] = shift_ref[:, at].astype(BF16)


def sum_kernel(keep_ref, *refs):
    main_ref, near_ref = refs[-2:]
    rows = keep_ref.shape[0]
    main = keep_ref[...]
    for ref in refs[:-2]:
        main = main + ref[...].astype(F32)
    main_ref[...] = main
    even = (lax.axis_index("facet") & 1) == 0
    near_ref[...] = jnp.where(even, main[rows - 2 : rows], main[0:2])


def prepare(first_ref, bias_ref, second_ref, one_ref, two_ref):
    hidden = first_ref.shape[2]
    depth = one_ref.shape[1]
    full = (BAND + 2) * 9
    bias_high, bias_low = split(bias_ref[...])
    line = iota((8, depth), 0)
    lane = iota((8, depth), 1)
    group = lane * 2731 >> 16
    term = group * 86 >> 8
    col = group - term * 3
    taps = one_hot(((line == col) & (term < 2)) | ((line - 3 == col) & (term == 2)))
    ends = one_hot(((line == 6) & (lane == full)) | ((line == 7) & (lane == full + 1)))
    values = []
    for a in range(3):
        high, low = split(first_ref[a])
        pieces = [high, low, bias_high, bias_low]
        weights = jnp.concatenate([p.astype(F32) for p in pieces], axis=0).astype(BF16)
        values.append(mm(weights, taps, ((0,), (0,))))
        if a == 0:
            offset = mm(weights, ends, ((0,), (0,)))
    lane = iota((hidden, depth), 1)
    yin = lane - (lane * 2731 >> 16) * (BAND + 2)
    for y in range(BAND):
        block = offset
        for a in range(3):
            block = block + jnp.where(yin == y + a, values[a], 0.0)
        one_ref[y * hidden : (y + 1) * hidden, :] = block.astype(BF16)

    wide = two_ref.shape[1]
    tall = BAND + 2
    expand = one_hot(iota((hidden, wide), 0) == (iota((hidden, wide), 1) & (hidden - 1)))
    pieces = [split(second_ref[a]) for a in range(3)]
    gap = iota((tall, wide), 1) // hidden + 2 - iota((tall, wide), 0)
    blocks = []
    for half in range(2):
        lines = [mm(pieces[a][half], expand) for a in range(3)]
        for b in range(3):
            total = jnp.zeros((tall, wide), F32)
            for a in range(3):
                total = jnp.where(gap == a, lines[a][b : b + 1, :], total)
            blocks.append(total)
    two_ref[...] = jnp.concatenate(blocks, axis=0).astype(BF16)


def band_prior(band, one_ref, two_ref, trim=None):
    tall, width = band.shape
    lane = iota((tall, width), 1)
    ones = jnp.where(iota((8, width), 0) < 2, 1.0, 0.0)
    high = band.astype(BF16).astype(F32)
    low = band - high

    def moved(value):
        return (
            jnp.where(lane == 0, 0.0, pltpu.roll(value, 1, 1)),
            jnp.where(lane == width - 1, 0.0, pltpu.roll(value, width - 1, 1)),
        )

    shifted = []
    for value in (high, low):
        left, right = moved(value)
        shifted.append([left, value, right])
    stack = jnp.concatenate(shifted[0] + shifted[1] + shifted[0] + [ones], axis=0).astype(BF16)
    hidden = jnp.maximum(mm(one_ref[...], stack), 0.0)
    if trim is not None:
        inner = one_ref.shape[0] // BAND
        first, last = trim
        hidden = jnp.concatenate(
            [
                jnp.where(first, 0.0, hidden[:inner]),
                hidden[inner:-inner],
                jnp.where(last, 0.0, hidden[-inner:]),
            ],
            axis=0,
        )
    taps = mm(two_ref[...], hidden.astype(BF16))
    parts = [
        taps[b * tall : (b + 1) * tall] + taps[(3 + b) * tall : (4 + b) * tall] for b in range(3)
    ]
    return parts[1] + moved(parts[0])[0] + moved(parts[2])[1]


def prior_kernel(main_ref, near_ref, one_ref, two_ref, sum_ref, base_ref):
    rows, width = main_ref.shape
    tall = BAND + 2
    main, near = main_ref[...], near_ref[...]
    even = (lax.axis_index("facet") & 1) == 0
    base_ref[8 : rows + 8, :] = main
    base_ref[6:8, :] = near
    base_ref[rows + 8 : rows + 10, :] = near
    sum_ref[0:8, :] = jnp.zeros((8, width), F32)
    sum_ref[8 : rows + 8, :] = main
    sum_ref[rows + 8 :, :] = jnp.zeros((8, width), F32)
    spots = [slice(k * BAND + 6, k * BAND + 6 + tall) for k in range((rows + 2) // BAND)]
    for spot in spots[1:-1]:
        share = band_prior(base_ref[spot, :], one_ref, two_ref)
        sum_ref[spot, :] = sum_ref[spot, :] + share
    band = jnp.where(even, base_ref[spots[-1], :], base_ref[spots[0], :])
    share = band_prior(band, one_ref, two_ref)
    sum_ref[spots[0], :] = sum_ref[spots[0], :] + jnp.where(even, 0.0, share)
    sum_ref[spots[-1], :] = sum_ref[spots[-1], :] + jnp.where(even, share, 0.0)


def edge_kernel(count, part, sum_ref, main_ref, *refs):
    far_refs = refs[:count]
    one_ref, two_ref, out_ref, base_ref, all_ref = refs[count:]
    rows, width = main_ref.shape
    tall = BAND + 2
    place = lax.axis_index("facet")
    last = lax.axis_size("facet") - 1
    even = (place & 1) == 0
    me = lax.axis_index("freq")
    start, _ = window(me, count, part * count)
    at = pl.ds(pl.multiple_of(start, LANES), width)
    far = far_refs[0][2:4, at]
    for ref in far_refs:
        far = far + ref[0:2, at]
    base_ref[0:2, :] = far
    base_ref[2:tall, :] = main_ref[0:BAND, :]
    base_ref[32 : 32 + BAND, :] = main_ref[rows - BAND : rows, :]
    base_ref[32 + BAND : 32 + tall, :] = far
    band = jnp.where(even, base_ref[0:tall, :], base_ref[32 : 32 + tall, :])
    share = band_prior(band, one_ref, two_ref, (place == 0, place == last))
    all_ref[...] = sum_ref[...]
    head, tail = slice(6, 6 + tall), slice(rows + 10 - tall, rows + 10)
    all_ref[head, :] = all_ref[head, :] + jnp.where(even, share, 0.0)
    all_ref[tail, :] = all_ref[tail, :] + jnp.where(even, 0.0, share)
    out_ref[...] = all_ref[8 : rows + 8, pl.ds(pl.multiple_of(me * part - start, LANES), part)]


def unpack_kernel(dest_ref, back_ref, out_ref):
    tiles = dest_ref.shape[1]
    total, width = back_ref.shape
    placing = one_hot(iota((total, tiles), 0) == dest_ref[...])
    mine = mm(placing, back_ref[...], ((0,), (0,))).astype(BF16)
    out_ref[...] = mm(mine, swap_matrix(width)).astype(BF16)


def shape(dims, dtype):
    return jax.ShapeDtypeStruct(dims, dtype)


def call(kernel, out_shape, flops, scratch=(), loaded=(), saved=(), limit=16):
    near = pl.BlockSpec(memory_space=pltpu.VMEM)
    far = pl.BlockSpec(memory_space=pltpu.HBM)

    def run(*args):
        return pl.pallas_call(
            kernel,
            out_shape=out_shape,
            in_specs=[far if i in loaded else near for i in range(len(args))],
            out_specs=[far if i in saved else near for i in range(len(out_shape))]
            if isinstance(out_shape, list)
            else near,
            scratch_shapes=scratch,
            compiler_params=pltpu.CompilerParams(vmem_limit_bytes=limit << 20),
            cost_estimate=pl.CostEstimate(flops=flops, bytes_accessed=4 << 20, transcendentals=0),
        )(*args)

    return run


def on_device(sky, beam, observed, facet_of, tile_slot, conv_first, bias_first, conv_second):
    rows, cols = sky.shape
    beam = beam.reshape(rows, cols)
    facets = lax.axis_size("facet")
    count = lax.axis_size("freq")
    tiles, width = observed.shape
    cap = 2 * tiles // facets
    total = facets * cap
    slots = (rows // S) * (cols // S)
    hidden = conv_first.shape[0]
    row_f, twist_f, mat_f = tables(rows, cols, -1)
    row_b, twist_b, mat_b = tables(rows, cols, 1)

    deep = (width // LANES) * cap + 8
    send, dest = call(
        functools.partial(pack_kernel, facets, cap),
        [shape((facets, deep, LANES), BF16), shape((1, tiles), jnp.int32)],
        1 << 28,
        scratch=[
            pltpu.VMEM((1, tiles), jnp.int32),
            pltpu.VMEM((1, tiles), jnp.int32),
            pltpu.VMEM((tiles, width), BF16),
            pltpu.SemaphoreType.DMA((3,)),
        ],
        loaded=(0, 1, 2),
    )(
        *(
            pltpu.with_memory_space_constraint(value, pltpu.HBM)
            for value in (facet_of.reshape(1, tiles), tile_slot.reshape(1, tiles), observed)
        )
    )
    got = lax.all_to_all(send, "facet", split_axis=0, concat_axis=0, tiled=True)

    high, low, first, second = call(
        forward_kernel,
        [
            shape((width, slots), BF16),
            shape((width, slots), BF16),
            shape((hidden * BAND, 9 * (BAND + 2) + 8), BF16),
            shape((6 * (BAND + 2), hidden * BAND), BF16),
        ],
        1 << 30,
    )(
        sky,
        beam,
        row_f,
        twist_f,
        mat_f,
        conv_first.transpose(1, 2, 0),
        bias_first.reshape(1, hidden),
        conv_second.transpose(1, 2, 0),
    )

    residual, select, own = call(
        functools.partial(residual_kernel, facets, cap),
        [shape((total, width), BF16), shape((total, slots), BF16), shape((total, width), BF16)],
        1 << 30,
        scratch=[pltpu.SemaphoreType.DMA((4,))],
        saved=(0,),
    )(got, *(pltpu.with_memory_space_constraint(value, pltpu.VMEM) for value in (high, low)))
    returned = lax.all_to_all(
        residual.reshape(facets, cap, width), "facet", split_axis=0, concat_axis=0, tiled=True
    ).reshape(total, width)

    _, wide = window(0, count, cols)
    keep, *shares, rim = call(
        functools.partial(inverse_kernel, count),
        [shape((rows, wide), F32)]
        + [shape((rows, wide), BF16)] * (count - 1)
        + [shape((4, cols), F32)],
        1 << 30,
        scratch=[
            pltpu.VMEM((rows, wide), F32),
            pltpu.VMEM((16, cols), F32),
            pltpu.VMEM((rows, cols), F32),
            pltpu.VMEM((4 * rows, cols), BF16),
            pltpu.VMEM((rows, cols), F32),
            pltpu.SemaphoreType.DMA((4,)),
        ],
        loaded=(5, 6),
    )(
        own,
        select,
        row_b,
        twist_b,
        mat_b,
        *(pltpu.with_memory_space_constraint(value, pltpu.HBM) for value in (sky, beam)),
    )

    def beside(value, to):
        pairs = [(p, to(p)) for p in range(facets) if 0 <= to(p) < facets]
        return lax.ppermute(value, "facet", pairs)

    def across(value, d):
        return lax.ppermute(value, "freq", [(f, (f + d) % count) for f in range(count)])

    gots = [across(value, d + 1) for d, value in enumerate(shares)]
    fars = [beside(rim, lambda p: p + 1 if p & 1 else p - 1)]
    main, near = call(
        sum_kernel, [shape((rows, wide), F32), shape((2, wide), F32)], 1 << 24
    )(keep, *gots)
    near = beside(near, lambda p: p ^ 1)
    fars += [across(fars[0], d) for d in range(1, count)]
    tall_rows = pltpu.VMEM((rows + 16, wide), F32)
    partial = call(
        prior_kernel, shape((rows + 16, wide), F32), 1 << 31, scratch=[tall_rows]
    )(main, near, first, second)
    image = call(
        functools.partial(edge_kernel, count, cols // count),
        shape((rows, cols // count), F32),
        1 << 30,
        scratch=[pltpu.VMEM((64, wide), F32), tall_rows],
    )(partial, main, *fars, first, second)

    tiles_out = call(unpack_kernel, shape((tiles, width), BF16), 1 << 28)(dest, returned)
    return tiles_out, image


def solution(mesh):
    placed = (
        P("facet", None),
        P("freq", "facet", None),
        P(("freq", "facet"), None),
        P(("freq", "facet")),
        P(("freq", "facet")),
        P(),
        P(),
        P(),
    )

    return jax.shard_map(
        on_device,
        mesh=mesh,
        in_specs=placed,
        out_specs=(P(("freq", "facet"), None), P("facet", "freq")),
        check_vma=False,
    )
```

```python
import functools
import math

import jax
import jax.numpy as jnp
import numpy as np
from jax import lax
from jax.experimental import pallas as pl
from jax.experimental.pallas import tpu as pltpu
from jax.sharding import PartitionSpec as P


S = 16
LANES = 128
BAND = 22
STEP = 0.5
F32 = jnp.float32
BF16 = jnp.bfloat16


def iota(shape, dim):
    return lax.broadcasted_iota(jnp.int32, shape, dim)


def mm(a, b, dims=((1,), (0,))):
    return lax.dot_general(a, b, (dims, ((), ())), preferred_element_type=F32)


def one_hot(cond):
    return jnp.where(cond, 1.0, 0.0).astype(BF16)


def split(x):
    high = x.astype(BF16)
    return high, (x - high.astype(F32)).astype(BF16)


def np_split(x):
    x = np.asarray(x, np.float32)
    high = x.astype(BF16)
    return high, (x - high.astype(np.float32)).astype(BF16)


def tables(rows, cols, sign):
    outer = cols // LANES
    scale = 1.0 / math.sqrt(rows * cols)
    k = np.arange(rows)
    angle = sign * 2.0 * np.pi * ((k[:, None] * k[None, :]) % rows) / rows
    cos_r, sin_r = np.cos(angle) * scale, np.sin(angle) * scale
    if sign < 0:
        row_high, row_low = np_split(np.concatenate([cos_r, sin_r], 0))
        row = np.concatenate([row_high, row_high, row_low], 1)
    else:
        row = np.concatenate(np_split(np.concatenate([cos_r, -sin_r], 1)), 1)
    i2 = np.arange(LANES)
    w = np.arange(outer)
    twist = sign * 2.0 * np.pi * ((w[:, None] * i2[None, :]) % cols) / cols
    inner = sign * 2.0 * np.pi * ((i2[:, None] * i2[None, :]) % LANES) / LANES
    c, s = np.cos(inner), np.sin(inner)
    mat_high, mat_low = np_split(np.block([[c, s], [-s, c]]))
    return (
        row,
        np.stack([np.cos(twist), np.sin(twist)]).astype(np.float32),
        np.stack([mat_high, mat_low]),
    )


def times_i(z, sign):
    re, im = z
    return (-im, re) if sign > 0 else (im, -re)


def add(a, b):
    return (a[0] + b[0], a[1] + b[1])


def sub(a, b):
    return (a[0] - b[0], a[1] - b[1])


def dft4(x, sign):
    s0, s1 = add(x[0], x[2]), sub(x[0], x[2])
    s2, s3 = add(x[1], x[3]), times_i(sub(x[1], x[3]), sign)
    return [add(s0, s2), add(s1, s3), sub(s0, s2), sub(s1, s3)]


def dft16(x, sign):
    mid = [dft4([x[4 * a + b] for a in range(4)], sign) for b in range(4)]
    out = [None] * 16
    for c in range(4):
        turned = []
        for b in range(4):
            re, im = mid[b][c]
            phase = (b * c) % 16
            if phase == 0:
                turned.append((re, im))
            elif phase == 4:
                turned.append(times_i((re, im), sign))
            else:
                wr = math.cos(2.0 * math.pi * phase / 16)
                wi = sign * math.sin(2.0 * math.pi * phase / 16)
                turned.append((re * wr - im * wi, re * wi + im * wr))
        for d, value in enumerate(dft4(turned, sign)):
            out[c + 4 * d] = value
    return out


def swap_matrix(size):
    src = iota((1, size), 1)
    swapped = (src & -256) | ((src & 15) << 4) | ((src >> 4) & 15)
    return one_hot(iota((size, size), 0) == swapped)


def pack_kernel(facets, cap, facet_hbm, slot_hbm, seen_hbm, send_ref, dest_ref, facet_ref, slot_ref, seen_ref, sems):
    tiles, width = seen_ref.shape
    total = facets * cap
    loads = [
        pltpu.make_async_copy(src, dst, sems.at[i])
        for i, (src, dst) in enumerate(
            ((facet_hbm, facet_ref), (slot_hbm, slot_ref), (seen_hbm, seen_ref))
        )
    ]
    for load in loads:
        load.start()
    swap = swap_matrix(width)
    loads[0].wait()
    facet = facet_ref[...]
    member = iota((facets, tiles), 0) == facet
    member_f = jnp.where(member, 1.0, 0.0)
    before = one_hot(iota((tiles, tiles), 0) < iota((tiles, tiles), 1))
    ranks = mm(member_f.astype(BF16), before)
    rank = jnp.sum(member_f * ranks, axis=0, keepdims=True).astype(jnp.int32)
    dest = facet * cap + rank
    dest_ref[...] = dest
    placing = one_hot(iota((total, tiles), 0) == dest)
    loads[2].wait()
    turned = mm(seen_ref[...], swap).astype(BF16)
    packed = mm(placing, turned).astype(BF16)
    loads[1].wait()
    code = slot_ref[...] + 1
    lane = iota((LANES, tiles), 0)
    slots = mm(
        (member_f * (code >> 4).astype(F32)).astype(BF16), one_hot(lane == rank), ((1,), (1,))
    ) + mm(
        (member_f * (code & 15).astype(F32)).astype(BF16),
        one_hot(lane - LANES // 2 == rank),
        ((1,), (1,)),
    )
    parts = width // LANES
    for d in range(facets):
        for part in range(parts):
            send_ref[d, part * cap : (part + 1) * cap, :] = packed[
                d * cap : (d + 1) * cap, part * LANES : (part + 1) * LANES
            ]
        send_ref[d, parts * cap : parts * cap + 8, :] = jnp.broadcast_to(
            slots[d : d + 1, :], (8, LANES)
        ).astype(BF16)


def forward_kernel(
    sky_ref,
    beam_ref,
    row_ref,
    twist_ref,
    mat_ref,
    first_ref,
    bias_ref,
    second_ref,
    high_ref,
    low_ref,
    one_ref,
    two_ref,
):
    prepare(first_ref, bias_ref, second_ref, one_ref, two_ref)
    rows, cols = sky_ref.shape
    outer = cols // LANES
    weighted = sky_ref[...] * beam_ref[...]
    w_high, w_low = split(weighted)
    mid = mm(row_ref[...], jnp.concatenate([w_high, w_low, w_high], axis=0))
    lines = [
        (
            mid[:rows, i * LANES : (i + 1) * LANES],
            mid[rows:, i * LANES : (i + 1) * LANES],
        )
        for i in range(outer)
    ]
    spread = dft16(lines, -1)
    blocks = []
    for w in range(outer):
        re, im = spread[w]
        tr, ti = twist_ref[0, w : w + 1, :], twist_ref[1, w : w + 1, :]
        blocks.append(jnp.concatenate([re * tr - im * ti, re * ti + im * tr], axis=1))
    high, low = split(jnp.concatenate(blocks, axis=0))
    mat_high, mat_low = mat_ref[0], mat_ref[1]
    model = mm(high, mat_high) + mm(low, mat_high) + mm(high, mat_low)
    for w in range(outer):
        for r in range(rows // S):
            for e in range(2):
                piece = model[
                    w * rows + r * S : w * rows + (r + 1) * S, e * LANES : (e + 1) * LANES
                ]
                piece_high, piece_low = split(piece)
                at = (pl.ds(e * 256 + w * S, S), pl.ds(r * LANES, LANES))
                high_ref[at] = piece_high
                low_ref[at] = piece_low


def residual_kernel(facets, cap, got_ref, high_ref, low_ref, res_hbm, sel_ref, own_ref, sems):
    total = facets * cap
    slots = high_ref.shape[1]
    parts = high_ref.shape[0] // LANES
    code = got_ref[:, parts * cap : parts * cap + 8, :].astype(F32).reshape(facets * 8, LANES)
    source = iota((total, facets * 8), 0) // cap
    spread = mm(one_hot(iota((total, facets * 8), 1) == source * 8), code.astype(BF16))
    lane = iota((total, LANES), 1)
    rank = iota((total, LANES), 0) % cap
    kept = jnp.where((lane & (LANES // 2 - 1)) == rank, spread, 0.0).astype(BF16)
    digit = jnp.where(iota((LANES, slots), 0) < LANES // 2, 16.0, 1.0).astype(BF16)
    code_all = mm(kept, digit)
    sel = one_hot(code_all.astype(jnp.int32) == iota((total, slots), 1) + 1)
    sel_ref[...] = sel
    contract = ((1,), (1,))
    predicted = mm(sel, high_ref[...], contract) + mm(sel, low_ref[...], contract)
    saves = []
    pieces = sems.shape[0]
    for i in range(pieces):
        here = facets // pieces
        at = slice(i * here * cap, (i + 1) * here * cap)
        for part in range(parts):
            cols = slice(part * LANES, (part + 1) * LANES)
            seen = got_ref[i * here : (i + 1) * here, part * cap : (part + 1) * cap, :]
            seen = seen.astype(F32).reshape(here * cap, LANES)
            own_ref[at, cols] = (predicted[at, cols] - seen).astype(BF16)
        save = pltpu.make_async_copy(own_ref.at[at, :], res_hbm.at[at, :], sems.at[i])
        save.start()
        saves.append(save)
    for save in saves:
        save.wait()


def window(index, count, cols):
    part = cols // count
    width = min(cols, part + (LANES if count == 2 else 2 * LANES))
    return jnp.clip(index * part - LANES, 0, cols - width), width


def inverse_kernel(
    count,
    res_ref,
    sel_ref,
    row_ref,
    twist_ref,
    mat_ref,
    sky_hbm,
    beam_hbm,
    keep_ref,
    *rest,
):
    send_refs = rest[: count - 1]
    sky_ref, beam_ref, lines_ref, shift_ref, sems = rest[count - 1 :]
    rows, cols = beam_ref.shape
    outer = cols // LANES
    me = lax.axis_index("freq")
    start, width = window(me, count, cols)
    sky_part = sky_hbm.at[:, pl.ds(pl.multiple_of(start, LANES), width)]
    loads = [
        pltpu.make_async_copy(beam_hbm, beam_ref, sems.at[0]),
        pltpu.make_async_copy(sky_part, sky_ref, sems.at[1]),
    ]
    for load in loads:
        load.start()
    grid = mm(res_ref[...], sel_ref[...], ((0,), (0,)))
    blocks = []
    for w in range(outer):
        blocks.append(
            jnp.concatenate(
                [
                    jnp.concatenate(
                        [
                            grid[
                                e * 256 + w * S : e * 256 + (w + 1) * S,
                                r * LANES : (r + 1) * LANES,
                            ]
                            for e in range(2)
                        ],
                        axis=1,
                    )
                    for r in range(rows // S)
                ],
                axis=0,
            )
        )
    cells = jnp.concatenate(blocks, axis=0).astype(BF16)
    mid = mm(jnp.concatenate([cells, cells], axis=1), mat_ref[...].reshape(4 * LANES, 2 * LANES))
    lines = []
    for w in range(outer):
        re = mid[w * rows : (w + 1) * rows, :LANES]
        im = mid[w * rows : (w + 1) * rows, LANES:]
        tr, ti = twist_ref[0, w : w + 1, :], twist_ref[1, w : w + 1, :]
        lines.append((re * tr - im * ti, re * ti + im * tr))
    spread = dft16(lines, 1)
    for i, pair in enumerate(spread):
        for e in range(2):
            line = pair[e].astype(BF16)
            lines_ref[e * rows : (e + 1) * rows, i * LANES : (i + 1) * LANES] = line
            lines_ref[(2 + e) * rows : (3 + e) * rows, i * LANES : (i + 1) * LANES] = line
    back = mm(row_ref[...], lines_ref[...])
    for load in loads:
        load.wait()
    shift_ref[...] = back * beam_ref[...] * (-STEP)
    for d in range(count):
        start, width = window(lax.rem(me + d, count), count, cols)
        at = pl.ds(pl.multiple_of(start, LANES), width)
        if d == 0:
            keep_ref[...] = shift_ref[:, at] + sky_ref[...]
        else:
            send_refs[d - 1][...] = shift_ref[:, at].astype(BF16)


def sum_kernel(keep_ref, *refs):
    main_ref, near_ref, far_ref = refs[-3:]
    rows = keep_ref.shape[0]
    main = keep_ref[...]
    for ref in refs[:-3]:
        main = main + ref[...].astype(F32)
    main_ref[...] = main
    even = (lax.axis_index("facet") & 1) == 0
    top, bottom = main[0:2], main[rows - 2 : rows]
    near_ref[...] = jnp.where(even, bottom, top)
    far_ref[...] = jnp.where(even, top, bottom)


def prepare(first_ref, bias_ref, second_ref, one_ref, two_ref):
    hidden = first_ref.shape[2]
    depth = one_ref.shape[1]
    full = (BAND + 2) * 9
    bias_high, bias_low = split(bias_ref[...])
    line = iota((8, depth), 0)
    lane = iota((8, depth), 1)
    group = lane * 2731 >> 16
    term = group * 86 >> 8
    col = group - term * 3
    taps = one_hot(((line == col) & (term < 2)) | ((line - 3 == col) & (term == 2)))
    ends = one_hot(((line == 6) & (lane == full)) | ((line == 7) & (lane == full + 1)))
    values = []
    for a in range(3):
        high, low = split(first_ref[a])
        pieces = [high, low, bias_high, bias_low]
        weights = jnp.concatenate([p.astype(F32) for p in pieces], axis=0).astype(BF16)
        values.append(mm(weights, taps, ((0,), (0,))))
        if a == 0:
            offset = mm(weights, ends, ((0,), (0,)))
    lane = iota((hidden, depth), 1)
    yin = lane - (lane * 2731 >> 16) * (BAND + 2)
    for y in range(BAND):
        block = offset
        for a in range(3):
            block = block + jnp.where(yin == y + a, values[a], 0.0)
        one_ref[y * hidden : (y + 1) * hidden, :] = block.astype(BF16)

    wide = two_ref.shape[1]
    tall = BAND + 2
    expand = one_hot(iota((hidden, wide), 0) == (iota((hidden, wide), 1) & (hidden - 1)))
    pieces = [split(second_ref[a]) for a in range(3)]
    gap = iota((tall, wide), 1) // hidden + 2 - iota((tall, wide), 0)
    blocks = []
    for half in range(2):
        lines = [mm(pieces[a][half], expand) for a in range(3)]
        for b in range(3):
            total = jnp.zeros((tall, wide), F32)
            for a in range(3):
                total = jnp.where(gap == a, lines[a][b : b + 1, :], total)
            blocks.append(total)
    two_ref[...] = jnp.concatenate(blocks, axis=0).astype(BF16)


def band_prior(band, one_ref, two_ref, trim=None):
    tall, width = band.shape
    lane = iota((tall, width), 1)
    ones = jnp.where(iota((8, width), 0) < 2, 1.0, 0.0)
    high = band.astype(BF16).astype(F32)
    low = band - high

    def moved(value):
        return (
            jnp.where(lane == 0, 0.0, pltpu.roll(value, 1, 1)),
            jnp.where(lane == width - 1, 0.0, pltpu.roll(value, width - 1, 1)),
        )

    shifted = []
    for value in (high, low):
        left, right = moved(value)
        shifted.append([left, value, right])
    stack = jnp.concatenate(shifted[0] + shifted[1] + shifted[0] + [ones], axis=0).astype(BF16)
    hidden = jnp.maximum(mm(one_ref[...], stack), 0.0)
    if trim is not None:
        inner = one_ref.shape[0] // BAND
        first, last = trim
        hidden = jnp.concatenate(
            [
                jnp.where(first, 0.0, hidden[:inner]),
                hidden[inner:-inner],
                jnp.where(last, 0.0, hidden[-inner:]),
            ],
            axis=0,
        )
    taps = mm(two_ref[...], hidden.astype(BF16))
    parts = [
        taps[b * tall : (b + 1) * tall] + taps[(3 + b) * tall : (4 + b) * tall] for b in range(3)
    ]
    return parts[1] + moved(parts[0])[0] + moved(parts[2])[1]


def prior_kernel(main_ref, near_ref, one_ref, two_ref, sum_ref, base_ref):
    rows, width = main_ref.shape
    tall = BAND + 2
    main, near = main_ref[...], near_ref[...]
    even = (lax.axis_index("facet") & 1) == 0
    base_ref[8 : rows + 8, :] = main
    base_ref[6:8, :] = near
    base_ref[rows + 8 : rows + 10, :] = near
    sum_ref[0:8, :] = jnp.zeros((8, width), F32)
    sum_ref[8 : rows + 8, :] = main
    sum_ref[rows + 8 :, :] = jnp.zeros((8, width), F32)
    spots = [slice(k * BAND + 6, k * BAND + 6 + tall) for k in range((rows + 2) // BAND)]
    for spot in spots[1:-1]:
        share = band_prior(base_ref[spot, :], one_ref, two_ref)
        sum_ref[spot, :] = sum_ref[spot, :] + share
    band = jnp.where(even, base_ref[spots[-1], :], base_ref[spots[0], :])
    share = band_prior(band, one_ref, two_ref)
    sum_ref[spots[0], :] = sum_ref[spots[0], :] + jnp.where(even, 0.0, share)
    sum_ref[spots[-1], :] = sum_ref[spots[-1], :] + jnp.where(even, share, 0.0)


def edge_kernel(
    count,
    part,
    sum_ref,
    main_ref,
    far_ref,
    one_ref,
    two_ref,
    out_hbm,
    base_ref,
    share_ref,
    last_ref,
    sems,
):
    rows, width = main_ref.shape
    tall = BAND + 2
    place = lax.axis_index("facet")
    final = lax.axis_size("facet") - 1
    even = (place & 1) == 0
    me = lax.axis_index("freq")
    start, _ = window(me, count, part * count)
    at = pl.ds(pl.multiple_of(me * part - start, LANES), part)
    done = rows - tall
    first = pl.multiple_of(jnp.where(even, tall, 0), 8)
    early = pltpu.make_async_copy(
        sum_ref.at[pl.ds(pl.multiple_of(first + 8, 8), done), at],
        out_hbm.at[pl.ds(first, done), :],
        sems.at[0],
    )
    early.start()
    far = far_ref[...]
    base_ref[0:2, :] = far
    base_ref[2:tall, :] = main_ref[0:BAND, :]
    base_ref[32 : 32 + BAND, :] = main_ref[rows - BAND : rows, :]
    base_ref[32 + BAND : 32 + tall, :] = far
    band = jnp.where(even, base_ref[0:tall, :], base_ref[32 : 32 + tall, :])
    share_ref[0:8, :] = jnp.zeros((8, width), F32)
    share_ref[8 : tall + 8, :] = band_prior(band, one_ref, two_ref, (place == 0, place == final))
    share_ref[tall + 8 : tall + 16, :] = jnp.zeros((8, width), F32)
    near_sum = jnp.where(even, sum_ref[8 : tall + 8, :], sum_ref[rows + 8 - tall : rows + 8, :])
    share = jnp.where(even, share_ref[10 : tall + 10, :], share_ref[6 : tall + 6, :])
    last_ref[...] = near_sum + share
    late = pltpu.make_async_copy(
        last_ref.at[:, at],
        out_hbm.at[pl.ds(pl.multiple_of(jnp.where(even, 0, done), 8), tall), :],
        sems.at[1],
    )
    late.start()
    early.wait()
    late.wait()


def unpack_kernel(dest_ref, back_ref, out_ref):
    tiles = dest_ref.shape[1]
    total, width = back_ref.shape
    placing = one_hot(iota((total, tiles), 0) == dest_ref[...])
    mine = mm(placing, back_ref[...], ((0,), (0,))).astype(BF16)
    out_ref[...] = mm(mine, swap_matrix(width)).astype(BF16)


def shape(dims, dtype):
    return jax.ShapeDtypeStruct(dims, dtype)


def call(kernel, out_shape, flops, scratch=(), loaded=(), saved=(), limit=16):
    near = pl.BlockSpec(memory_space=pltpu.VMEM)
    far = pl.BlockSpec(memory_space=pltpu.HBM)

    def run(*args):
        return pl.pallas_call(
            kernel,
            out_shape=out_shape,
            in_specs=[far if i in loaded else near for i in range(len(args))],
            out_specs=[far if i in saved else near for i in range(len(out_shape))]
            if isinstance(out_shape, list)
            else near,
            scratch_shapes=scratch,
            compiler_params=pltpu.CompilerParams(vmem_limit_bytes=limit << 20),
            cost_estimate=pl.CostEstimate(flops=flops, bytes_accessed=4 << 20, transcendentals=0),
        )(*args)

    return run


def on_device(sky, beam, observed, facet_of, tile_slot, conv_first, bias_first, conv_second):
    rows, cols = sky.shape
    beam = beam.reshape(rows, cols)
    facets = lax.axis_size("facet")
    count = lax.axis_size("freq")
    tiles, width = observed.shape
    cap = 2 * tiles // facets
    total = facets * cap
    slots = (rows // S) * (cols // S)
    hidden = conv_first.shape[0]
    row_f, twist_f, mat_f = tables(rows, cols, -1)
    row_b, twist_b, mat_b = tables(rows, cols, 1)

    deep = (width // LANES) * cap + 8
    send, dest = call(
        functools.partial(pack_kernel, facets, cap),
        [shape((facets, deep, LANES), BF16), shape((1, tiles), jnp.int32)],
        1 << 28,
        scratch=[
            pltpu.VMEM((1, tiles), jnp.int32),
            pltpu.VMEM((1, tiles), jnp.int32),
            pltpu.VMEM((tiles, width), BF16),
            pltpu.SemaphoreType.DMA((3,)),
        ],
        loaded=(0, 1, 2),
    )(
        *(
            pltpu.with_memory_space_constraint(value, pltpu.HBM)
            for value in (facet_of.reshape(1, tiles), tile_slot.reshape(1, tiles), observed)
        )
    )
    got = lax.all_to_all(send, "facet", split_axis=0, concat_axis=0, tiled=True)

    high, low, first, second = call(
        forward_kernel,
        [
            shape((width, slots), BF16),
            shape((width, slots), BF16),
            shape((hidden * BAND, 9 * (BAND + 2) + 8), BF16),
            shape((6 * (BAND + 2), hidden * BAND), BF16),
        ],
        1 << 30,
    )(
        sky,
        beam,
        row_f,
        twist_f,
        mat_f,
        conv_first.transpose(1, 2, 0),
        bias_first.reshape(1, hidden),
        conv_second.transpose(1, 2, 0),
    )

    residual, select, own = call(
        functools.partial(residual_kernel, facets, cap),
        [shape((total, width), BF16), shape((total, slots), BF16), shape((total, width), BF16)],
        1 << 30,
        scratch=[pltpu.SemaphoreType.DMA((4,))],
        saved=(0,),
    )(got, *(pltpu.with_memory_space_constraint(value, pltpu.VMEM) for value in (high, low)))
    returned = lax.all_to_all(
        residual.reshape(facets, cap, width), "facet", split_axis=0, concat_axis=0, tiled=True
    ).reshape(total, width)

    _, wide = window(0, count, cols)
    keep, *sends = call(
        functools.partial(inverse_kernel, count),
        [shape((rows, wide), F32)] + [shape((rows, wide), BF16)] * (count - 1),
        1 << 30,
        scratch=[
            pltpu.VMEM((rows, wide), F32),
            pltpu.VMEM((rows, cols), F32),
            pltpu.VMEM((4 * rows, cols), BF16),
            pltpu.VMEM((rows, cols), F32),
            pltpu.SemaphoreType.DMA((2,)),
        ],
        loaded=(5, 6),
    )(
        own,
        select,
        row_b,
        twist_b,
        mat_b,
        *(pltpu.with_memory_space_constraint(value, pltpu.HBM) for value in (sky, beam)),
    )

    def beside(value, to):
        pairs = [(p, to(p)) for p in range(facets) if 0 <= to(p) < facets]
        return lax.ppermute(value, "facet", pairs)

    gots = [
        lax.ppermute(value, "freq", [(f, (f + d + 1) % count) for f in range(count)])
        for d, value in enumerate(sends)
    ]
    main, near, far = call(
        sum_kernel,
        [shape((rows, wide), F32), shape((2, wide), F32), shape((2, wide), F32)],
        1 << 24,
    )(keep, *gots)
    far = beside(far, lambda p: p + 1 if p & 1 else p - 1)
    near = beside(near, lambda p: p ^ 1)
    tall_rows = pltpu.VMEM((rows + 16, wide), F32)
    partial = call(
        prior_kernel, shape((rows + 16, wide), F32), 1 << 31, scratch=[tall_rows]
    )(main, near, first, second)
    (image,) = call(
        functools.partial(edge_kernel, count, cols // count),
        [shape((rows, cols // count), F32)],
        1 << 30,
        scratch=[
            pltpu.VMEM((64, wide), F32),
            pltpu.VMEM((BAND + 18, wide), F32),
            pltpu.VMEM((BAND + 2, wide), F32),
            pltpu.SemaphoreType.DMA((2,)),
        ],
        saved=(0,),
    )(partial, main, far, first, second)

    tiles_out = call(unpack_kernel, shape((tiles, width), BF16), 1 << 28)(dest, returned)
    return tiles_out, image


def solution(mesh):
    placed = (
        P("facet", None),
        P("freq", "facet", None),
        P(("freq", "facet"), None),
        P(("freq", "facet")),
        P(("freq", "facet")),
        P(),
        P(),
        P(),
    )

    return jax.shard_map(
        on_device,
        mesh=mesh,
        in_specs=placed,
        out_specs=(P(("freq", "facet"), None), P("facet", "freq")),
        check_vma=False,
    )
```

```python
import functools
import math

import jax
import jax.numpy as jnp
import numpy as np
from jax import lax
from jax.experimental import pallas as pl
from jax.experimental.pallas import tpu as pltpu
from jax.sharding import PartitionSpec as P


S = 16
LANES = 128
BAND = 22
STEP = 0.5
F32 = jnp.float32
BF16 = jnp.bfloat16


def iota(shape, dim):
    return lax.broadcasted_iota(jnp.int32, shape, dim)


def mm(a, b, dims=((1,), (0,))):
    return lax.dot_general(a, b, (dims, ((), ())), preferred_element_type=F32)


def one_hot(cond):
    return jnp.where(cond, 1.0, 0.0).astype(BF16)


def split(x):
    high = x.astype(BF16)
    return high, (x - high.astype(F32)).astype(BF16)


def np_split(x):
    x = np.asarray(x, np.float32)
    high = x.astype(BF16)
    return high, (x - high.astype(np.float32)).astype(BF16)


def tables(rows, cols, sign):
    outer = cols // LANES
    scale = 1.0 / math.sqrt(rows * cols)
    k = np.arange(rows)
    angle = sign * 2.0 * np.pi * ((k[:, None] * k[None, :]) % rows) / rows
    cos_r, sin_r = np.cos(angle) * scale, np.sin(angle) * scale
    if sign < 0:
        row_high, row_low = np_split(np.concatenate([cos_r, sin_r], 0))
        row = np.concatenate([row_high, row_high, row_low], 1)
    else:
        row = np.concatenate(np_split(np.concatenate([cos_r, -sin_r], 1)), 1)
    i2 = np.arange(LANES)
    w = np.arange(outer)
    twist = sign * 2.0 * np.pi * ((w[:, None] * i2[None, :]) % cols) / cols
    inner = sign * 2.0 * np.pi * ((i2[:, None] * i2[None, :]) % LANES) / LANES
    c, s = np.cos(inner), np.sin(inner)
    mat_high, mat_low = np_split(np.block([[c, s], [-s, c]]))
    return (
        row,
        np.stack([np.cos(twist), np.sin(twist)]).astype(np.float32),
        np.stack([mat_high, mat_low]),
    )


def times_i(z, sign):
    re, im = z
    return (-im, re) if sign > 0 else (im, -re)


def add(a, b):
    return (a[0] + b[0], a[1] + b[1])


def sub(a, b):
    return (a[0] - b[0], a[1] - b[1])


def dft4(x, sign):
    s0, s1 = add(x[0], x[2]), sub(x[0], x[2])
    s2, s3 = add(x[1], x[3]), times_i(sub(x[1], x[3]), sign)
    return [add(s0, s2), add(s1, s3), sub(s0, s2), sub(s1, s3)]


def dft16(x, sign):
    mid = [dft4([x[4 * a + b] for a in range(4)], sign) for b in range(4)]
    out = [None] * 16
    for c in range(4):
        turned = []
        for b in range(4):
            re, im = mid[b][c]
            phase = (b * c) % 16
            if phase == 0:
                turned.append((re, im))
            elif phase == 4:
                turned.append(times_i((re, im), sign))
            else:
                wr = math.cos(2.0 * math.pi * phase / 16)
                wi = sign * math.sin(2.0 * math.pi * phase / 16)
                turned.append((re * wr - im * wi, re * wi + im * wr))
        for d, value in enumerate(dft4(turned, sign)):
            out[c + 4 * d] = value
    return out


def swap_matrix(size):
    src = iota((1, size), 1)
    swapped = (src & -256) | ((src & 15) << 4) | ((src >> 4) & 15)
    return one_hot(iota((size, size), 0) == swapped)


def pack_kernel(
    facets,
    cap,
    facet_hbm,
    slot_hbm,
    seen_hbm,
    send_hbm,
    dest_ref,
    facet_ref,
    slot_ref,
    seen_ref,
    send_ref,
    sems,
):
    tiles, width = seen_ref.shape
    total = facets * cap
    loads = [
        pltpu.make_async_copy(src, dst, sems.at[i])
        for i, (src, dst) in enumerate(
            ((facet_hbm, facet_ref), (slot_hbm, slot_ref), (seen_hbm, seen_ref))
        )
    ]
    for load in loads:
        load.start()
    before = one_hot(iota((tiles, tiles), 0) < iota((tiles, tiles), 1))
    loads[0].wait()
    facet = facet_ref[...]
    member = iota((facets, tiles), 0) == facet
    member_f = jnp.where(member, 1.0, 0.0)
    ranks = mm(member_f.astype(BF16), before)
    rank = jnp.sum(member_f * ranks, axis=0, keepdims=True).astype(jnp.int32)
    dest = facet * cap + rank
    dest_ref[...] = dest
    loads[1].wait()
    code = slot_ref[...] + 1
    lane = iota((LANES, tiles), 0)
    slots = mm(
        (member_f * (code >> 4).astype(F32)).astype(BF16), one_hot(lane == rank), ((1,), (1,))
    ) + mm(
        (member_f * (code & 15).astype(F32)).astype(BF16),
        one_hot(lane - LANES // 2 == rank),
        ((1,), (1,)),
    )
    parts = width // LANES
    groups = 4
    here = facets // groups
    loads[2].wait()
    saves = []
    for g in range(groups):
        placing = one_hot(iota((total // groups, tiles), 0) + g * (total // groups) == dest)
        packed = mm(placing, seen_ref[...]).astype(BF16)
        for i in range(here):
            d = g * here + i
            for part in range(parts):
                send_ref[d, part * cap : (part + 1) * cap, :] = packed[
                    i * cap : (i + 1) * cap, part * LANES : (part + 1) * LANES
                ]
            send_ref[d, parts * cap : parts * cap + 8, :] = jnp.broadcast_to(
                slots[d : d + 1, :], (8, LANES)
            ).astype(BF16)
        span = pl.ds(g * here, here)
        save = pltpu.make_async_copy(send_ref.at[span], send_hbm.at[span], sems.at[3 + g])
        save.start()
        saves.append(save)
    for save in saves:
        save.wait()


def forward_kernel(
    sky_ref,
    beam_ref,
    row_ref,
    twist_ref,
    mat_ref,
    first_ref,
    bias_ref,
    second_ref,
    high_ref,
    low_ref,
    one_ref,
    two_ref,
    part_ref,
):
    prepare(first_ref, bias_ref, second_ref, one_ref, two_ref)
    rows, cols = sky_ref.shape
    outer = cols // LANES
    weighted = sky_ref[...] * beam_ref[...]
    w_high, w_low = split(weighted)
    mid = mm(row_ref[...], jnp.concatenate([w_high, w_low, w_high], axis=0))
    lines = [
        (
            mid[:rows, i * LANES : (i + 1) * LANES],
            mid[rows:, i * LANES : (i + 1) * LANES],
        )
        for i in range(outer)
    ]
    spread = dft16(lines, -1)
    blocks = []
    for w in range(outer):
        re, im = spread[w]
        tr, ti = twist_ref[0, w : w + 1, :], twist_ref[1, w : w + 1, :]
        blocks.append(jnp.concatenate([re * tr - im * ti, re * ti + im * tr], axis=1))
    high, low = split(jnp.concatenate(blocks, axis=0))
    mat_high, mat_low = mat_ref[0], mat_ref[1]
    model = mm(high, mat_high) + mm(low, mat_high) + mm(high, mat_low)
    for w in range(outer):
        for r in range(rows // S):
            for e in range(2):
                piece = model[
                    w * rows + r * S : w * rows + (r + 1) * S, e * LANES : (e + 1) * LANES
                ]
                piece_high, piece_low = split(piece)
                at = (pl.ds(e * 256 + w * S, S), pl.ds(r * LANES, LANES))
                part_ref[(0,) + at] = piece_high
                part_ref[(1,) + at] = piece_low
    swap = swap_matrix(high_ref.shape[0])
    high_ref[...] = mm(swap, part_ref[0]).astype(BF16)
    low_ref[...] = mm(swap, part_ref[1]).astype(BF16)


def residual_kernel(facets, cap, got_ref, high_ref, low_ref, res_hbm, sel_ref, own_ref, sems):
    total = facets * cap
    slots = high_ref.shape[1]
    parts = high_ref.shape[0] // LANES
    code = got_ref[:, parts * cap : parts * cap + 8, :].astype(F32).reshape(facets * 8, LANES)
    source = iota((total, facets * 8), 0) // cap
    spread = mm(one_hot(iota((total, facets * 8), 1) == source * 8), code.astype(BF16))
    lane = iota((total, LANES), 1)
    rank = iota((total, LANES), 0) % cap
    kept = jnp.where((lane & (LANES // 2 - 1)) == rank, spread, 0.0).astype(BF16)
    digit = jnp.where(iota((LANES, slots), 0) < LANES // 2, 16.0, 1.0).astype(BF16)
    code_all = mm(kept, digit)
    sel = one_hot(code_all.astype(jnp.int32) == iota((total, slots), 1) + 1)
    sel_ref[...] = sel
    contract = ((1,), (1,))
    predicted = mm(sel, high_ref[...], contract) + mm(sel, low_ref[...], contract)
    saves = []
    pieces = sems.shape[0]
    for i in range(pieces):
        here = facets // pieces
        at = slice(i * here * cap, (i + 1) * here * cap)
        for part in range(parts):
            cols = slice(part * LANES, (part + 1) * LANES)
            seen = got_ref[i * here : (i + 1) * here, part * cap : (part + 1) * cap, :]
            seen = seen.astype(F32).reshape(here * cap, LANES)
            own_ref[at, cols] = (predicted[at, cols] - seen).astype(BF16)
        save = pltpu.make_async_copy(own_ref.at[at, :], res_hbm.at[at, :], sems.at[i])
        save.start()
        saves.append(save)
    for save in saves:
        save.wait()


def window(index, count, cols):
    part = cols // count
    width = min(cols, part + (LANES if count == 2 else 2 * LANES))
    return jnp.clip(index * part - LANES, 0, cols - width), width


def inverse_kernel(
    count,
    res_ref,
    sel_ref,
    row_ref,
    twist_ref,
    mat_ref,
    sky_hbm,
    beam_hbm,
    keep_ref,
    *rest,
):
    send_refs = rest[: count - 1]
    sky_ref, beam_ref, lines_ref, shift_ref, grid_ref, sems = rest[count - 1 :]
    rows, cols = beam_ref.shape
    outer = cols // LANES
    me = lax.axis_index("freq")
    start, width = window(me, count, cols)
    sky_part = sky_hbm.at[:, pl.ds(pl.multiple_of(start, LANES), width)]
    loads = [
        pltpu.make_async_copy(beam_hbm, beam_ref, sems.at[0]),
        pltpu.make_async_copy(sky_part, sky_ref, sems.at[1]),
    ]
    for load in loads:
        load.start()
    grid = mm(res_ref[...], sel_ref[...], ((0,), (0,)))
    for r in range(rows // S):
        grid_ref[r] = grid[:, r * LANES : (r + 1) * LANES]
    blocks = []
    for w in range(outer):
        blocks.append(
            jnp.concatenate(
                [
                    jnp.concatenate(
                        [
                            grid_ref[r, pl.ds(e * S * S + w, S, stride=S), :]
                            for e in range(2)
                        ],
                        axis=1,
                    )
                    for r in range(rows // S)
                ],
                axis=0,
            )
        )
    cells = jnp.concatenate(blocks, axis=0).astype(BF16)
    mid = mm(jnp.concatenate([cells, cells], axis=1), mat_ref[...].reshape(4 * LANES, 2 * LANES))
    lines = []
    for w in range(outer):
        re = mid[w * rows : (w + 1) * rows, :LANES]
        im = mid[w * rows : (w + 1) * rows, LANES:]
        tr, ti = twist_ref[0, w : w + 1, :], twist_ref[1, w : w + 1, :]
        lines.append((re * tr - im * ti, re * ti + im * tr))
    spread = dft16(lines, 1)
    for i, pair in enumerate(spread):
        for e in range(2):
            line = pair[e].astype(BF16)
            lines_ref[e * rows : (e + 1) * rows, i * LANES : (i + 1) * LANES] = line
            lines_ref[(2 + e) * rows : (3 + e) * rows, i * LANES : (i + 1) * LANES] = line
    back = mm(row_ref[...], lines_ref[...])
    for load in loads:
        load.wait()
    shift_ref[...] = back * beam_ref[...] * (-STEP)
    for d in range(count):
        start, width = window(lax.rem(me + d, count), count, cols)
        at = pl.ds(pl.multiple_of(start, LANES), width)
        if d == 0:
            keep_ref[...] = shift_ref[:, at] + sky_ref[...]
        else:
            send_refs[d - 1][...] = shift_ref[:, at].astype(BF16)


def sum_kernel(keep_ref, *refs):
    main_ref, near_ref, far_ref = refs[-3:]
    rows = keep_ref.shape[0]
    main = keep_ref[...]
    for ref in refs[:-3]:
        main = main + ref[...].astype(F32)
    main_ref[...] = main
    even = (lax.axis_index("facet") & 1) == 0
    top, bottom = main[0:2], main[rows - 2 : rows]
    near_ref[...] = jnp.where(even, bottom, top)
    far_ref[...] = jnp.where(even, top, bottom)


def prepare(first_ref, bias_ref, second_ref, one_ref, two_ref):
    hidden = first_ref.shape[2]
    depth = one_ref.shape[1]
    full = (BAND + 2) * 9
    bias_high, bias_low = split(bias_ref[...])
    line = iota((8, depth), 0)
    lane = iota((8, depth), 1)
    group = lane * 2731 >> 16
    term = group * 86 >> 8
    col = group - term * 3
    taps = one_hot(((line == col) & (term < 2)) | ((line - 3 == col) & (term == 2)))
    ends = one_hot(((line == 6) & (lane == full)) | ((line == 7) & (lane == full + 1)))
    values = []
    for a in range(3):
        high, low = split(first_ref[a])
        pieces = [high, low, bias_high, bias_low]
        weights = jnp.concatenate([p.astype(F32) for p in pieces], axis=0).astype(BF16)
        values.append(mm(weights, taps, ((0,), (0,))))
        if a == 0:
            offset = mm(weights, ends, ((0,), (0,)))
    lane = iota((hidden, depth), 1)
    yin = lane - (lane * 2731 >> 16) * (BAND + 2)
    for y in range(BAND):
        block = offset
        for a in range(3):
            block = block + jnp.where(yin == y + a, values[a], 0.0)
        one_ref[y * hidden : (y + 1) * hidden, :] = block.astype(BF16)

    wide = two_ref.shape[1]
    tall = BAND + 2
    expand = one_hot(iota((hidden, wide), 0) == (iota((hidden, wide), 1) & (hidden - 1)))
    pieces = [split(second_ref[a]) for a in range(3)]
    gap = iota((tall, wide), 1) // hidden + 2 - iota((tall, wide), 0)
    blocks = []
    for half in range(2):
        lines = [mm(pieces[a][half], expand) for a in range(3)]
        for b in range(3):
            total = jnp.zeros((tall, wide), F32)
            for a in range(3):
                total = jnp.where(gap == a, lines[a][b : b + 1, :], total)
            blocks.append(total)
    two_ref[...] = jnp.concatenate(blocks, axis=0).astype(BF16)


def band_prior(band, one_ref, two_ref, trim=None):
    tall, width = band.shape
    lane = iota((tall, width), 1)
    ones = jnp.where(iota((8, width), 0) < 2, 1.0, 0.0)
    high = band.astype(BF16).astype(F32)
    low = band - high

    def moved(value):
        return (
            jnp.where(lane == 0, 0.0, pltpu.roll(value, 1, 1)),
            jnp.where(lane == width - 1, 0.0, pltpu.roll(value, width - 1, 1)),
        )

    shifted = []
    for value in (high, low):
        left, right = moved(value)
        shifted.append([left, value, right])
    stack = jnp.concatenate(shifted[0] + shifted[1] + shifted[0] + [ones], axis=0).astype(BF16)
    hidden = jnp.maximum(mm(one_ref[...], stack), 0.0)
    if trim is not None:
        inner = one_ref.shape[0] // BAND
        first, last = trim
        hidden = jnp.concatenate(
            [
                jnp.where(first, 0.0, hidden[:inner]),
                hidden[inner:-inner],
                jnp.where(last, 0.0, hidden[-inner:]),
            ],
            axis=0,
        )
    taps = mm(two_ref[...], hidden.astype(BF16))
    parts = [
        taps[b * tall : (b + 1) * tall] + taps[(3 + b) * tall : (4 + b) * tall] for b in range(3)
    ]
    return parts[1] + moved(parts[0])[0] + moved(parts[2])[1]


def prior_kernel(main_ref, near_ref, one_ref, two_ref, sum_ref, base_ref):
    rows, width = main_ref.shape
    tall = BAND + 2
    main, near = main_ref[...], near_ref[...]
    even = (lax.axis_index("facet") & 1) == 0
    base_ref[8 : rows + 8, :] = main
    base_ref[6:8, :] = near
    base_ref[rows + 8 : rows + 10, :] = near
    sum_ref[0:8, :] = jnp.zeros((8, width), F32)
    sum_ref[8 : rows + 8, :] = main
    sum_ref[rows + 8 :, :] = jnp.zeros((8, width), F32)
    spots = [slice(k * BAND + 6, k * BAND + 6 + tall) for k in range((rows + 2) // BAND)]
    for spot in spots[1:-1]:
        share = band_prior(base_ref[spot, :], one_ref, two_ref)
        sum_ref[spot, :] = sum_ref[spot, :] + share
    band = jnp.where(even, base_ref[spots[-1], :], base_ref[spots[0], :])
    share = band_prior(band, one_ref, two_ref)
    sum_ref[spots[0], :] = sum_ref[spots[0], :] + jnp.where(even, 0.0, share)
    sum_ref[spots[-1], :] = sum_ref[spots[-1], :] + jnp.where(even, share, 0.0)


def edge_kernel(
    count,
    part,
    sum_ref,
    main_ref,
    far_ref,
    one_ref,
    two_ref,
    out_hbm,
    base_ref,
    share_ref,
    last_ref,
    sems,
):
    rows, width = main_ref.shape
    tall = BAND + 2
    place = lax.axis_index("facet")
    final = lax.axis_size("facet") - 1
    even = (place & 1) == 0
    me = lax.axis_index("freq")
    start, _ = window(me, count, part * count)
    at = pl.ds(pl.multiple_of(me * part - start, LANES), part)
    done = rows - tall
    first = pl.multiple_of(jnp.where(even, tall, 0), 8)
    early = pltpu.make_async_copy(
        sum_ref.at[pl.ds(pl.multiple_of(first + 8, 8), done), at],
        out_hbm.at[pl.ds(first, done), :],
        sems.at[0],
    )
    early.start()
    far = far_ref[...]
    base_ref[0:2, :] = far
    base_ref[2:tall, :] = main_ref[0:BAND, :]
    base_ref[32 : 32 + BAND, :] = main_ref[rows - BAND : rows, :]
    base_ref[32 + BAND : 32 + tall, :] = far
    band = jnp.where(even, base_ref[0:tall, :], base_ref[32 : 32 + tall, :])
    share_ref[0:8, :] = jnp.zeros((8, width), F32)
    share_ref[8 : tall + 8, :] = band_prior(band, one_ref, two_ref, (place == 0, place == final))
    share_ref[tall + 8 : tall + 16, :] = jnp.zeros((8, width), F32)
    near_sum = jnp.where(even, sum_ref[8 : tall + 8, :], sum_ref[rows + 8 - tall : rows + 8, :])
    share = jnp.where(even, share_ref[10 : tall + 10, :], share_ref[6 : tall + 6, :])
    last_ref[...] = near_sum + share
    late = pltpu.make_async_copy(
        last_ref.at[:, at],
        out_hbm.at[pl.ds(pl.multiple_of(jnp.where(even, 0, done), 8), tall), :],
        sems.at[1],
    )
    late.start()
    early.wait()
    late.wait()


def unpack_kernel(dest_ref, back_ref, out_ref):
    tiles = dest_ref.shape[1]
    total, _ = back_ref.shape
    placing = one_hot(iota((total, tiles), 0) == dest_ref[...])
    out_ref[...] = mm(placing, back_ref[...], ((0,), (0,))).astype(BF16)


def shape(dims, dtype):
    return jax.ShapeDtypeStruct(dims, dtype)


def call(kernel, out_shape, flops, scratch=(), loaded=(), saved=(), limit=16):
    near = pl.BlockSpec(memory_space=pltpu.VMEM)
    far = pl.BlockSpec(memory_space=pltpu.HBM)

    def run(*args):
        return pl.pallas_call(
            kernel,
            out_shape=out_shape,
            in_specs=[far if i in loaded else near for i in range(len(args))],
            out_specs=[far if i in saved else near for i in range(len(out_shape))]
            if isinstance(out_shape, list)
            else near,
            scratch_shapes=scratch,
            compiler_params=pltpu.CompilerParams(vmem_limit_bytes=limit << 20),
            cost_estimate=pl.CostEstimate(flops=flops, bytes_accessed=4 << 20, transcendentals=0),
        )(*args)

    return run


def on_device(sky, beam, observed, facet_of, tile_slot, conv_first, bias_first, conv_second):
    rows, cols = sky.shape
    beam = beam.reshape(rows, cols)
    facets = lax.axis_size("facet")
    count = lax.axis_size("freq")
    tiles, width = observed.shape
    cap = 2 * tiles // facets
    total = facets * cap
    slots = (rows // S) * (cols // S)
    hidden = conv_first.shape[0]
    row_f, twist_f, mat_f = tables(rows, cols, -1)
    row_b, twist_b, mat_b = tables(rows, cols, 1)

    deep = (width // LANES) * cap + 8
    send, dest = call(
        functools.partial(pack_kernel, facets, cap),
        [shape((facets, deep, LANES), BF16), shape((1, tiles), jnp.int32)],
        1 << 28,
        scratch=[
            pltpu.VMEM((1, tiles), jnp.int32),
            pltpu.VMEM((1, tiles), jnp.int32),
            pltpu.VMEM((tiles, width), BF16),
            pltpu.VMEM((facets, deep, LANES), BF16),
            pltpu.SemaphoreType.DMA((7,)),
        ],
        loaded=(0, 1, 2),
        saved=(0,),
    )(
        *(
            pltpu.with_memory_space_constraint(value, pltpu.HBM)
            for value in (facet_of.reshape(1, tiles), tile_slot.reshape(1, tiles), observed)
        )
    )
    got = lax.all_to_all(send, "facet", split_axis=0, concat_axis=0, tiled=True)

    high, low, first, second = call(
        forward_kernel,
        [
            shape((width, slots), BF16),
            shape((width, slots), BF16),
            shape((hidden * BAND, 9 * (BAND + 2) + 8), BF16),
            shape((6 * (BAND + 2), hidden * BAND), BF16),
        ],
        1 << 30,
        scratch=[pltpu.VMEM((2, width, slots), BF16)],
    )(
        sky,
        beam,
        row_f,
        twist_f,
        mat_f,
        conv_first.transpose(1, 2, 0),
        bias_first.reshape(1, hidden),
        conv_second.transpose(1, 2, 0),
    )

    residual, select, own = call(
        functools.partial(residual_kernel, facets, cap),
        [shape((total, width), BF16), shape((total, slots), BF16), shape((total, width), BF16)],
        1 << 30,
        scratch=[pltpu.SemaphoreType.DMA((4,))],
        saved=(0,),
    )(got, *(pltpu.with_memory_space_constraint(value, pltpu.VMEM) for value in (high, low)))
    returned = lax.all_to_all(
        residual.reshape(facets, cap, width), "facet", split_axis=0, concat_axis=0, tiled=True
    ).reshape(total, width)

    _, wide = window(0, count, cols)
    keep, *sends = call(
        functools.partial(inverse_kernel, count),
        [shape((rows, wide), F32)] + [shape((rows, wide), BF16)] * (count - 1),
        1 << 30,
        scratch=[
            pltpu.VMEM((rows, wide), F32),
            pltpu.VMEM((rows, cols), F32),
            pltpu.VMEM((4 * rows, cols), BF16),
            pltpu.VMEM((rows, cols), F32),
            pltpu.VMEM((rows // S, width, LANES), F32),
            pltpu.SemaphoreType.DMA((2,)),
        ],
        loaded=(5, 6),
    )(
        own,
        select,
        row_b,
        twist_b,
        mat_b,
        *(pltpu.with_memory_space_constraint(value, pltpu.HBM) for value in (sky, beam)),
    )

    def beside(value, to):
        pairs = [(p, to(p)) for p in range(facets) if 0 <= to(p) < facets]
        return lax.ppermute(value, "facet", pairs)

    gots = [
        lax.ppermute(value, "freq", [(f, (f + d + 1) % count) for f in range(count)])
        for d, value in enumerate(sends)
    ]
    main, near, far = call(
        sum_kernel,
        [shape((rows, wide), F32), shape((2, wide), F32), shape((2, wide), F32)],
        1 << 24,
    )(keep, *gots)
    far = beside(far, lambda p: p + 1 if p & 1 else p - 1)
    near = beside(near, lambda p: p ^ 1)
    tall_rows = pltpu.VMEM((rows + 16, wide), F32)
    partial = call(
        prior_kernel, shape((rows + 16, wide), F32), 1 << 31, scratch=[tall_rows]
    )(main, near, first, second)
    (image,) = call(
        functools.partial(edge_kernel, count, cols // count),
        [shape((rows, cols // count), F32)],
        1 << 30,
        scratch=[
            pltpu.VMEM((64, wide), F32),
            pltpu.VMEM((BAND + 18, wide), F32),
            pltpu.VMEM((BAND + 2, wide), F32),
            pltpu.SemaphoreType.DMA((2,)),
        ],
        saved=(0,),
    )(partial, main, far, first, second)

    tiles_out = call(unpack_kernel, shape((tiles, width), BF16), 1 << 28)(dest, returned)
    return tiles_out, image


def solution(mesh):
    placed = (
        P("facet", None),
        P("freq", "facet", None),
        P(("freq", "facet"), None),
        P(("freq", "facet")),
        P(("freq", "facet")),
        P(),
        P(),
        P(),
    )

    return jax.shard_map(
        on_device,
        mesh=mesh,
        in_specs=placed,
        out_specs=(P(("freq", "facet"), None), P("facet", "freq")),
        check_vma=False,
    )
```

```python
import functools
import math

import jax
import jax.numpy as jnp
import numpy as np
from jax import lax
from jax.experimental import pallas as pl
from jax.experimental.pallas import tpu as pltpu
from jax.sharding import PartitionSpec as P


S = 16
LANES = 128
BAND = 22
STEP = 0.5
F32 = jnp.float32
BF16 = jnp.bfloat16


def iota(shape, dim):
    return lax.broadcasted_iota(jnp.int32, shape, dim)


def mm(a, b, dims=((1,), (0,))):
    return lax.dot_general(a, b, (dims, ((), ())), preferred_element_type=F32)


def one_hot(cond):
    return jnp.where(cond, 1.0, 0.0).astype(BF16)


def split(x):
    high = x.astype(BF16)
    return high, (x - high.astype(F32)).astype(BF16)


def np_split(x):
    x = np.asarray(x, np.float32)
    high = x.astype(BF16)
    return high, (x - high.astype(np.float32)).astype(BF16)


def tables(rows, cols, sign):
    outer = cols // LANES
    scale = 1.0 / math.sqrt(rows * cols)
    k = np.arange(rows)
    angle = sign * 2.0 * np.pi * ((k[:, None] * k[None, :]) % rows) / rows
    cos_r, sin_r = np.cos(angle) * scale, np.sin(angle) * scale
    if sign < 0:
        row_high, row_low = np_split(np.concatenate([cos_r, sin_r], 0))
        row = np.concatenate([row_high, row_high, row_low], 1)
    else:
        row = np.concatenate(np_split(np.concatenate([cos_r, -sin_r], 1)), 1)
    i2 = np.arange(LANES)
    w = np.arange(outer)
    twist = sign * 2.0 * np.pi * ((w[:, None] * i2[None, :]) % cols) / cols
    inner = sign * 2.0 * np.pi * ((i2[:, None] * i2[None, :]) % LANES) / LANES
    c, s = np.cos(inner), np.sin(inner)
    mat_high, mat_low = np_split(np.block([[c, s], [-s, c]]))
    return (
        row,
        np.stack([np.cos(twist), np.sin(twist)]).astype(np.float32),
        np.stack([mat_high, mat_low]),
    )


def times_i(z, sign):
    re, im = z
    return (-im, re) if sign > 0 else (im, -re)


def add(a, b):
    return (a[0] + b[0], a[1] + b[1])


def sub(a, b):
    return (a[0] - b[0], a[1] - b[1])


def dft4(x, sign):
    s0, s1 = add(x[0], x[2]), sub(x[0], x[2])
    s2, s3 = add(x[1], x[3]), times_i(sub(x[1], x[3]), sign)
    return [add(s0, s2), add(s1, s3), sub(s0, s2), sub(s1, s3)]


def dft16(x, sign):
    mid = [dft4([x[4 * a + b] for a in range(4)], sign) for b in range(4)]
    out = [None] * 16
    for c in range(4):
        turned = []
        for b in range(4):
            re, im = mid[b][c]
            phase = (b * c) % 16
            if phase == 0:
                turned.append((re, im))
            elif phase == 4:
                turned.append(times_i((re, im), sign))
            else:
                wr = math.cos(2.0 * math.pi * phase / 16)
                wi = sign * math.sin(2.0 * math.pi * phase / 16)
                turned.append((re * wr - im * wi, re * wi + im * wr))
        for d, value in enumerate(dft4(turned, sign)):
            out[c + 4 * d] = value
    return out


def swap_matrix(size):
    src = iota((1, size), 1)
    swapped = (src & -256) | ((src & 15) << 4) | ((src >> 4) & 15)
    return one_hot(iota((size, size), 0) == swapped)


def pack_kernel(
    facets,
    cap,
    facet_hbm,
    slot_hbm,
    seen_hbm,
    send_hbm,
    dest_ref,
    facet_ref,
    slot_ref,
    seen_ref,
    send_ref,
    sems,
):
    tiles, width = seen_ref.shape
    total = facets * cap
    loads = [
        pltpu.make_async_copy(src, dst, sems.at[i])
        for i, (src, dst) in enumerate(
            ((facet_hbm, facet_ref), (slot_hbm, slot_ref), (seen_hbm, seen_ref))
        )
    ]
    for load in loads:
        load.start()
    before = one_hot(iota((tiles, tiles), 0) < iota((tiles, tiles), 1))
    loads[0].wait()
    facet = facet_ref[...]
    member = iota((facets, tiles), 0) == facet
    member_f = jnp.where(member, 1.0, 0.0)
    ranks = mm(member_f.astype(BF16), before)
    rank = jnp.sum(member_f * ranks, axis=0, keepdims=True).astype(jnp.int32)
    dest = facet * cap + rank
    dest_ref[...] = dest
    loads[1].wait()
    code = slot_ref[...] + 1
    lane = iota((LANES, tiles), 0)
    slots = mm(
        (member_f * (code >> 4).astype(F32)).astype(BF16), one_hot(lane == rank), ((1,), (1,))
    ) + mm(
        (member_f * (code & 15).astype(F32)).astype(BF16),
        one_hot(lane - LANES // 2 == rank),
        ((1,), (1,)),
    )
    parts = width // LANES
    groups = 4
    here = facets // groups
    loads[2].wait()
    saves = []
    for g in range(groups):
        placing = one_hot(iota((total // groups, tiles), 0) + g * (total // groups) == dest)
        packed = mm(placing, seen_ref[...]).astype(BF16)
        for i in range(here):
            d = g * here + i
            for part in range(parts):
                send_ref[d, part * cap : (part + 1) * cap, :] = packed[
                    i * cap : (i + 1) * cap, part * LANES : (part + 1) * LANES
                ]
            send_ref[d, parts * cap : parts * cap + 8, :] = jnp.broadcast_to(
                slots[d : d + 1, :], (8, LANES)
            ).astype(BF16)
        span = pl.ds(g * here, here)
        save = pltpu.make_async_copy(send_ref.at[span], send_hbm.at[span], sems.at[3 + g])
        save.start()
        saves.append(save)
    for save in saves:
        save.wait()


def forward_kernel(
    sky_ref,
    beam_ref,
    row_ref,
    twist_ref,
    mat_ref,
    first_ref,
    bias_ref,
    second_ref,
    high_ref,
    low_ref,
    one_ref,
    two_ref,
    part_ref,
):
    prepare(first_ref, bias_ref, second_ref, one_ref, two_ref)
    rows, cols = sky_ref.shape
    outer = cols // LANES
    weighted = sky_ref[...] * beam_ref[...]
    w_high, w_low = split(weighted)
    mid = mm(row_ref[...], jnp.concatenate([w_high, w_low, w_high], axis=0))
    lines = [
        (
            mid[:rows, i * LANES : (i + 1) * LANES],
            mid[rows:, i * LANES : (i + 1) * LANES],
        )
        for i in range(outer)
    ]
    spread = dft16(lines, -1)
    blocks = []
    for w in range(outer):
        re, im = spread[w]
        tr, ti = twist_ref[0, w : w + 1, :], twist_ref[1, w : w + 1, :]
        blocks.append(jnp.concatenate([re * tr - im * ti, re * ti + im * tr], axis=1))
    high, low = split(jnp.concatenate(blocks, axis=0))
    mat_high, mat_low = mat_ref[0], mat_ref[1]
    model = mm(high, mat_high) + mm(low, mat_high) + mm(high, mat_low)
    for w in range(outer):
        for r in range(rows // S):
            for e in range(2):
                piece = model[
                    w * rows + r * S : w * rows + (r + 1) * S, e * LANES : (e + 1) * LANES
                ]
                piece_high, piece_low = split(piece)
                at = (pl.ds(e * 256 + w * S, S), pl.ds(r * LANES, LANES))
                part_ref[(0,) + at] = piece_high
                part_ref[(1,) + at] = piece_low
    swap = swap_matrix(high_ref.shape[0])
    high_ref[...] = mm(swap, part_ref[0]).astype(BF16)
    low_ref[...] = mm(swap, part_ref[1]).astype(BF16)


def residual_kernel(facets, cap, got_ref, high_ref, low_ref, res_hbm, sel_ref, own_ref, sems):
    total = facets * cap
    slots = high_ref.shape[1]
    parts = high_ref.shape[0] // LANES
    code = got_ref[:, parts * cap : parts * cap + 8, :].astype(F32).reshape(facets * 8, LANES)
    source = iota((total, facets * 8), 0) // cap
    spread = mm(one_hot(iota((total, facets * 8), 1) == source * 8), code.astype(BF16))
    lane = iota((total, LANES), 1)
    rank = iota((total, LANES), 0) % cap
    kept = jnp.where((lane & (LANES // 2 - 1)) == rank, spread, 0.0).astype(BF16)
    digit = jnp.where(iota((LANES, slots), 0) < LANES // 2, 16.0, 1.0).astype(BF16)
    code_all = mm(kept, digit)
    sel = one_hot(code_all.astype(jnp.int32) == iota((total, slots), 1) + 1)
    sel_ref[...] = sel
    contract = ((1,), (1,))
    predicted = mm(sel, high_ref[...], contract) + mm(sel, low_ref[...], contract)
    saves = []
    pieces = sems.shape[0]
    for i in range(pieces):
        here = facets // pieces
        at = slice(i * here * cap, (i + 1) * here * cap)
        for part in range(parts):
            cols = slice(part * LANES, (part + 1) * LANES)
            seen = got_ref[i * here : (i + 1) * here, part * cap : (part + 1) * cap, :]
            seen = seen.astype(F32).reshape(here * cap, LANES)
            own_ref[at, cols] = (predicted[at, cols] - seen).astype(BF16)
        save = pltpu.make_async_copy(own_ref.at[at, :], res_hbm.at[at, :], sems.at[i])
        save.start()
        saves.append(save)
    for save in saves:
        save.wait()


def window(index, count, cols):
    part = cols // count
    width = min(cols, part + (LANES if count == 2 else 2 * LANES))
    return jnp.clip(index * part - LANES, 0, cols - width), width


def inverse_kernel(
    count,
    res_ref,
    sel_ref,
    row_ref,
    twist_ref,
    mat_ref,
    sky_hbm,
    beam_hbm,
    keep_ref,
    *rest,
):
    send_refs = rest[: count - 1]
    sky_ref, beam_ref, lines_ref, shift_ref, grid_ref, sems = rest[count - 1 :]
    rows, cols = beam_ref.shape
    outer = cols // LANES
    me = lax.axis_index("freq")
    start, width = window(me, count, cols)
    sky_part = sky_hbm.at[:, pl.ds(pl.multiple_of(start, LANES), width)]
    loads = [
        pltpu.make_async_copy(beam_hbm, beam_ref, sems.at[0]),
        pltpu.make_async_copy(sky_part, sky_ref, sems.at[1]),
    ]
    for load in loads:
        load.start()
    grid = mm(res_ref[...], sel_ref[...], ((0,), (0,)))
    for r in range(rows // S):
        grid_ref[r] = grid[:, r * LANES : (r + 1) * LANES]
    blocks = []
    for w in range(outer):
        blocks.append(
            jnp.concatenate(
                [
                    jnp.concatenate(
                        [
                            grid_ref[r, pl.ds(e * S * S + w, S, stride=S), :]
                            for e in range(2)
                        ],
                        axis=1,
                    )
                    for r in range(rows // S)
                ],
                axis=0,
            )
        )
    cells = jnp.concatenate(blocks, axis=0).astype(BF16)
    mid = mm(jnp.concatenate([cells, cells], axis=1), mat_ref[...].reshape(4 * LANES, 2 * LANES))
    lines = []
    for w in range(outer):
        re = mid[w * rows : (w + 1) * rows, :LANES]
        im = mid[w * rows : (w + 1) * rows, LANES:]
        tr, ti = twist_ref[0, w : w + 1, :], twist_ref[1, w : w + 1, :]
        lines.append((re * tr - im * ti, re * ti + im * tr))
    spread = dft16(lines, 1)
    for i, pair in enumerate(spread):
        for e in range(2):
            line = pair[e].astype(BF16)
            lines_ref[e * rows : (e + 1) * rows, i * LANES : (i + 1) * LANES] = line
            lines_ref[(2 + e) * rows : (3 + e) * rows, i * LANES : (i + 1) * LANES] = line
    back = mm(row_ref[...], lines_ref[...])
    for load in loads:
        load.wait()
    shift_ref[...] = back * beam_ref[...] * (-STEP)
    for d in range(count):
        start, width = window(lax.rem(me + d, count), count, cols)
        at = pl.ds(pl.multiple_of(start, LANES), width)
        if d == 0:
            keep_ref[...] = shift_ref[:, at] + sky_ref[...]
        else:
            send_refs[d - 1][...] = shift_ref[:, at].astype(BF16)


def sum_kernel(keep_ref, *refs):
    main_ref, near_ref, far_ref = refs[-3:]
    rows = keep_ref.shape[0]
    main = keep_ref[...]
    for ref in refs[:-3]:
        main = main + ref[...].astype(F32)
    main_ref[...] = main
    even = (lax.axis_index("facet") & 1) == 0
    top, bottom = main[0:2], main[rows - 2 : rows]
    near_ref[...] = jnp.where(even, bottom, top)
    far_ref[...] = jnp.where(even, top, bottom)


def prepare(first_ref, bias_ref, second_ref, one_ref, two_ref):
    hidden = first_ref.shape[2]
    depth = one_ref.shape[1]
    full = (BAND + 2) * 9
    bias_high, bias_low = split(bias_ref[...])
    line = iota((8, depth), 0)
    lane = iota((8, depth), 1)
    group = lane * 2731 >> 16
    term = group * 86 >> 8
    col = group - term * 3
    taps = one_hot(((line == col) & (term < 2)) | ((line - 3 == col) & (term == 2)))
    ends = one_hot(((line == 6) & (lane == full)) | ((line == 7) & (lane == full + 1)))
    values = []
    for a in range(3):
        high, low = split(first_ref[a])
        pieces = [high, low, bias_high, bias_low]
        weights = jnp.concatenate([p.astype(F32) for p in pieces], axis=0).astype(BF16)
        values.append(mm(weights, taps, ((0,), (0,))))
        if a == 0:
            offset = mm(weights, ends, ((0,), (0,)))
    lane = iota((hidden, depth), 1)
    yin = lane - (lane * 2731 >> 16) * (BAND + 2)
    for y in range(BAND):
        block = offset
        for a in range(3):
            block = block + jnp.where(yin == y + a, values[a], 0.0)
        one_ref[y * hidden : (y + 1) * hidden, :] = block.astype(BF16)

    wide = two_ref.shape[1]
    tall = BAND + 2
    expand = one_hot(iota((hidden, wide), 0) == (iota((hidden, wide), 1) & (hidden - 1)))
    pieces = [split(second_ref[a]) for a in range(3)]
    gap = iota((tall, wide), 1) // hidden + 2 - iota((tall, wide), 0)
    blocks = []
    for half in range(2):
        lines = [mm(pieces[a][half], expand) for a in range(3)]
        for b in range(3):
            total = jnp.zeros((tall, wide), F32)
            for a in range(3):
                total = jnp.where(gap == a, lines[a][b : b + 1, :], total)
            blocks.append(total)
    two_ref[...] = jnp.concatenate(blocks, axis=0).astype(BF16)


def band_prior(bands, one_ref, two_ref, trim=None):
    tall, width = bands[0].shape
    lane = iota((tall, width), 1)
    ones = jnp.where(iota((8, width), 0) < 2, 1.0, 0.0)

    def moved(value):
        return (
            jnp.where(lane == 0, 0.0, pltpu.roll(value, 1, 1)),
            jnp.where(lane == width - 1, 0.0, pltpu.roll(value, width - 1, 1)),
        )

    stacks = []
    for band in bands:
        high = band.astype(BF16).astype(F32)
        shifted = []
        for value in (high, band - high):
            left, right = moved(value)
            shifted.append([left, value, right])
        stacks.append(
            jnp.concatenate(shifted[0] + shifted[1] + shifted[0] + [ones], axis=0).astype(BF16)
        )
    hidden = jnp.maximum(mm(one_ref[...], jnp.concatenate(stacks, axis=1)), 0.0)
    if trim is not None:
        inner = one_ref.shape[0] // BAND
        first, last = trim
        hidden = jnp.concatenate(
            [
                jnp.where(first, 0.0, hidden[:inner]),
                hidden[inner:-inner],
                jnp.where(last, 0.0, hidden[-inner:]),
            ],
            axis=0,
        )
    taps = mm(two_ref[...], hidden.astype(BF16))
    shares = []
    for i in range(len(bands)):
        own = taps[:, i * width : (i + 1) * width]
        parts = [
            own[b * tall : (b + 1) * tall] + own[(3 + b) * tall : (4 + b) * tall] for b in range(3)
        ]
        shares.append(parts[1] + moved(parts[0])[0] + moved(parts[2])[1])
    return shares


def prior_kernel(main_ref, near_ref, one_ref, two_ref, sum_ref, base_ref):
    rows, width = main_ref.shape
    tall = BAND + 2
    main, near = main_ref[...], near_ref[...]
    even = (lax.axis_index("facet") & 1) == 0
    base_ref[8 : rows + 8, :] = main
    base_ref[6:8, :] = near
    base_ref[rows + 8 : rows + 10, :] = near
    sum_ref[0:8, :] = jnp.zeros((8, width), F32)
    sum_ref[8 : rows + 8, :] = main
    sum_ref[rows + 8 :, :] = jnp.zeros((8, width), F32)
    spots = [slice(k * BAND + 6, k * BAND + 6 + tall) for k in range((rows + 2) // BAND)]
    bands = [base_ref[spot, :] for spot in spots[1:-1]]
    bands.append(jnp.where(even, base_ref[spots[-1], :], base_ref[spots[0], :]))
    *inner, share = band_prior(bands, one_ref, two_ref)
    for spot, value in zip(spots[1:-1], inner):
        sum_ref[spot, :] = sum_ref[spot, :] + value
    sum_ref[spots[0], :] = sum_ref[spots[0], :] + jnp.where(even, 0.0, share)
    sum_ref[spots[-1], :] = sum_ref[spots[-1], :] + jnp.where(even, share, 0.0)


def edge_kernel(
    count,
    part,
    sum_ref,
    main_ref,
    far_ref,
    one_ref,
    two_ref,
    dest_ref,
    back_ref,
    out_hbm,
    tiles_hbm,
    base_ref,
    share_ref,
    last_ref,
    tiles_ref,
    sems,
):
    rows, width = main_ref.shape
    tall = BAND + 2
    place = lax.axis_index("facet")
    final = lax.axis_size("facet") - 1
    even = (place & 1) == 0
    me = lax.axis_index("freq")
    start, _ = window(me, count, part * count)
    at = pl.ds(pl.multiple_of(me * part - start, LANES), part)
    done = rows - tall
    first = pl.multiple_of(jnp.where(even, tall, 0), 8)
    early = pltpu.make_async_copy(
        sum_ref.at[pl.ds(pl.multiple_of(first + 8, 8), done), at],
        out_hbm.at[pl.ds(first, done), :],
        sems.at[0],
    )
    early.start()
    placing = one_hot(
        iota((back_ref.shape[0], dest_ref.shape[1]), 0) == dest_ref[...]
    )
    tiles_ref[...] = mm(placing, back_ref[...], ((0,), (0,))).astype(BF16)
    tiles = pltpu.make_async_copy(tiles_ref, tiles_hbm, sems.at[2])
    tiles.start()
    far = far_ref[...]
    base_ref[0:2, :] = far
    base_ref[2:tall, :] = main_ref[0:BAND, :]
    base_ref[32 : 32 + BAND, :] = main_ref[rows - BAND : rows, :]
    base_ref[32 + BAND : 32 + tall, :] = far
    band = jnp.where(even, base_ref[0:tall, :], base_ref[32 : 32 + tall, :])
    share_ref[0:8, :] = jnp.zeros((8, width), F32)
    share_ref[8 : tall + 8, :] = band_prior(
        [band], one_ref, two_ref, (place == 0, place == final)
    )[0]
    share_ref[tall + 8 : tall + 16, :] = jnp.zeros((8, width), F32)
    near_sum = jnp.where(even, sum_ref[8 : tall + 8, :], sum_ref[rows + 8 - tall : rows + 8, :])
    share = jnp.where(even, share_ref[10 : tall + 10, :], share_ref[6 : tall + 6, :])
    last_ref[...] = near_sum + share
    late = pltpu.make_async_copy(
        last_ref.at[:, at],
        out_hbm.at[pl.ds(pl.multiple_of(jnp.where(even, 0, done), 8), tall), :],
        sems.at[1],
    )
    late.start()
    early.wait()
    tiles.wait()
    late.wait()


def shape(dims, dtype):
    return jax.ShapeDtypeStruct(dims, dtype)


def call(kernel, out_shape, flops, scratch=(), loaded=(), saved=(), limit=16):
    near = pl.BlockSpec(memory_space=pltpu.VMEM)
    far = pl.BlockSpec(memory_space=pltpu.HBM)

    def run(*args):
        return pl.pallas_call(
            kernel,
            out_shape=out_shape,
            in_specs=[far if i in loaded else near for i in range(len(args))],
            out_specs=[far if i in saved else near for i in range(len(out_shape))]
            if isinstance(out_shape, list)
            else near,
            scratch_shapes=scratch,
            compiler_params=pltpu.CompilerParams(vmem_limit_bytes=limit << 20),
            cost_estimate=pl.CostEstimate(flops=flops, bytes_accessed=4 << 20, transcendentals=0),
        )(*args)

    return run


def on_device(sky, beam, observed, facet_of, tile_slot, conv_first, bias_first, conv_second):
    rows, cols = sky.shape
    beam = beam.reshape(rows, cols)
    facets = lax.axis_size("facet")
    count = lax.axis_size("freq")
    tiles, width = observed.shape
    cap = 2 * tiles // facets
    total = facets * cap
    slots = (rows // S) * (cols // S)
    hidden = conv_first.shape[0]
    row_f, twist_f, mat_f = tables(rows, cols, -1)
    row_b, twist_b, mat_b = tables(rows, cols, 1)

    deep = (width // LANES) * cap + 8
    send, dest = call(
        functools.partial(pack_kernel, facets, cap),
        [shape((facets, deep, LANES), BF16), shape((1, tiles), jnp.int32)],
        1 << 28,
        scratch=[
            pltpu.VMEM((1, tiles), jnp.int32),
            pltpu.VMEM((1, tiles), jnp.int32),
            pltpu.VMEM((tiles, width), BF16),
            pltpu.VMEM((facets, deep, LANES), BF16),
            pltpu.SemaphoreType.DMA((7,)),
        ],
        loaded=(0, 1, 2),
        saved=(0,),
    )(
        *(
            pltpu.with_memory_space_constraint(value, pltpu.HBM)
            for value in (facet_of.reshape(1, tiles), tile_slot.reshape(1, tiles), observed)
        )
    )
    got = lax.all_to_all(send, "facet", split_axis=0, concat_axis=0, tiled=True)

    high, low, first, second = call(
        forward_kernel,
        [
            shape((width, slots), BF16),
            shape((width, slots), BF16),
            shape((hidden * BAND, 9 * (BAND + 2) + 8), BF16),
            shape((6 * (BAND + 2), hidden * BAND), BF16),
        ],
        1 << 30,
        scratch=[pltpu.VMEM((2, width, slots), BF16)],
    )(
        sky,
        beam,
        row_f,
        twist_f,
        mat_f,
        conv_first.transpose(1, 2, 0),
        bias_first.reshape(1, hidden),
        conv_second.transpose(1, 2, 0),
    )

    residual, select, own = call(
        functools.partial(residual_kernel, facets, cap),
        [shape((total, width), BF16), shape((total, slots), BF16), shape((total, width), BF16)],
        1 << 30,
        scratch=[pltpu.SemaphoreType.DMA((4,))],
        saved=(0,),
    )(got, *(pltpu.with_memory_space_constraint(value, pltpu.VMEM) for value in (high, low)))
    returned = lax.all_to_all(
        residual.reshape(facets, cap, width), "facet", split_axis=0, concat_axis=0, tiled=True
    ).reshape(total, width)

    _, wide = window(0, count, cols)
    keep, *sends = call(
        functools.partial(inverse_kernel, count),
        [shape((rows, wide), F32)] + [shape((rows, wide), BF16)] * (count - 1),
        1 << 30,
        scratch=[
            pltpu.VMEM((rows, wide), F32),
            pltpu.VMEM((rows, cols), F32),
            pltpu.VMEM((4 * rows, cols), BF16),
            pltpu.VMEM((rows, cols), F32),
            pltpu.VMEM((rows // S, width, LANES), F32),
            pltpu.SemaphoreType.DMA((2,)),
        ],
        loaded=(5, 6),
    )(
        own,
        select,
        row_b,
        twist_b,
        mat_b,
        *(pltpu.with_memory_space_constraint(value, pltpu.HBM) for value in (sky, beam)),
    )

    def beside(value, to):
        pairs = [(p, to(p)) for p in range(facets) if 0 <= to(p) < facets]
        return lax.ppermute(value, "facet", pairs)

    gots = [
        lax.ppermute(value, "freq", [(f, (f + d + 1) % count) for f in range(count)])
        for d, value in enumerate(sends)
    ]
    main, near, far = call(
        sum_kernel,
        [shape((rows, wide), F32), shape((2, wide), F32), shape((2, wide), F32)],
        1 << 24,
    )(keep, *gots)
    far = beside(far, lambda p: p + 1 if p & 1 else p - 1)
    near = beside(near, lambda p: p ^ 1)
    tall_rows = pltpu.VMEM((rows + 16, wide), F32)
    partial = call(
        prior_kernel, shape((rows + 16, wide), F32), 1 << 31, scratch=[tall_rows]
    )(main, near, first, second)
    image, tiles_out = call(
        functools.partial(edge_kernel, count, cols // count),
        [shape((rows, cols // count), F32), shape((tiles, width), BF16)],
        1 << 30,
        scratch=[
            pltpu.VMEM((64, wide), F32),
            pltpu.VMEM((BAND + 18, wide), F32),
            pltpu.VMEM((BAND + 2, wide), F32),
            pltpu.VMEM((tiles, width), BF16),
            pltpu.SemaphoreType.DMA((3,)),
        ],
        saved=(0, 1),
    )(partial, main, far, first, second, dest, returned)
    return tiles_out, image


def solution(mesh):
    placed = (
        P("facet", None),
        P("freq", "facet", None),
        P(("freq", "facet"), None),
        P(("freq", "facet")),
        P(("freq", "facet")),
        P(),
        P(),
        P(),
    )

    return jax.shard_map(
        on_device,
        mesh=mesh,
        in_specs=placed,
        out_specs=(P(("freq", "facet"), None), P("facet", "freq")),
        check_vma=False,
    )
```

```python
import functools
import math

import jax
import jax.numpy as jnp
import numpy as np
from jax import lax
from jax.experimental import pallas as pl
from jax.experimental.pallas import tpu as pltpu
from jax.sharding import PartitionSpec as P


S = 16
LANES = 128
BAND = 22
STEP = 0.5
F32 = jnp.float32
BF16 = jnp.bfloat16


def iota(shape, dim):
    return lax.broadcasted_iota(jnp.int32, shape, dim)


def mm(a, b, dims=((1,), (0,))):
    return lax.dot_general(a, b, (dims, ((), ())), preferred_element_type=F32)


def one_hot(cond):
    return jnp.where(cond, 1.0, 0.0).astype(BF16)


def split(x):
    high = x.astype(BF16)
    return high, (x - high.astype(F32)).astype(BF16)


def np_split(x):
    x = np.asarray(x, np.float32)
    high = x.astype(BF16)
    return high, (x - high.astype(np.float32)).astype(BF16)


def tables(rows, cols, sign):
    outer = cols // LANES
    scale = 1.0 / math.sqrt(rows * cols)
    k = np.arange(rows)
    angle = sign * 2.0 * np.pi * ((k[:, None] * k[None, :]) % rows) / rows
    cos_r, sin_r = np.cos(angle) * scale, np.sin(angle) * scale
    if sign < 0:
        row_high, row_low = np_split(np.concatenate([cos_r, sin_r], 0))
        row = np.concatenate([row_high, row_high, row_low], 1)
    else:
        row = np.concatenate(np_split(np.concatenate([cos_r, -sin_r], 1)), 1)
    i2 = np.arange(LANES)
    w = np.arange(outer)
    twist = sign * 2.0 * np.pi * ((w[:, None] * i2[None, :]) % cols) / cols
    inner = sign * 2.0 * np.pi * ((i2[:, None] * i2[None, :]) % LANES) / LANES
    c, s = np.cos(inner), np.sin(inner)
    mat_high, mat_low = np_split(np.block([[c, s], [-s, c]]))
    return (
        row,
        np.stack([np.cos(twist), np.sin(twist)]).astype(np.float32),
        np.stack([mat_high, mat_low]),
    )


def times_i(z, sign):
    re, im = z
    return (-im, re) if sign > 0 else (im, -re)


def add(a, b):
    return (a[0] + b[0], a[1] + b[1])


def sub(a, b):
    return (a[0] - b[0], a[1] - b[1])


def dft4(x, sign):
    s0, s1 = add(x[0], x[2]), sub(x[0], x[2])
    s2, s3 = add(x[1], x[3]), times_i(sub(x[1], x[3]), sign)
    return [add(s0, s2), add(s1, s3), sub(s0, s2), sub(s1, s3)]


def dft16(x, sign):
    mid = [dft4([x[4 * a + b] for a in range(4)], sign) for b in range(4)]
    out = [None] * 16
    for c in range(4):
        turned = []
        for b in range(4):
            re, im = mid[b][c]
            phase = (b * c) % 16
            if phase == 0:
                turned.append((re, im))
            elif phase == 4:
                turned.append(times_i((re, im), sign))
            else:
                wr = math.cos(2.0 * math.pi * phase / 16)
                wi = sign * math.sin(2.0 * math.pi * phase / 16)
                turned.append((re * wr - im * wi, re * wi + im * wr))
        for d, value in enumerate(dft4(turned, sign)):
            out[c + 4 * d] = value
    return out


def swap_matrix(size):
    src = iota((1, size), 1)
    swapped = (src & -256) | ((src & 15) << 4) | ((src >> 4) & 15)
    return one_hot(iota((size, size), 0) == swapped)


def pack_kernel(
    facets,
    cap,
    facet_hbm,
    slot_hbm,
    seen_hbm,
    send_hbm,
    dest_ref,
    facet_ref,
    slot_ref,
    seen_ref,
    send_ref,
    sems,
):
    tiles, width = seen_ref.shape
    total = facets * cap
    loads = [
        pltpu.make_async_copy(src, dst, sems.at[i])
        for i, (src, dst) in enumerate(
            ((facet_hbm, facet_ref), (slot_hbm, slot_ref), (seen_hbm, seen_ref))
        )
    ]
    for load in loads:
        load.start()
    before = one_hot(iota((tiles, tiles), 0) < iota((tiles, tiles), 1))
    loads[0].wait()
    facet = facet_ref[...]
    member = iota((facets, tiles), 0) == facet
    member_f = jnp.where(member, 1.0, 0.0)
    ranks = mm(member_f.astype(BF16), before)
    rank = jnp.sum(member_f * ranks, axis=0, keepdims=True).astype(jnp.int32)
    dest = facet * cap + rank
    dest_ref[...] = dest
    loads[1].wait()
    code = slot_ref[...] + 1
    lane = iota((LANES, tiles), 0)
    slots = mm(
        (member_f * (code >> 4).astype(F32)).astype(BF16), one_hot(lane == rank), ((1,), (1,))
    ) + mm(
        (member_f * (code & 15).astype(F32)).astype(BF16),
        one_hot(lane - LANES // 2 == rank),
        ((1,), (1,)),
    )
    parts = width // LANES
    groups = 4
    here = facets // groups
    loads[2].wait()
    saves = []
    for g in range(groups):
        placing = one_hot(iota((total // groups, tiles), 0) + g * (total // groups) == dest)
        packed = mm(placing, seen_ref[...]).astype(BF16)
        for i in range(here):
            d = g * here + i
            for part in range(parts):
                send_ref[d, part * cap : (part + 1) * cap, :] = packed[
                    i * cap : (i + 1) * cap, part * LANES : (part + 1) * LANES
                ]
            send_ref[d, parts * cap : parts * cap + 8, :] = jnp.broadcast_to(
                slots[d : d + 1, :], (8, LANES)
            ).astype(BF16)
        span = pl.ds(g * here, here)
        save = pltpu.make_async_copy(send_ref.at[span], send_hbm.at[span], sems.at[3 + g])
        save.start()
        saves.append(save)
    for save in saves:
        save.wait()


def forward_kernel(
    sky_ref,
    beam_ref,
    row_ref,
    twist_ref,
    mat_ref,
    first_ref,
    bias_ref,
    second_ref,
    high_ref,
    low_ref,
    one_ref,
    two_ref,
    part_ref,
):
    prepare(first_ref, bias_ref, second_ref, one_ref, two_ref)
    rows, cols = sky_ref.shape
    outer = cols // LANES
    weighted = sky_ref[...] * beam_ref[...]
    w_high, w_low = split(weighted)
    mid = mm(row_ref[...], jnp.concatenate([w_high, w_low, w_high], axis=0))
    lines = [
        (
            mid[:rows, i * LANES : (i + 1) * LANES],
            mid[rows:, i * LANES : (i + 1) * LANES],
        )
        for i in range(outer)
    ]
    spread = dft16(lines, -1)
    blocks = []
    for w in range(outer):
        re, im = spread[w]
        tr, ti = twist_ref[0, w : w + 1, :], twist_ref[1, w : w + 1, :]
        blocks.append(jnp.concatenate([re * tr - im * ti, re * ti + im * tr], axis=1))
    high, low = split(jnp.concatenate(blocks, axis=0))
    mat_high, mat_low = mat_ref[0], mat_ref[1]
    model = mm(high, mat_high) + mm(low, mat_high) + mm(high, mat_low)
    for w in range(outer):
        for r in range(rows // S):
            for e in range(2):
                piece = model[
                    w * rows + r * S : w * rows + (r + 1) * S, e * LANES : (e + 1) * LANES
                ]
                piece_high, piece_low = split(piece)
                at = (pl.ds(e * 256 + w * S, S), pl.ds(r * LANES, LANES))
                part_ref[(0,) + at] = piece_high
                part_ref[(1,) + at] = piece_low
    swap = swap_matrix(high_ref.shape[0])
    high_ref[...] = mm(swap, part_ref[0]).astype(BF16)
    low_ref[...] = mm(swap, part_ref[1]).astype(BF16)


def residual_kernel(facets, cap, got_ref, high_ref, low_ref, res_hbm, sel_ref, own_ref, sems):
    total = facets * cap
    slots = high_ref.shape[1]
    parts = high_ref.shape[0] // LANES
    code = got_ref[:, parts * cap : parts * cap + 8, :].astype(F32).reshape(facets * 8, LANES)
    source = iota((total, facets * 8), 0) // cap
    spread = mm(one_hot(iota((total, facets * 8), 1) == source * 8), code.astype(BF16))
    lane = iota((total, LANES), 1)
    rank = iota((total, LANES), 0) % cap
    kept = jnp.where((lane & (LANES // 2 - 1)) == rank, spread, 0.0).astype(BF16)
    digit = jnp.where(iota((LANES, slots), 0) < LANES // 2, 16.0, 1.0).astype(BF16)
    code_all = mm(kept, digit)
    sel = one_hot(code_all.astype(jnp.int32) == iota((total, slots), 1) + 1)
    sel_ref[...] = sel
    contract = ((1,), (1,))
    predicted = mm(sel, high_ref[...], contract) + mm(sel, low_ref[...], contract)
    saves = []
    pieces = sems.shape[0]
    for i in range(pieces):
        here = facets // pieces
        at = slice(i * here * cap, (i + 1) * here * cap)
        for part in range(parts):
            cols = slice(part * LANES, (part + 1) * LANES)
            seen = got_ref[i * here : (i + 1) * here, part * cap : (part + 1) * cap, :]
            seen = seen.astype(F32).reshape(here * cap, LANES)
            own_ref[at, cols] = (predicted[at, cols] - seen).astype(BF16)
        save = pltpu.make_async_copy(own_ref.at[at, :], res_hbm.at[at, :], sems.at[i])
        save.start()
        saves.append(save)
    for save in saves:
        save.wait()


def window(index, count, cols):
    part = cols // count
    width = min(cols, part + (LANES if count == 2 else 2 * LANES))
    return jnp.clip(index * part - LANES, 0, cols - width), width


def inverse_kernel(
    count,
    res_ref,
    sel_ref,
    row_ref,
    twist_ref,
    mat_ref,
    sky_hbm,
    beam_hbm,
    keep_ref,
    *rest,
):
    send_refs = rest[: count - 1]
    sky_ref, beam_ref, lines_ref, shift_ref, grid_ref, sems = rest[count - 1 :]
    rows, cols = beam_ref.shape
    outer = cols // LANES
    me = lax.axis_index("freq")
    start, width = window(me, count, cols)
    sky_part = sky_hbm.at[:, pl.ds(pl.multiple_of(start, LANES), width)]
    loads = [
        pltpu.make_async_copy(beam_hbm, beam_ref, sems.at[0]),
        pltpu.make_async_copy(sky_part, sky_ref, sems.at[1]),
    ]
    for load in loads:
        load.start()
    grid = mm(res_ref[...], sel_ref[...], ((0,), (0,)))
    for r in range(rows // S):
        grid_ref[r] = grid[:, r * LANES : (r + 1) * LANES]
    blocks = []
    for w in range(outer):
        blocks.append(
            jnp.concatenate(
                [
                    jnp.concatenate(
                        [
                            grid_ref[r, pl.ds(e * S * S + w, S, stride=S), :]
                            for e in range(2)
                        ],
                        axis=1,
                    )
                    for r in range(rows // S)
                ],
                axis=0,
            )
        )
    cells = jnp.concatenate(blocks, axis=0).astype(BF16)
    mid = mm(jnp.concatenate([cells, cells], axis=1), mat_ref[...].reshape(4 * LANES, 2 * LANES))
    lines = []
    for w in range(outer):
        re = mid[w * rows : (w + 1) * rows, :LANES]
        im = mid[w * rows : (w + 1) * rows, LANES:]
        tr, ti = twist_ref[0, w : w + 1, :], twist_ref[1, w : w + 1, :]
        lines.append((re * tr - im * ti, re * ti + im * tr))
    spread = dft16(lines, 1)
    for i, pair in enumerate(spread):
        for e in range(2):
            line = pair[e].astype(BF16)
            lines_ref[e * rows : (e + 1) * rows, i * LANES : (i + 1) * LANES] = line
            lines_ref[(2 + e) * rows : (3 + e) * rows, i * LANES : (i + 1) * LANES] = line
    back = mm(row_ref[...], lines_ref[...])
    for load in loads:
        load.wait()
    shift_ref[...] = back * beam_ref[...] * (-STEP)
    for d in range(count):
        start, width = window(lax.rem(me + d, count), count, cols)
        at = pl.ds(pl.multiple_of(start, LANES), width)
        if d == 0:
            keep_ref[...] = shift_ref[:, at] + sky_ref[...]
        else:
            send_refs[d - 1][...] = shift_ref[:, at].astype(BF16)


def sum_kernel(keep_ref, *refs):
    main_ref, near_ref, far_ref = refs[-3:]
    rows = keep_ref.shape[0]
    main = keep_ref[...]
    for ref in refs[:-3]:
        main = main + ref[...].astype(F32)
    main_ref[...] = main
    even = (lax.axis_index("facet") & 1) == 0
    top, bottom = main[0:2], main[rows - 2 : rows]
    near_ref[...] = jnp.where(even, bottom, top)
    far_ref[...] = jnp.where(even, top, bottom)


def prepare(first_ref, bias_ref, second_ref, one_ref, two_ref):
    hidden = first_ref.shape[2]
    depth = one_ref.shape[1]
    full = (BAND + 2) * 9
    bias_high, bias_low = split(bias_ref[...])
    line = iota((8, depth), 0)
    lane = iota((8, depth), 1)
    group = lane * 2731 >> 16
    term = group * 86 >> 8
    col = group - term * 3
    taps = one_hot(((line == col) & (term < 2)) | ((line - 3 == col) & (term == 2)))
    ends = one_hot(((line == 6) & (lane == full)) | ((line == 7) & (lane == full + 1)))
    values = []
    for a in range(3):
        high, low = split(first_ref[a])
        pieces = [high, low, bias_high, bias_low]
        weights = jnp.concatenate([p.astype(F32) for p in pieces], axis=0).astype(BF16)
        values.append(mm(weights, taps, ((0,), (0,))))
        if a == 0:
            offset = mm(weights, ends, ((0,), (0,)))
    lane = iota((hidden, depth), 1)
    yin = lane - (lane * 2731 >> 16) * (BAND + 2)
    for y in range(BAND):
        block = offset
        for a in range(3):
            block = block + jnp.where(yin == y + a, values[a], 0.0)
        one_ref[y * hidden : (y + 1) * hidden, :] = block.astype(BF16)

    wide = two_ref.shape[1]
    tall = BAND + 2
    expand = one_hot(iota((hidden, wide), 0) == (iota((hidden, wide), 1) & (hidden - 1)))
    pieces = [split(second_ref[a]) for a in range(3)]
    gap = iota((tall, wide), 1) // hidden + 2 - iota((tall, wide), 0)
    blocks = []
    for half in range(2):
        lines = [mm(pieces[a][half], expand) for a in range(3)]
        for b in range(3):
            total = jnp.zeros((tall, wide), F32)
            for a in range(3):
                total = jnp.where(gap == a, lines[a][b : b + 1, :], total)
            blocks.append(total)
    two_ref[...] = jnp.concatenate(blocks, axis=0).astype(BF16)


def moved(value):
    width = value.shape[1]
    lane = iota(value.shape, 1)
    return (
        jnp.where(lane == 0, 0.0, pltpu.roll(value, 1, 1)),
        jnp.where(lane == width - 1, 0.0, pltpu.roll(value, width - 1, 1)),
    )


def stack_of(band):
    ones = jnp.where(iota((8, band.shape[1]), 0) < 2, 1.0, 0.0)
    high = band.astype(BF16).astype(F32)
    shifted = []
    for value in (high, band - high):
        left, right = moved(value)
        shifted.append([left, value, right])
    return jnp.concatenate(shifted[0] + shifted[1] + shifted[0] + [ones], axis=0).astype(BF16)


def share_of(taps):
    tall = BAND + 2
    parts = [
        taps[b * tall : (b + 1) * tall] + taps[(3 + b) * tall : (4 + b) * tall] for b in range(3)
    ]
    return parts[1] + moved(parts[0])[0] + moved(parts[2])[1]


def prior_kernel(main_ref, near_ref, one_ref, two_ref, sum_ref, base_ref):
    rows, width = main_ref.shape
    tall = BAND + 2
    pair = 2 * one_ref.shape[0] // BAND
    main, near = main_ref[...], near_ref[...]
    even = (lax.axis_index("facet") & 1) == 0
    base_ref[8 : rows + 8, :] = main
    base_ref[6:8, :] = jnp.where(even, 0.0, near)
    base_ref[rows + 8 : rows + 10, :] = jnp.where(even, near, 0.0)
    sum_ref[0:8, :] = jnp.zeros((8, width), F32)
    sum_ref[8 : rows + 8, :] = main
    sum_ref[rows + 8 :, :] = jnp.zeros((8, width), F32)
    spots = [slice(k * BAND + 6, k * BAND + 6 + tall) for k in range((rows + 2) // BAND)]
    stack = jnp.concatenate([stack_of(base_ref[spot, :]) for spot in spots], axis=1)
    hidden = jnp.maximum(mm(one_ref[...], stack), 0.0)
    head, body, foot = hidden[:pair], hidden[pair:-pair], hidden[-pair:]
    head = jnp.concatenate([jnp.where(even, 0.0, head[:, :width]), head[:, width:]], axis=1)
    foot = jnp.concatenate([foot[:, :-width], jnp.where(even, foot[:, -width:], 0.0)], axis=1)
    hidden = jnp.concatenate([head, body, foot], axis=0).astype(BF16)
    taps = mm(two_ref[...], hidden)
    for k, spot in enumerate(spots):
        sum_ref[spot, :] = sum_ref[spot, :] + share_of(taps[:, k * width : (k + 1) * width])


def edge_kernel(
    count,
    part,
    sum_ref,
    main_ref,
    far_ref,
    one_ref,
    two_ref,
    dest_ref,
    back_ref,
    out_hbm,
    tiles_hbm,
    base_ref,
    share_ref,
    last_ref,
    tiles_ref,
    sems,
):
    rows, width = main_ref.shape
    tall = BAND + 2
    height = one_ref.shape[0]
    inner = height // BAND
    pair = 2 * inner
    place = lax.axis_index("facet")
    final = lax.axis_size("facet") - 1
    even = (place & 1) == 0
    me = lax.axis_index("freq")
    start, _ = window(me, count, part * count)
    at = pl.ds(pl.multiple_of(me * part - start, LANES), part)
    done = rows - 8
    first = pl.multiple_of(jnp.where(even, 8, 0), 8)
    early = pltpu.make_async_copy(
        sum_ref.at[pl.ds(pl.multiple_of(first + 8, 8), done), at],
        out_hbm.at[pl.ds(first, done), :],
        sems.at[0],
    )
    early.start()
    placing = one_hot(iota((back_ref.shape[0], dest_ref.shape[1]), 0) == dest_ref[...])
    tiles_ref[...] = mm(placing, back_ref[...], ((0,), (0,))).astype(BF16)
    tiles = pltpu.make_async_copy(tiles_ref, tiles_hbm, sems.at[2])
    tiles.start()
    far = far_ref[...]
    base_ref[0:2, :] = far
    base_ref[2:tall, :] = main_ref[0:BAND, :]
    base_ref[32 : 32 + BAND, :] = main_ref[rows - BAND : rows, :]
    base_ref[32 + BAND : 32 + tall, :] = far
    band = jnp.where(even, base_ref[0:tall, :], base_ref[32 : 32 + tall, :])
    table = one_ref[pl.ds(pl.multiple_of(jnp.where(even, 0, height - pair), 16), pair), :]
    hidden = jnp.maximum(mm(table, stack_of(band)), 0.0)
    hidden = jnp.concatenate(
        [
            jnp.where(place == 0, 0.0, hidden[:inner]),
            jnp.where(place == final, 0.0, hidden[inner:]),
        ],
        axis=0,
    )
    second = jnp.where(
        even, two_ref[:, :pair].astype(F32), two_ref[:, height - pair :].astype(F32)
    )
    share_ref[0:8, :] = jnp.zeros((8, width), F32)
    share_ref[8 : tall + 8, :] = share_of(mm(second.astype(BF16), hidden.astype(BF16)))
    near_sum = jnp.where(even, sum_ref[8:16, :], sum_ref[rows : rows + 8, :])
    share = jnp.where(even, share_ref[10:18, :], share_ref[tall - 2 : tall + 6, :])
    last_ref[...] = near_sum + share
    late = pltpu.make_async_copy(
        last_ref.at[:, at],
        out_hbm.at[pl.ds(pl.multiple_of(jnp.where(even, 0, done), 8), 8), :],
        sems.at[1],
    )
    late.start()
    early.wait()
    tiles.wait()
    late.wait()


def shape(dims, dtype):
    return jax.ShapeDtypeStruct(dims, dtype)


def call(kernel, out_shape, flops, scratch=(), loaded=(), saved=(), limit=16):
    near = pl.BlockSpec(memory_space=pltpu.VMEM)
    far = pl.BlockSpec(memory_space=pltpu.HBM)

    def run(*args):
        return pl.pallas_call(
            kernel,
            out_shape=out_shape,
            in_specs=[far if i in loaded else near for i in range(len(args))],
            out_specs=[far if i in saved else near for i in range(len(out_shape))]
            if isinstance(out_shape, list)
            else near,
            scratch_shapes=scratch,
            compiler_params=pltpu.CompilerParams(vmem_limit_bytes=limit << 20),
            cost_estimate=pl.CostEstimate(flops=flops, bytes_accessed=4 << 20, transcendentals=0),
        )(*args)

    return run


def on_device(sky, beam, observed, facet_of, tile_slot, conv_first, bias_first, conv_second):
    rows, cols = sky.shape
    beam = beam.reshape(rows, cols)
    facets = lax.axis_size("facet")
    count = lax.axis_size("freq")
    tiles, width = observed.shape
    cap = 2 * tiles // facets
    total = facets * cap
    slots = (rows // S) * (cols // S)
    hidden = conv_first.shape[0]
    row_f, twist_f, mat_f = tables(rows, cols, -1)
    row_b, twist_b, mat_b = tables(rows, cols, 1)

    deep = (width // LANES) * cap + 8
    send, dest = call(
        functools.partial(pack_kernel, facets, cap),
        [shape((facets, deep, LANES), BF16), shape((1, tiles), jnp.int32)],
        1 << 28,
        scratch=[
            pltpu.VMEM((1, tiles), jnp.int32),
            pltpu.VMEM((1, tiles), jnp.int32),
            pltpu.VMEM((tiles, width), BF16),
            pltpu.VMEM((facets, deep, LANES), BF16),
            pltpu.SemaphoreType.DMA((7,)),
        ],
        loaded=(0, 1, 2),
        saved=(0,),
    )(
        *(
            pltpu.with_memory_space_constraint(value, pltpu.HBM)
            for value in (facet_of.reshape(1, tiles), tile_slot.reshape(1, tiles), observed)
        )
    )
    got = lax.all_to_all(send, "facet", split_axis=0, concat_axis=0, tiled=True)

    high, low, first, second = call(
        forward_kernel,
        [
            shape((width, slots), BF16),
            shape((width, slots), BF16),
            shape((hidden * BAND, 9 * (BAND + 2) + 8), BF16),
            shape((6 * (BAND + 2), hidden * BAND), BF16),
        ],
        1 << 30,
        scratch=[pltpu.VMEM((2, width, slots), BF16)],
    )(
        sky,
        beam,
        row_f,
        twist_f,
        mat_f,
        conv_first.transpose(1, 2, 0),
        bias_first.reshape(1, hidden),
        conv_second.transpose(1, 2, 0),
    )

    residual, select, own = call(
        functools.partial(residual_kernel, facets, cap),
        [shape((total, width), BF16), shape((total, slots), BF16), shape((total, width), BF16)],
        1 << 30,
        scratch=[pltpu.SemaphoreType.DMA((4,))],
        saved=(0,),
    )(got, *(pltpu.with_memory_space_constraint(value, pltpu.VMEM) for value in (high, low)))
    returned = lax.all_to_all(
        residual.reshape(facets, cap, width), "facet", split_axis=0, concat_axis=0, tiled=True
    ).reshape(total, width)

    _, wide = window(0, count, cols)
    keep, *sends = call(
        functools.partial(inverse_kernel, count),
        [shape((rows, wide), F32)] + [shape((rows, wide), BF16)] * (count - 1),
        1 << 30,
        scratch=[
            pltpu.VMEM((rows, wide), F32),
            pltpu.VMEM((rows, cols), F32),
            pltpu.VMEM((4 * rows, cols), BF16),
            pltpu.VMEM((rows, cols), F32),
            pltpu.VMEM((rows // S, width, LANES), F32),
            pltpu.SemaphoreType.DMA((2,)),
        ],
        loaded=(5, 6),
    )(
        own,
        select,
        row_b,
        twist_b,
        mat_b,
        *(pltpu.with_memory_space_constraint(value, pltpu.HBM) for value in (sky, beam)),
    )

    def beside(value, to):
        pairs = [(p, to(p)) for p in range(facets) if 0 <= to(p) < facets]
        return lax.ppermute(value, "facet", pairs)

    gots = [
        lax.ppermute(value, "freq", [(f, (f + d + 1) % count) for f in range(count)])
        for d, value in enumerate(sends)
    ]
    main, near, far = call(
        sum_kernel,
        [shape((rows, wide), F32), shape((2, wide), F32), shape((2, wide), F32)],
        1 << 24,
    )(keep, *gots)
    far = beside(far, lambda p: p + 1 if p & 1 else p - 1)
    near = beside(near, lambda p: p ^ 1)
    tall_rows = pltpu.VMEM((rows + 16, wide), F32)
    partial = call(
        prior_kernel, shape((rows + 16, wide), F32), 1 << 31, scratch=[tall_rows], limit=32
    )(main, near, first, second)
    image, tiles_out = call(
        functools.partial(edge_kernel, count, cols // count),
        [shape((rows, cols // count), F32), shape((tiles, width), BF16)],
        1 << 30,
        scratch=[
            pltpu.VMEM((64, wide), F32),
            pltpu.VMEM((BAND + 10, wide), F32),
            pltpu.VMEM((8, wide), F32),
            pltpu.VMEM((tiles, width), BF16),
            pltpu.SemaphoreType.DMA((3,)),
        ],
        saved=(0, 1),
    )(partial, main, far, first, second, dest, returned)
    return tiles_out, image


def solution(mesh):
    placed = (
        P("facet", None),
        P("freq", "facet", None),
        P(("freq", "facet"), None),
        P(("freq", "facet")),
        P(("freq", "facet")),
        P(),
        P(),
        P(),
    )

    return jax.shard_map(
        on_device,
        mesh=mesh,
        in_specs=placed,
        out_specs=(P(("freq", "facet"), None), P("facet", "freq")),
        check_vma=False,
    )
```

```python
import functools
import math

import jax
import jax.numpy as jnp
import numpy as np
from jax import lax
from jax.experimental import pallas as pl
from jax.experimental.pallas import tpu as pltpu
from jax.sharding import PartitionSpec as P


S = 16
LANES = 128
BAND = 22
STEP = 0.5
F32 = jnp.float32
BF16 = jnp.bfloat16


def iota(shape, dim):
    return lax.broadcasted_iota(jnp.int32, shape, dim)


def mm(a, b, dims=((1,), (0,))):
    return lax.dot_general(a, b, (dims, ((), ())), preferred_element_type=F32)


def one_hot(cond):
    return jnp.where(cond, 1.0, 0.0).astype(BF16)


def split(x):
    high = x.astype(BF16)
    return high, (x - high.astype(F32)).astype(BF16)


def np_split(x):
    x = np.asarray(x, np.float32)
    high = x.astype(BF16)
    return high, (x - high.astype(np.float32)).astype(BF16)


def tables(rows, cols, sign):
    outer = cols // LANES
    scale = 1.0 / math.sqrt(rows * cols)
    k = np.arange(rows)
    angle = sign * 2.0 * np.pi * ((k[:, None] * k[None, :]) % rows) / rows
    cos_r, sin_r = np.cos(angle) * scale, np.sin(angle) * scale
    if sign < 0:
        row_high, row_low = np_split(np.concatenate([cos_r, sin_r], 0))
        row = np.concatenate([row_high, row_high, row_low], 1)
    else:
        row = np.concatenate(np_split(np.concatenate([cos_r, -sin_r], 1)), 1)
    i2 = np.arange(LANES)
    w = np.arange(outer)
    twist = sign * 2.0 * np.pi * ((w[:, None] * i2[None, :]) % cols) / cols
    inner = sign * 2.0 * np.pi * ((i2[:, None] * i2[None, :]) % LANES) / LANES
    c, s = np.cos(inner), np.sin(inner)
    mat_high, mat_low = np_split(np.block([[c, s], [-s, c]]))
    return (
        row,
        np.stack([np.cos(twist), np.sin(twist)]).astype(np.float32),
        np.stack([mat_high, mat_low]),
    )


def times_i(z, sign):
    re, im = z
    return (-im, re) if sign > 0 else (im, -re)


def add(a, b):
    return (a[0] + b[0], a[1] + b[1])


def sub(a, b):
    return (a[0] - b[0], a[1] - b[1])


def dft4(x, sign):
    s0, s1 = add(x[0], x[2]), sub(x[0], x[2])
    s2, s3 = add(x[1], x[3]), times_i(sub(x[1], x[3]), sign)
    return [add(s0, s2), add(s1, s3), sub(s0, s2), sub(s1, s3)]


def dft16(x, sign):
    mid = [dft4([x[4 * a + b] for a in range(4)], sign) for b in range(4)]
    out = [None] * 16
    for c in range(4):
        turned = []
        for b in range(4):
            re, im = mid[b][c]
            phase = (b * c) % 16
            if phase == 0:
                turned.append((re, im))
            elif phase == 4:
                turned.append(times_i((re, im), sign))
            else:
                wr = math.cos(2.0 * math.pi * phase / 16)
                wi = sign * math.sin(2.0 * math.pi * phase / 16)
                turned.append((re * wr - im * wi, re * wi + im * wr))
        for d, value in enumerate(dft4(turned, sign)):
            out[c + 4 * d] = value
    return out


def swap_matrix(size):
    src = iota((1, size), 1)
    swapped = (src & -256) | ((src & 15) << 4) | ((src >> 4) & 15)
    return one_hot(iota((size, size), 0) == swapped)


def pack_kernel(
    facets,
    cap,
    facet_hbm,
    slot_hbm,
    seen_hbm,
    send_hbm,
    dest_ref,
    facet_ref,
    slot_ref,
    seen_ref,
    send_ref,
    sems,
):
    tiles, width = seen_ref.shape
    total = facets * cap
    loads = [
        pltpu.make_async_copy(src, dst, sems.at[i])
        for i, (src, dst) in enumerate(
            ((facet_hbm, facet_ref), (slot_hbm, slot_ref), (seen_hbm, seen_ref))
        )
    ]
    for load in loads:
        load.start()
    before = one_hot(iota((tiles, tiles), 0) < iota((tiles, tiles), 1))
    loads[0].wait()
    facet = facet_ref[...]
    member = iota((facets, tiles), 0) == facet
    member_f = jnp.where(member, 1.0, 0.0)
    ranks = mm(member_f.astype(BF16), before)
    rank = jnp.sum(member_f * ranks, axis=0, keepdims=True).astype(jnp.int32)
    dest = facet * cap + rank
    dest_ref[...] = dest
    loads[1].wait()
    code = slot_ref[...] + 1
    lane = iota((LANES, tiles), 0)
    slots = mm(
        (member_f * (code >> 4).astype(F32)).astype(BF16), one_hot(lane == rank), ((1,), (1,))
    ) + mm(
        (member_f * (code & 15).astype(F32)).astype(BF16),
        one_hot(lane - LANES // 2 == rank),
        ((1,), (1,)),
    )
    parts = width // LANES
    groups = 4
    here = facets // groups
    loads[2].wait()
    saves = []
    for g in range(groups):
        placing = one_hot(iota((total // groups, tiles), 0) + g * (total // groups) == dest)
        packed = mm(placing, seen_ref[...]).astype(BF16)
        for i in range(here):
            d = g * here + i
            for part in range(parts):
                send_ref[d, part * cap : (part + 1) * cap, :] = packed[
                    i * cap : (i + 1) * cap, part * LANES : (part + 1) * LANES
                ]
            send_ref[d, parts * cap : parts * cap + 8, :] = jnp.broadcast_to(
                slots[d : d + 1, :], (8, LANES)
            ).astype(BF16)
        span = pl.ds(g * here, here)
        save = pltpu.make_async_copy(send_ref.at[span], send_hbm.at[span], sems.at[3 + g])
        save.start()
        saves.append(save)
    for save in saves:
        save.wait()


def forward_kernel(
    sky_ref,
    beam_ref,
    row_ref,
    twist_ref,
    mat_ref,
    first_ref,
    bias_ref,
    second_ref,
    high_ref,
    low_ref,
    one_ref,
    two_ref,
    part_ref,
):
    prepare(first_ref, bias_ref, second_ref, one_ref, two_ref)
    rows, cols = sky_ref.shape
    outer = cols // LANES
    weighted = sky_ref[...] * beam_ref[...]
    w_high, w_low = split(weighted)
    mid = mm(row_ref[...], jnp.concatenate([w_high, w_low, w_high], axis=0))
    lines = [
        (
            mid[:rows, i * LANES : (i + 1) * LANES],
            mid[rows:, i * LANES : (i + 1) * LANES],
        )
        for i in range(outer)
    ]
    spread = dft16(lines, -1)
    blocks = []
    for w in range(outer):
        re, im = spread[w]
        tr, ti = twist_ref[0, w : w + 1, :], twist_ref[1, w : w + 1, :]
        blocks.append(jnp.concatenate([re * tr - im * ti, re * ti + im * tr], axis=1))
    high, low = split(jnp.concatenate(blocks, axis=0))
    mat_high, mat_low = mat_ref[0], mat_ref[1]
    model = mm(high, mat_high) + mm(low, mat_high) + mm(high, mat_low)
    for w in range(outer):
        for r in range(rows // S):
            for e in range(2):
                piece = model[
                    w * rows + r * S : w * rows + (r + 1) * S, e * LANES : (e + 1) * LANES
                ]
                piece_high, piece_low = split(piece)
                at = (pl.ds(e * 256 + w * S, S), pl.ds(r * LANES, LANES))
                part_ref[(0,) + at] = piece_high
                part_ref[(1,) + at] = piece_low
    swap = swap_matrix(high_ref.shape[0])
    high_ref[...] = mm(swap, part_ref[0]).astype(BF16)
    low_ref[...] = mm(swap, part_ref[1]).astype(BF16)


def residual_kernel(facets, cap, got_ref, high_ref, low_ref, res_hbm, sel_ref, own_ref, sems):
    slots = high_ref.shape[1]
    parts = high_ref.shape[0] // LANES
    pieces = sems.shape[0]
    here = facets // pieces
    count = here * cap
    contract = ((1,), (1,))
    lane = iota((count, LANES), 1)
    rank = iota((count, LANES), 0) % cap
    mine = (lane & (LANES // 2 - 1)) == rank
    digit = jnp.where(iota((LANES, LANES), 0) < LANES // 2, 16.0, 1.0).astype(BF16)
    saves = []
    for i in range(pieces):
        group = slice(i * here, (i + 1) * here)
        at = slice(i * count, (i + 1) * count)
        code = got_ref[group, parts * cap : parts * cap + 8, :].astype(F32)
        code = jnp.broadcast_to(code[:, 0:1, :], (here, cap, LANES)).reshape(count, LANES)
        slot = mm(jnp.where(mine, code, 0.0).astype(BF16), digit).astype(jnp.int32) - 1
        sel = jnp.concatenate(
            [one_hot(slot == lane + r * LANES) for r in range(slots // LANES)], axis=1
        )
        sel_ref[at, :] = sel
        predicted = mm(sel, high_ref[...], contract) + mm(sel, low_ref[...], contract)
        for part in range(parts):
            cols = slice(part * LANES, (part + 1) * LANES)
            seen = got_ref[group, part * cap : (part + 1) * cap, :]
            seen = seen.astype(F32).reshape(count, LANES)
            own_ref[at, cols] = (predicted[:, cols] - seen).astype(BF16)
        save = pltpu.make_async_copy(own_ref.at[at, :], res_hbm.at[at, :], sems.at[i])
        save.start()
        saves.append(save)
    for save in saves:
        save.wait()


def window(index, count, cols):
    part = cols // count
    width = min(cols, part + (LANES if count == 2 else 2 * LANES))
    return jnp.clip(index * part - LANES, 0, cols - width), width


def inverse_kernel(
    count,
    res_ref,
    sel_ref,
    row_ref,
    twist_ref,
    mat_ref,
    sky_hbm,
    beam_hbm,
    keep_ref,
    *rest,
):
    send_refs = rest[: count - 1]
    sky_ref, beam_ref, lines_ref, shift_ref, grid_ref, sems = rest[count - 1 :]
    rows, cols = beam_ref.shape
    outer = cols // LANES
    me = lax.axis_index("freq")
    start, width = window(me, count, cols)
    sky_part = sky_hbm.at[:, pl.ds(pl.multiple_of(start, LANES), width)]
    loads = [
        pltpu.make_async_copy(beam_hbm, beam_ref, sems.at[0]),
        pltpu.make_async_copy(sky_part, sky_ref, sems.at[1]),
    ]
    for load in loads:
        load.start()
    grid = mm(res_ref[...], sel_ref[...], ((0,), (0,)))
    for r in range(rows // S):
        grid_ref[r] = grid[:, r * LANES : (r + 1) * LANES]
    blocks = []
    for w in range(outer):
        blocks.append(
            jnp.concatenate(
                [
                    jnp.concatenate(
                        [
                            grid_ref[r, pl.ds(e * S * S + w, S, stride=S), :]
                            for e in range(2)
                        ],
                        axis=1,
                    )
                    for r in range(rows // S)
                ],
                axis=0,
            )
        )
    cells = jnp.concatenate(blocks, axis=0).astype(BF16)
    mid = mm(jnp.concatenate([cells, cells], axis=1), mat_ref[...].reshape(4 * LANES, 2 * LANES))
    lines = []
    for w in range(outer):
        re = mid[w * rows : (w + 1) * rows, :LANES]
        im = mid[w * rows : (w + 1) * rows, LANES:]
        tr, ti = twist_ref[0, w : w + 1, :], twist_ref[1, w : w + 1, :]
        lines.append((re * tr - im * ti, re * ti + im * tr))
    spread = dft16(lines, 1)
    for i, pair in enumerate(spread):
        for e in range(2):
            line = pair[e].astype(BF16)
            lines_ref[e * rows : (e + 1) * rows, i * LANES : (i + 1) * LANES] = line
            lines_ref[(2 + e) * rows : (3 + e) * rows, i * LANES : (i + 1) * LANES] = line
    back = mm(row_ref[...], lines_ref[...])
    for load in loads:
        load.wait()
    shift_ref[...] = back * beam_ref[...] * (-STEP)
    for d in range(count):
        start, width = window(lax.rem(me + d, count), count, cols)
        at = pl.ds(pl.multiple_of(start, LANES), width)
        if d == 0:
            keep_ref[...] = shift_ref[:, at] + sky_ref[...]
        else:
            send_refs[d - 1][...] = shift_ref[:, at].astype(BF16)


def sum_kernel(keep_ref, *refs):
    main_ref, near_ref, far_ref = refs[-3:]
    rows = keep_ref.shape[0]
    main = keep_ref[...]
    for ref in refs[:-3]:
        main = main + ref[...].astype(F32)
    main_ref[...] = main
    even = (lax.axis_index("facet") & 1) == 0
    top, bottom = main[0:2], main[rows - 2 : rows]
    near_ref[...] = jnp.where(even, bottom, top)
    far_ref[...] = jnp.where(even, top, bottom)


def prepare(first_ref, bias_ref, second_ref, one_ref, two_ref):
    hidden = first_ref.shape[2]
    depth = one_ref.shape[1]
    full = (BAND + 2) * 9
    bias_high, bias_low = split(bias_ref[...])
    line = iota((8, depth), 0)
    lane = iota((8, depth), 1)
    group = lane * 2731 >> 16
    term = group * 86 >> 8
    col = group - term * 3
    taps = one_hot(((line == col) & (term < 2)) | ((line - 3 == col) & (term == 2)))
    ends = one_hot(((line == 6) & (lane == full)) | ((line == 7) & (lane == full + 1)))
    values = []
    for a in range(3):
        high, low = split(first_ref[a])
        pieces = [high, low, bias_high, bias_low]
        weights = jnp.concatenate([p.astype(F32) for p in pieces], axis=0).astype(BF16)
        values.append(mm(weights, taps, ((0,), (0,))))
        if a == 0:
            offset = mm(weights, ends, ((0,), (0,)))
    lane = iota((hidden, depth), 1)
    yin = lane - (lane * 2731 >> 16) * (BAND + 2)
    for y in range(BAND):
        block = offset
        for a in range(3):
            block = block + jnp.where(yin == y + a, values[a], 0.0)
        one_ref[y * hidden : (y + 1) * hidden, :] = block.astype(BF16)

    wide = two_ref.shape[1]
    tall = BAND + 2
    expand = one_hot(iota((hidden, wide), 0) == (iota((hidden, wide), 1) & (hidden - 1)))
    pieces = [split(second_ref[a]) for a in range(3)]
    gap = iota((tall, wide), 1) // hidden + 2 - iota((tall, wide), 0)
    blocks = []
    for half in range(2):
        lines = [mm(pieces[a][half], expand) for a in range(3)]
        for b in range(3):
            total = jnp.zeros((tall, wide), F32)
            for a in range(3):
                total = jnp.where(gap == a, lines[a][b : b + 1, :], total)
            blocks.append(total)
    two_ref[...] = jnp.concatenate(blocks, axis=0).astype(BF16)


def moved(value):
    width = value.shape[1]
    lane = iota(value.shape, 1)
    return (
        jnp.where(lane == 0, 0.0, pltpu.roll(value, 1, 1)),
        jnp.where(lane == width - 1, 0.0, pltpu.roll(value, width - 1, 1)),
    )


def stack_of(band):
    ones = jnp.where(iota((8, band.shape[1]), 0) < 2, 1.0, 0.0)
    high = band.astype(BF16).astype(F32)
    shifted = []
    for value in (high, band - high):
        left, right = moved(value)
        shifted.append([left, value, right])
    return jnp.concatenate(shifted[0] + shifted[1] + shifted[0] + [ones], axis=0).astype(BF16)


def share_of(taps):
    tall = BAND + 2
    parts = [
        taps[b * tall : (b + 1) * tall] + taps[(3 + b) * tall : (4 + b) * tall] for b in range(3)
    ]
    return parts[1] + moved(parts[0])[0] + moved(parts[2])[1]


def prior_kernel(main_ref, near_ref, one_ref, two_ref, sum_ref, base_ref):
    rows, width = main_ref.shape
    tall = BAND + 2
    pair = 2 * one_ref.shape[0] // BAND
    main, near = main_ref[...], near_ref[...]
    even = (lax.axis_index("facet") & 1) == 0
    base_ref[8 : rows + 8, :] = main
    base_ref[6:8, :] = jnp.where(even, 0.0, near)
    base_ref[rows + 8 : rows + 10, :] = jnp.where(even, near, 0.0)
    sum_ref[0:8, :] = jnp.zeros((8, width), F32)
    sum_ref[8 : rows + 8, :] = main
    sum_ref[rows + 8 :, :] = jnp.zeros((8, width), F32)
    spots = [slice(k * BAND + 6, k * BAND + 6 + tall) for k in range((rows + 2) // BAND)]
    stack = jnp.concatenate([stack_of(base_ref[spot, :]) for spot in spots], axis=1)
    hidden = jnp.maximum(mm(one_ref[...], stack), 0.0)
    head, body, foot = hidden[:pair], hidden[pair:-pair], hidden[-pair:]
    head = jnp.concatenate([jnp.where(even, 0.0, head[:, :width]), head[:, width:]], axis=1)
    foot = jnp.concatenate([foot[:, :-width], jnp.where(even, foot[:, -width:], 0.0)], axis=1)
    hidden = jnp.concatenate([head, body, foot], axis=0).astype(BF16)
    taps = mm(two_ref[...], hidden)
    for k, spot in enumerate(spots):
        sum_ref[spot, :] = sum_ref[spot, :] + share_of(taps[:, k * width : (k + 1) * width])


def edge_kernel(
    count,
    part,
    sum_ref,
    main_ref,
    far_ref,
    one_ref,
    two_ref,
    dest_ref,
    back_ref,
    out_hbm,
    tiles_hbm,
    base_ref,
    share_ref,
    last_ref,
    tiles_ref,
    sems,
):
    rows, width = main_ref.shape
    tall = BAND + 2
    height = one_ref.shape[0]
    inner = height // BAND
    pair = 2 * inner
    place = lax.axis_index("facet")
    final = lax.axis_size("facet") - 1
    even = (place & 1) == 0
    me = lax.axis_index("freq")
    start, _ = window(me, count, part * count)
    at = pl.ds(pl.multiple_of(me * part - start, LANES), part)
    done = rows - 8
    first = pl.multiple_of(jnp.where(even, 8, 0), 8)
    early = pltpu.make_async_copy(
        sum_ref.at[pl.ds(pl.multiple_of(first + 8, 8), done), at],
        out_hbm.at[pl.ds(first, done), :],
        sems.at[0],
    )
    early.start()
    placing = one_hot(iota((back_ref.shape[0], dest_ref.shape[1]), 0) == dest_ref[...])
    tiles_ref[...] = mm(placing, back_ref[...], ((0,), (0,))).astype(BF16)
    tiles = pltpu.make_async_copy(tiles_ref, tiles_hbm, sems.at[2])
    tiles.start()
    far = far_ref[...]
    base_ref[0:2, :] = far
    base_ref[2:tall, :] = main_ref[0:BAND, :]
    base_ref[32 : 32 + BAND, :] = main_ref[rows - BAND : rows, :]
    base_ref[32 + BAND : 32 + tall, :] = far
    band = jnp.where(even, base_ref[0:tall, :], base_ref[32 : 32 + tall, :])
    table = one_ref[pl.ds(pl.multiple_of(jnp.where(even, 0, height - pair), 16), pair), :]
    hidden = jnp.maximum(mm(table, stack_of(band)), 0.0)
    hidden = jnp.concatenate(
        [
            jnp.where(place == 0, 0.0, hidden[:inner]),
            jnp.where(place == final, 0.0, hidden[inner:]),
        ],
        axis=0,
    )
    second = jnp.where(
        even, two_ref[:, :pair].astype(F32), two_ref[:, height - pair :].astype(F32)
    )
    share_ref[0:8, :] = jnp.zeros((8, width), F32)
    share_ref[8 : tall + 8, :] = share_of(mm(second.astype(BF16), hidden.astype(BF16)))
    near_sum = jnp.where(even, sum_ref[8:16, :], sum_ref[rows : rows + 8, :])
    share = jnp.where(even, share_ref[10:18, :], share_ref[tall - 2 : tall + 6, :])
    last_ref[...] = near_sum + share
    late = pltpu.make_async_copy(
        last_ref.at[:, at],
        out_hbm.at[pl.ds(pl.multiple_of(jnp.where(even, 0, done), 8), 8), :],
        sems.at[1],
    )
    late.start()
    early.wait()
    tiles.wait()
    late.wait()


def shape(dims, dtype):
    return jax.ShapeDtypeStruct(dims, dtype)


def call(kernel, out_shape, flops, scratch=(), loaded=(), saved=(), limit=16):
    near = pl.BlockSpec(memory_space=pltpu.VMEM)
    far = pl.BlockSpec(memory_space=pltpu.HBM)

    def run(*args):
        return pl.pallas_call(
            kernel,
            out_shape=out_shape,
            in_specs=[far if i in loaded else near for i in range(len(args))],
            out_specs=[far if i in saved else near for i in range(len(out_shape))]
            if isinstance(out_shape, list)
            else near,
            scratch_shapes=scratch,
            compiler_params=pltpu.CompilerParams(vmem_limit_bytes=limit << 20),
            cost_estimate=pl.CostEstimate(flops=flops, bytes_accessed=4 << 20, transcendentals=0),
        )(*args)

    return run


def on_device(sky, beam, observed, facet_of, tile_slot, conv_first, bias_first, conv_second):
    rows, cols = sky.shape
    beam = beam.reshape(rows, cols)
    facets = lax.axis_size("facet")
    count = lax.axis_size("freq")
    tiles, width = observed.shape
    cap = 2 * tiles // facets
    total = facets * cap
    slots = (rows // S) * (cols // S)
    hidden = conv_first.shape[0]
    row_f, twist_f, mat_f = tables(rows, cols, -1)
    row_b, twist_b, mat_b = tables(rows, cols, 1)

    deep = (width // LANES) * cap + 8
    send, dest = call(
        functools.partial(pack_kernel, facets, cap),
        [shape((facets, deep, LANES), BF16), shape((1, tiles), jnp.int32)],
        1 << 28,
        scratch=[
            pltpu.VMEM((1, tiles), jnp.int32),
            pltpu.VMEM((1, tiles), jnp.int32),
            pltpu.VMEM((tiles, width), BF16),
            pltpu.VMEM((facets, deep, LANES), BF16),
            pltpu.SemaphoreType.DMA((7,)),
        ],
        loaded=(0, 1, 2),
        saved=(0,),
    )(
        *(
            pltpu.with_memory_space_constraint(value, pltpu.HBM)
            for value in (facet_of.reshape(1, tiles), tile_slot.reshape(1, tiles), observed)
        )
    )
    got = lax.all_to_all(send, "facet", split_axis=0, concat_axis=0, tiled=True)

    high, low, first, second = call(
        forward_kernel,
        [
            shape((width, slots), BF16),
            shape((width, slots), BF16),
            shape((hidden * BAND, 9 * (BAND + 2) + 8), BF16),
            shape((6 * (BAND + 2), hidden * BAND), BF16),
        ],
        1 << 30,
        scratch=[pltpu.VMEM((2, width, slots), BF16)],
    )(
        sky,
        beam,
        row_f,
        twist_f,
        mat_f,
        conv_first.transpose(1, 2, 0),
        bias_first.reshape(1, hidden),
        conv_second.transpose(1, 2, 0),
    )

    residual, select, own = call(
        functools.partial(residual_kernel, facets, cap),
        [shape((total, width), BF16), shape((total, slots), BF16), shape((total, width), BF16)],
        1 << 30,
        scratch=[pltpu.SemaphoreType.DMA((2,))],
        saved=(0,),
    )(got, *(pltpu.with_memory_space_constraint(value, pltpu.VMEM) for value in (high, low)))
    returned = lax.all_to_all(
        residual.reshape(facets, cap, width), "facet", split_axis=0, concat_axis=0, tiled=True
    ).reshape(total, width)

    _, wide = window(0, count, cols)
    keep, *sends = call(
        functools.partial(inverse_kernel, count),
        [shape((rows, wide), F32)] + [shape((rows, wide), BF16)] * (count - 1),
        1 << 30,
        scratch=[
            pltpu.VMEM((rows, wide), F32),
            pltpu.VMEM((rows, cols), F32),
            pltpu.VMEM((4 * rows, cols), BF16),
            pltpu.VMEM((rows, cols), F32),
            pltpu.VMEM((rows // S, width, LANES), F32),
            pltpu.SemaphoreType.DMA((2,)),
        ],
        loaded=(5, 6),
    )(
        own,
        select,
        row_b,
        twist_b,
        mat_b,
        *(pltpu.with_memory_space_constraint(value, pltpu.HBM) for value in (sky, beam)),
    )

    def beside(value, to):
        pairs = [(p, to(p)) for p in range(facets) if 0 <= to(p) < facets]
        return lax.ppermute(value, "facet", pairs)

    gots = [
        lax.ppermute(value, "freq", [(f, (f + d + 1) % count) for f in range(count)])
        for d, value in enumerate(sends)
    ]
    main, near, far = call(
        sum_kernel,
        [shape((rows, wide), F32), shape((2, wide), F32), shape((2, wide), F32)],
        1 << 24,
    )(keep, *gots)
    far = beside(far, lambda p: p + 1 if p & 1 else p - 1)
    near = beside(near, lambda p: p ^ 1)
    tall_rows = pltpu.VMEM((rows + 16, wide), F32)
    partial = call(
        prior_kernel, shape((rows + 16, wide), F32), 1 << 31, scratch=[tall_rows], limit=32
    )(main, near, first, second)
    image, tiles_out = call(
        functools.partial(edge_kernel, count, cols // count),
        [shape((rows, cols // count), F32), shape((tiles, width), BF16)],
        1 << 30,
        scratch=[
            pltpu.VMEM((64, wide), F32),
            pltpu.VMEM((BAND + 10, wide), F32),
            pltpu.VMEM((8, wide), F32),
            pltpu.VMEM((tiles, width), BF16),
            pltpu.SemaphoreType.DMA((3,)),
        ],
        saved=(0, 1),
    )(partial, main, far, first, second, dest, returned)
    return tiles_out, image


def solution(mesh):
    placed = (
        P("facet", None),
        P("freq", "facet", None),
        P(("freq", "facet"), None),
        P(("freq", "facet")),
        P(("freq", "facet")),
        P(),
        P(),
        P(),
    )

    return jax.shard_map(
        on_device,
        mesh=mesh,
        in_specs=placed,
        out_specs=(P(("freq", "facet"), None), P("facet", "freq")),
        check_vma=False,
    )
```

```python
import functools
import math

import jax
import jax.numpy as jnp
import numpy as np
from jax import lax
from jax.experimental import pallas as pl
from jax.experimental.pallas import tpu as pltpu
from jax.sharding import PartitionSpec as P


S = 16
LANES = 128
BAND = 22
STEP = 0.5
F32 = jnp.float32
BF16 = jnp.bfloat16


def iota(shape, dim):
    return lax.broadcasted_iota(jnp.int32, shape, dim)


def mm(a, b, dims=((1,), (0,))):
    return lax.dot_general(a, b, (dims, ((), ())), preferred_element_type=F32)


def one_hot(cond):
    return jnp.where(cond, 1.0, 0.0).astype(BF16)


def split(x):
    high = x.astype(BF16)
    return high, (x - high.astype(F32)).astype(BF16)


def np_split(x):
    x = np.asarray(x, np.float32)
    high = x.astype(BF16)
    return high, (x - high.astype(np.float32)).astype(BF16)


def tables(rows, cols, sign):
    outer = cols // LANES
    scale = 1.0 / math.sqrt(rows * cols)
    k = np.arange(rows)
    angle = sign * 2.0 * np.pi * ((k[:, None] * k[None, :]) % rows) / rows
    cos_r, sin_r = np.cos(angle) * scale, np.sin(angle) * scale
    if sign < 0:
        row_high, row_low = np_split(np.concatenate([cos_r, sin_r], 0))
        row = np.concatenate([row_high, row_high, row_low], 1)
    else:
        row = np.concatenate(np_split(np.concatenate([cos_r, -sin_r], 1)), 1)
    i2 = np.arange(LANES)
    w = np.arange(outer)
    twist = sign * 2.0 * np.pi * ((w[:, None] * i2[None, :]) % cols) / cols
    inner = sign * 2.0 * np.pi * ((i2[:, None] * i2[None, :]) % LANES) / LANES
    c, s = np.cos(inner), np.sin(inner)
    mat_high, mat_low = np_split(np.block([[c, s], [-s, c]]))
    return (
        row,
        np.stack([np.cos(twist), np.sin(twist)]).astype(np.float32),
        np.stack([mat_high, mat_low]),
    )


def times_i(z, sign):
    re, im = z
    return (-im, re) if sign > 0 else (im, -re)


def add(a, b):
    return (a[0] + b[0], a[1] + b[1])


def sub(a, b):
    return (a[0] - b[0], a[1] - b[1])


def dft4(x, sign):
    s0, s1 = add(x[0], x[2]), sub(x[0], x[2])
    s2, s3 = add(x[1], x[3]), times_i(sub(x[1], x[3]), sign)
    return [add(s0, s2), add(s1, s3), sub(s0, s2), sub(s1, s3)]


def dft16(x, sign):
    mid = [dft4([x[4 * a + b] for a in range(4)], sign) for b in range(4)]
    out = [None] * 16
    for c in range(4):
        turned = []
        for b in range(4):
            re, im = mid[b][c]
            phase = (b * c) % 16
            if phase == 0:
                turned.append((re, im))
            elif phase == 4:
                turned.append(times_i((re, im), sign))
            else:
                wr = math.cos(2.0 * math.pi * phase / 16)
                wi = sign * math.sin(2.0 * math.pi * phase / 16)
                turned.append((re * wr - im * wi, re * wi + im * wr))
        for d, value in enumerate(dft4(turned, sign)):
            out[c + 4 * d] = value
    return out


def swap_matrix(size):
    src = iota((1, size), 1)
    swapped = (src & -256) | ((src & 15) << 4) | ((src >> 4) & 15)
    return one_hot(iota((size, size), 0) == swapped)


def pack_kernel(
    facets,
    cap,
    facet_hbm,
    slot_hbm,
    seen_hbm,
    send_hbm,
    dest_ref,
    facet_ref,
    slot_ref,
    seen_ref,
    send_ref,
    sems,
):
    tiles, width = seen_ref.shape
    total = facets * cap
    loads = [
        pltpu.make_async_copy(src, dst, sems.at[i])
        for i, (src, dst) in enumerate(
            ((facet_hbm, facet_ref), (slot_hbm, slot_ref), (seen_hbm, seen_ref))
        )
    ]
    for load in loads:
        load.start()
    before = one_hot(iota((tiles, tiles), 0) < iota((tiles, tiles), 1))
    loads[0].wait()
    facet = facet_ref[...]
    member = iota((facets, tiles), 0) == facet
    member_f = jnp.where(member, 1.0, 0.0)
    ranks = mm(member_f.astype(BF16), before)
    rank = jnp.sum(member_f * ranks, axis=0, keepdims=True).astype(jnp.int32)
    dest = facet * cap + rank
    dest_ref[...] = dest
    loads[1].wait()
    code = slot_ref[...] + 1
    lane = iota((LANES, tiles), 0)
    slots = mm(
        (member_f * (code >> 4).astype(F32)).astype(BF16), one_hot(lane == rank), ((1,), (1,))
    ) + mm(
        (member_f * (code & 15).astype(F32)).astype(BF16),
        one_hot(lane - LANES // 2 == rank),
        ((1,), (1,)),
    )
    parts = width // LANES
    groups = 4
    here = facets // groups
    loads[2].wait()
    saves = []
    for g in range(groups):
        placing = one_hot(iota((total // groups, tiles), 0) + g * (total // groups) == dest)
        packed = mm(placing, seen_ref[...]).astype(BF16)
        for i in range(here):
            d = g * here + i
            for part in range(parts):
                send_ref[d, part * cap : (part + 1) * cap, :] = packed[
                    i * cap : (i + 1) * cap, part * LANES : (part + 1) * LANES
                ]
            send_ref[d, parts * cap : parts * cap + 8, :] = jnp.broadcast_to(
                slots[d : d + 1, :], (8, LANES)
            ).astype(BF16)
        span = pl.ds(g * here, here)
        save = pltpu.make_async_copy(send_ref.at[span], send_hbm.at[span], sems.at[3 + g])
        save.start()
        saves.append(save)
    for save in saves:
        save.wait()


def forward_kernel(
    sky_ref,
    beam_ref,
    row_ref,
    twist_ref,
    mat_ref,
    first_ref,
    bias_ref,
    second_ref,
    dest_ref,
    high_ref,
    low_ref,
    one_ref,
    two_ref,
    place_ref,
    part_ref,
):
    spots = iota(place_ref.shape[::-1], 0)
    place_ref[...] = jnp.where(spots == dest_ref[...], 1.0, 0.0).T.astype(BF16)
    prepare(first_ref, bias_ref, second_ref, one_ref, two_ref)
    rows, cols = sky_ref.shape
    outer = cols // LANES
    weighted = sky_ref[...] * beam_ref[...]
    w_high, w_low = split(weighted)
    mid = mm(row_ref[...], jnp.concatenate([w_high, w_low, w_high], axis=0))
    lines = [
        (
            mid[:rows, i * LANES : (i + 1) * LANES],
            mid[rows:, i * LANES : (i + 1) * LANES],
        )
        for i in range(outer)
    ]
    spread = dft16(lines, -1)
    blocks = []
    for w in range(outer):
        re, im = spread[w]
        tr, ti = twist_ref[0, w : w + 1, :], twist_ref[1, w : w + 1, :]
        blocks.append(jnp.concatenate([re * tr - im * ti, re * ti + im * tr], axis=1))
    high, low = split(jnp.concatenate(blocks, axis=0))
    mat_high, mat_low = mat_ref[0], mat_ref[1]
    model = mm(high, mat_high) + mm(low, mat_high) + mm(high, mat_low)
    for w in range(outer):
        for r in range(rows // S):
            for e in range(2):
                piece = model[
                    w * rows + r * S : w * rows + (r + 1) * S, e * LANES : (e + 1) * LANES
                ]
                piece_high, piece_low = split(piece)
                at = (pl.ds(e * 256 + w * S, S), pl.ds(r * LANES, LANES))
                part_ref[(0,) + at] = piece_high
                part_ref[(1,) + at] = piece_low
    swap = swap_matrix(high_ref.shape[0])
    high_ref[...] = mm(swap, part_ref[0]).astype(BF16)
    low_ref[...] = mm(swap, part_ref[1]).astype(BF16)


def residual_kernel(facets, cap, got_ref, high_ref, low_ref, res_hbm, sel_ref, own_ref, sems):
    slots = high_ref.shape[1]
    parts = high_ref.shape[0] // LANES
    pieces = sems.shape[0]
    here = facets // pieces
    count = here * cap
    contract = ((1,), (1,))
    lane = iota((count, LANES), 1)
    rank = iota((count, LANES), 0) % cap
    mine = (lane & (LANES // 2 - 1)) == rank
    digit = jnp.where(iota((LANES, LANES), 0) < LANES // 2, 16.0, 1.0).astype(BF16)
    saves = []
    for i in range(pieces):
        group = slice(i * here, (i + 1) * here)
        at = slice(i * count, (i + 1) * count)
        code = got_ref[group, parts * cap : parts * cap + 8, :].astype(F32)
        code = jnp.broadcast_to(code[:, 0:1, :], (here, cap, LANES)).reshape(count, LANES)
        slot = mm(jnp.where(mine, code, 0.0).astype(BF16), digit).astype(jnp.int32) - 1
        sel = jnp.concatenate(
            [one_hot(slot == lane + r * LANES) for r in range(slots // LANES)], axis=1
        )
        sel_ref[at, :] = sel
        predicted = mm(sel, high_ref[...], contract) + mm(sel, low_ref[...], contract)
        for part in range(parts):
            cols = slice(part * LANES, (part + 1) * LANES)
            seen = got_ref[group, part * cap : (part + 1) * cap, :]
            seen = seen.astype(F32).reshape(count, LANES)
            own_ref[at, cols] = (predicted[:, cols] - seen).astype(BF16)
        save = pltpu.make_async_copy(own_ref.at[at, :], res_hbm.at[at, :], sems.at[i])
        save.start()
        saves.append(save)
    for save in saves:
        save.wait()


def window(index, count, cols):
    part = cols // count
    width = min(cols, part + (LANES if count == 2 else 2 * LANES))
    return jnp.clip(index * part - LANES, 0, cols - width), width


def inverse_kernel(
    count,
    res_ref,
    sel_ref,
    row_ref,
    twist_ref,
    mat_ref,
    sky_hbm,
    beam_hbm,
    keep_ref,
    *rest,
):
    send_refs = rest[: count - 1]
    sky_ref, beam_ref, lines_ref, shift_ref, grid_ref, sems = rest[count - 1 :]
    rows, cols = beam_ref.shape
    outer = cols // LANES
    me = lax.axis_index("freq")
    start, width = window(me, count, cols)
    sky_part = sky_hbm.at[:, pl.ds(pl.multiple_of(start, LANES), width)]
    loads = [
        pltpu.make_async_copy(beam_hbm, beam_ref, sems.at[0]),
        pltpu.make_async_copy(sky_part, sky_ref, sems.at[1]),
    ]
    for load in loads:
        load.start()
    grid = mm(res_ref[...], sel_ref[...], ((0,), (0,)))
    for r in range(rows // S):
        grid_ref[r] = grid[:, r * LANES : (r + 1) * LANES]
    blocks = []
    for w in range(outer):
        blocks.append(
            jnp.concatenate(
                [
                    jnp.concatenate(
                        [
                            grid_ref[r, pl.ds(e * S * S + w, S, stride=S), :]
                            for e in range(2)
                        ],
                        axis=1,
                    )
                    for r in range(rows // S)
                ],
                axis=0,
            )
        )
    cells = jnp.concatenate(blocks, axis=0).astype(BF16)
    mid = mm(jnp.concatenate([cells, cells], axis=1), mat_ref[...].reshape(4 * LANES, 2 * LANES))
    lines = []
    for w in range(outer):
        re = mid[w * rows : (w + 1) * rows, :LANES]
        im = mid[w * rows : (w + 1) * rows, LANES:]
        tr, ti = twist_ref[0, w : w + 1, :], twist_ref[1, w : w + 1, :]
        lines.append((re * tr - im * ti, re * ti + im * tr))
    spread = dft16(lines, 1)
    for i, pair in enumerate(spread):
        for e in range(2):
            line = pair[e].astype(BF16)
            lines_ref[e * rows : (e + 1) * rows, i * LANES : (i + 1) * LANES] = line
            lines_ref[(2 + e) * rows : (3 + e) * rows, i * LANES : (i + 1) * LANES] = line
    back = mm(row_ref[...], lines_ref[...])
    for load in loads:
        load.wait()
    shift_ref[...] = back * beam_ref[...] * (-STEP)
    for d in range(count):
        start, width = window(lax.rem(me + d, count), count, cols)
        at = pl.ds(pl.multiple_of(start, LANES), width)
        if d == 0:
            keep_ref[...] = shift_ref[:, at] + sky_ref[...]
        else:
            send_refs[d - 1][...] = shift_ref[:, at].astype(BF16)


def sum_kernel(keep_ref, *refs):
    main_ref, near_ref, far_ref = refs[-3:]
    rows = keep_ref.shape[0]
    main = keep_ref[...]
    for ref in refs[:-3]:
        main = main + ref[...].astype(F32)
    main_ref[...] = main
    even = (lax.axis_index("facet") & 1) == 0
    top, bottom = main[0:2], main[rows - 2 : rows]
    near_ref[...] = jnp.where(even, bottom, top)
    far_ref[...] = jnp.where(even, top, bottom)


def prepare(first_ref, bias_ref, second_ref, one_ref, two_ref):
    hidden = first_ref.shape[2]
    depth = one_ref.shape[1]
    full = (BAND + 2) * 9
    bias_high, bias_low = split(bias_ref[...])
    line = iota((8, depth), 0)
    lane = iota((8, depth), 1)
    group = lane * 2731 >> 16
    term = group * 86 >> 8
    col = group - term * 3
    taps = one_hot(((line == col) & (term < 2)) | ((line - 3 == col) & (term == 2)))
    ends = one_hot(((line == 6) & (lane == full)) | ((line == 7) & (lane == full + 1)))
    values = []
    for a in range(3):
        high, low = split(first_ref[a])
        pieces = [high, low, bias_high, bias_low]
        weights = jnp.concatenate([p.astype(F32) for p in pieces], axis=0).astype(BF16)
        values.append(mm(weights, taps, ((0,), (0,))))
        if a == 0:
            offset = mm(weights, ends, ((0,), (0,)))
    lane = iota((hidden, depth), 1)
    yin = lane - (lane * 2731 >> 16) * (BAND + 2)
    for y in range(BAND):
        block = offset
        for a in range(3):
            block = block + jnp.where(yin == y + a, values[a], 0.0)
        one_ref[y * hidden : (y + 1) * hidden, :] = block.astype(BF16)

    wide = two_ref.shape[1]
    tall = BAND + 2
    expand = one_hot(iota((hidden, wide), 0) == (iota((hidden, wide), 1) & (hidden - 1)))
    pieces = [split(second_ref[a]) for a in range(3)]
    gap = iota((tall, wide), 1) // hidden + 2 - iota((tall, wide), 0)
    blocks = []
    for half in range(2):
        lines = [mm(pieces[a][half], expand) for a in range(3)]
        for b in range(3):
            total = jnp.zeros((tall, wide), F32)
            for a in range(3):
                total = jnp.where(gap == a, lines[a][b : b + 1, :], total)
            blocks.append(total)
    two_ref[...] = jnp.concatenate(blocks, axis=0).astype(BF16)


def moved(value):
    width = value.shape[1]
    lane = iota(value.shape, 1)
    return (
        jnp.where(lane == 0, 0.0, pltpu.roll(value, 1, 1)),
        jnp.where(lane == width - 1, 0.0, pltpu.roll(value, width - 1, 1)),
    )


def stack_of(band):
    ones = jnp.where(iota((8, band.shape[1]), 0) < 2, 1.0, 0.0)
    high = band.astype(BF16).astype(F32)
    shifted = []
    for value in (high, band - high):
        left, right = moved(value)
        shifted.append([left, value, right])
    return jnp.concatenate(shifted[0] + shifted[1] + shifted[0] + [ones], axis=0).astype(BF16)


def share_of(taps):
    tall = BAND + 2
    parts = [
        taps[b * tall : (b + 1) * tall] + taps[(3 + b) * tall : (4 + b) * tall] for b in range(3)
    ]
    return parts[1] + moved(parts[0])[0] + moved(parts[2])[1]


def prior_kernel(main_ref, near_ref, one_ref, two_ref, sum_ref, base_ref):
    rows, width = main_ref.shape
    tall = BAND + 2
    pair = 2 * one_ref.shape[0] // BAND
    main, near = main_ref[...], near_ref[...]
    even = (lax.axis_index("facet") & 1) == 0
    base_ref[8 : rows + 8, :] = main
    base_ref[6:8, :] = jnp.where(even, 0.0, near)
    base_ref[rows + 8 : rows + 10, :] = jnp.where(even, near, 0.0)
    sum_ref[0:8, :] = jnp.zeros((8, width), F32)
    sum_ref[8 : rows + 8, :] = main
    sum_ref[rows + 8 :, :] = jnp.zeros((8, width), F32)
    spots = [slice(k * BAND + 6, k * BAND + 6 + tall) for k in range((rows + 2) // BAND)]
    stack = jnp.concatenate([stack_of(base_ref[spot, :]) for spot in spots], axis=1)
    hidden = jnp.maximum(mm(one_ref[...], stack), 0.0)
    head, body, foot = hidden[:pair], hidden[pair:-pair], hidden[-pair:]
    head = jnp.concatenate([jnp.where(even, 0.0, head[:, :width]), head[:, width:]], axis=1)
    foot = jnp.concatenate([foot[:, :-width], jnp.where(even, foot[:, -width:], 0.0)], axis=1)
    hidden = jnp.concatenate([head, body, foot], axis=0).astype(BF16)
    taps = mm(two_ref[...], hidden)
    for k, spot in enumerate(spots):
        sum_ref[spot, :] = sum_ref[spot, :] + share_of(taps[:, k * width : (k + 1) * width])


def edge_kernel(
    count,
    part,
    sum_ref,
    main_ref,
    far_ref,
    one_ref,
    two_ref,
    place_ref,
    back_ref,
    out_hbm,
    tiles_hbm,
    base_ref,
    share_ref,
    last_ref,
    tiles_ref,
    sems,
):
    rows, width = main_ref.shape
    tall = BAND + 2
    height = one_ref.shape[0]
    inner = height // BAND
    pair = 2 * inner
    place = lax.axis_index("facet")
    final = lax.axis_size("facet") - 1
    even = (place & 1) == 0
    me = lax.axis_index("freq")
    start, _ = window(me, count, part * count)
    at = pl.ds(pl.multiple_of(me * part - start, LANES), part)
    done = rows - 8
    first = pl.multiple_of(jnp.where(even, 8, 0), 8)
    early = pltpu.make_async_copy(
        sum_ref.at[pl.ds(pl.multiple_of(first + 8, 8), done), at],
        out_hbm.at[pl.ds(first, done), :],
        sems.at[0],
    )
    early.start()
    tiles_ref[...] = mm(place_ref[...], back_ref[...]).astype(BF16)
    tiles = pltpu.make_async_copy(tiles_ref, tiles_hbm, sems.at[2])
    tiles.start()
    far = far_ref[...]
    base_ref[0:2, :] = far
    base_ref[2:tall, :] = main_ref[0:BAND, :]
    base_ref[32 : 32 + BAND, :] = main_ref[rows - BAND : rows, :]
    base_ref[32 + BAND : 32 + tall, :] = far
    band = jnp.where(even, base_ref[0:tall, :], base_ref[32 : 32 + tall, :])
    table = one_ref[pl.ds(pl.multiple_of(jnp.where(even, 0, height - pair), 16), pair), :]
    hidden = jnp.maximum(mm(table, stack_of(band)), 0.0)
    hidden = jnp.concatenate(
        [
            jnp.where(place == 0, 0.0, hidden[:inner]),
            jnp.where(place == final, 0.0, hidden[inner:]),
        ],
        axis=0,
    )
    second = jnp.where(
        even, two_ref[:, :pair].astype(F32), two_ref[:, height - pair :].astype(F32)
    )
    share_ref[0:8, :] = jnp.zeros((8, width), F32)
    share_ref[8 : tall + 8, :] = share_of(mm(second.astype(BF16), hidden.astype(BF16)))
    near_sum = jnp.where(even, sum_ref[8:16, :], sum_ref[rows : rows + 8, :])
    share = jnp.where(even, share_ref[10:18, :], share_ref[tall - 2 : tall + 6, :])
    last_ref[...] = near_sum + share
    late = pltpu.make_async_copy(
        last_ref.at[:, at],
        out_hbm.at[pl.ds(pl.multiple_of(jnp.where(even, 0, done), 8), 8), :],
        sems.at[1],
    )
    late.start()
    early.wait()
    tiles.wait()
    late.wait()


def shape(dims, dtype):
    return jax.ShapeDtypeStruct(dims, dtype)


def call(kernel, out_shape, flops, scratch=(), loaded=(), saved=(), limit=16):
    near = pl.BlockSpec(memory_space=pltpu.VMEM)
    far = pl.BlockSpec(memory_space=pltpu.HBM)

    def run(*args):
        return pl.pallas_call(
            kernel,
            out_shape=out_shape,
            in_specs=[far if i in loaded else near for i in range(len(args))],
            out_specs=[far if i in saved else near for i in range(len(out_shape))]
            if isinstance(out_shape, list)
            else near,
            scratch_shapes=scratch,
            compiler_params=pltpu.CompilerParams(vmem_limit_bytes=limit << 20),
            cost_estimate=pl.CostEstimate(flops=flops, bytes_accessed=4 << 20, transcendentals=0),
        )(*args)

    return run


def on_device(sky, beam, observed, facet_of, tile_slot, conv_first, bias_first, conv_second):
    rows, cols = sky.shape
    beam = beam.reshape(rows, cols)
    facets = lax.axis_size("facet")
    count = lax.axis_size("freq")
    tiles, width = observed.shape
    cap = 2 * tiles // facets
    total = facets * cap
    slots = (rows // S) * (cols // S)
    hidden = conv_first.shape[0]
    row_f, twist_f, mat_f = tables(rows, cols, -1)
    row_b, twist_b, mat_b = tables(rows, cols, 1)

    deep = (width // LANES) * cap + 8
    send, dest = call(
        functools.partial(pack_kernel, facets, cap),
        [shape((facets, deep, LANES), BF16), shape((1, tiles), jnp.int32)],
        1 << 28,
        scratch=[
            pltpu.VMEM((1, tiles), jnp.int32),
            pltpu.VMEM((1, tiles), jnp.int32),
            pltpu.VMEM((tiles, width), BF16),
            pltpu.VMEM((facets, deep, LANES), BF16),
            pltpu.SemaphoreType.DMA((7,)),
        ],
        loaded=(0, 1, 2),
        saved=(0,),
    )(
        *(
            pltpu.with_memory_space_constraint(value, pltpu.HBM)
            for value in (facet_of.reshape(1, tiles), tile_slot.reshape(1, tiles), observed)
        )
    )
    got = lax.all_to_all(send, "facet", split_axis=0, concat_axis=0, tiled=True)

    high, low, first, second, placed = call(
        forward_kernel,
        [
            shape((width, slots), BF16),
            shape((width, slots), BF16),
            shape((hidden * BAND, 9 * (BAND + 2) + 8), BF16),
            shape((6 * (BAND + 2), hidden * BAND), BF16),
            shape((tiles, total), BF16),
        ],
        1 << 30,
        scratch=[pltpu.VMEM((2, width, slots), BF16)],
    )(
        sky,
        beam,
        row_f,
        twist_f,
        mat_f,
        conv_first.transpose(1, 2, 0),
        bias_first.reshape(1, hidden),
        conv_second.transpose(1, 2, 0),
        dest,
    )

    residual, select, own = call(
        functools.partial(residual_kernel, facets, cap),
        [shape((total, width), BF16), shape((total, slots), BF16), shape((total, width), BF16)],
        1 << 30,
        scratch=[pltpu.SemaphoreType.DMA((2,))],
        saved=(0,),
    )(got, *(pltpu.with_memory_space_constraint(value, pltpu.VMEM) for value in (high, low)))
    returned = lax.all_to_all(
        residual.reshape(facets, cap, width), "facet", split_axis=0, concat_axis=0, tiled=True
    ).reshape(total, width)

    _, wide = window(0, count, cols)
    keep, *sends = call(
        functools.partial(inverse_kernel, count),
        [shape((rows, wide), F32)] + [shape((rows, wide), BF16)] * (count - 1),
        1 << 30,
        scratch=[
            pltpu.VMEM((rows, wide), F32),
            pltpu.VMEM((rows, cols), F32),
            pltpu.VMEM((4 * rows, cols), BF16),
            pltpu.VMEM((rows, cols), F32),
            pltpu.VMEM((rows // S, width, LANES), F32),
            pltpu.SemaphoreType.DMA((2,)),
        ],
        loaded=(5, 6),
    )(
        own,
        select,
        row_b,
        twist_b,
        mat_b,
        *(pltpu.with_memory_space_constraint(value, pltpu.HBM) for value in (sky, beam)),
    )

    def beside(value, to):
        pairs = [(p, to(p)) for p in range(facets) if 0 <= to(p) < facets]
        return lax.ppermute(value, "facet", pairs)

    gots = [
        lax.ppermute(value, "freq", [(f, (f + d + 1) % count) for f in range(count)])
        for d, value in enumerate(sends)
    ]
    main, near, far = call(
        sum_kernel,
        [shape((rows, wide), F32), shape((2, wide), F32), shape((2, wide), F32)],
        1 << 24,
    )(keep, *gots)
    far = beside(far, lambda p: p + 1 if p & 1 else p - 1)
    near = beside(near, lambda p: p ^ 1)
    tall_rows = pltpu.VMEM((rows + 16, wide), F32)
    partial = call(
        prior_kernel, shape((rows + 16, wide), F32), 1 << 31, scratch=[tall_rows], limit=32
    )(main, near, first, second)
    image, tiles_out = call(
        functools.partial(edge_kernel, count, cols // count),
        [shape((rows, cols // count), F32), shape((tiles, width), BF16)],
        1 << 30,
        scratch=[
            pltpu.VMEM((64, wide), F32),
            pltpu.VMEM((BAND + 10, wide), F32),
            pltpu.VMEM((8, wide), F32),
            pltpu.VMEM((tiles, width), BF16),
            pltpu.SemaphoreType.DMA((3,)),
        ],
        saved=(0, 1),
    )(partial, main, far, first, second, placed, returned)
    return tiles_out, image


def solution(mesh):
    placed = (
        P("facet", None),
        P("freq", "facet", None),
        P(("freq", "facet"), None),
        P(("freq", "facet")),
        P(("freq", "facet")),
        P(),
        P(),
        P(),
    )

    return jax.shard_map(
        on_device,
        mesh=mesh,
        in_specs=placed,
        out_specs=(P(("freq", "facet"), None), P("facet", "freq")),
        check_vma=False,
    )
```

```python
import functools
import math

import jax
import jax.numpy as jnp
import numpy as np
from jax import lax
from jax.experimental import pallas as pl
from jax.experimental.pallas import tpu as pltpu
from jax.sharding import PartitionSpec as P


S = 16
LANES = 128
BAND = 22
STEP = 0.5
F32 = jnp.float32
BF16 = jnp.bfloat16


def iota(shape, dim):
    return lax.broadcasted_iota(jnp.int32, shape, dim)


def mm(a, b, dims=((1,), (0,))):
    return lax.dot_general(a, b, (dims, ((), ())), preferred_element_type=F32)


def one_hot(cond):
    return jnp.where(cond, 1.0, 0.0).astype(BF16)


def split(x):
    high = x.astype(BF16)
    return high, (x - high.astype(F32)).astype(BF16)


def np_split(x):
    x = np.asarray(x, np.float32)
    high = x.astype(BF16)
    return high, (x - high.astype(np.float32)).astype(BF16)


def tables(rows, cols, sign):
    outer = cols // LANES
    scale = 1.0 / math.sqrt(rows * cols)
    k = np.arange(rows)
    angle = sign * 2.0 * np.pi * ((k[:, None] * k[None, :]) % rows) / rows
    cos_r, sin_r = np.cos(angle) * scale, np.sin(angle) * scale
    if sign < 0:
        row_high, row_low = np_split(np.concatenate([cos_r, sin_r], 0))
        row = np.concatenate([row_high, row_high, row_low], 1)
    else:
        row = np.concatenate(np_split(np.concatenate([cos_r, -sin_r], 1)), 1)
    i2 = np.arange(LANES)
    w = np.arange(outer)
    twist = sign * 2.0 * np.pi * ((w[:, None] * i2[None, :]) % cols) / cols
    inner = sign * 2.0 * np.pi * ((i2[:, None] * i2[None, :]) % LANES) / LANES
    c, s = np.cos(inner), np.sin(inner)
    mat_high, mat_low = np_split(np.block([[c, s], [-s, c]]))
    return (
        row,
        np.stack([np.cos(twist), np.sin(twist)]).astype(np.float32),
        np.stack([mat_high, mat_low]),
    )


def times_i(z, sign):
    re, im = z
    return (-im, re) if sign > 0 else (im, -re)


def add(a, b):
    return (a[0] + b[0], a[1] + b[1])


def sub(a, b):
    return (a[0] - b[0], a[1] - b[1])


def dft4(x, sign):
    s0, s1 = add(x[0], x[2]), sub(x[0], x[2])
    s2, s3 = add(x[1], x[3]), times_i(sub(x[1], x[3]), sign)
    return [add(s0, s2), add(s1, s3), sub(s0, s2), sub(s1, s3)]


def dft16(x, sign):
    mid = [dft4([x[4 * a + b] for a in range(4)], sign) for b in range(4)]
    out = [None] * 16
    for c in range(4):
        turned = []
        for b in range(4):
            re, im = mid[b][c]
            phase = (b * c) % 16
            if phase == 0:
                turned.append((re, im))
            elif phase == 4:
                turned.append(times_i((re, im), sign))
            else:
                wr = math.cos(2.0 * math.pi * phase / 16)
                wi = sign * math.sin(2.0 * math.pi * phase / 16)
                turned.append((re * wr - im * wi, re * wi + im * wr))
        for d, value in enumerate(dft4(turned, sign)):
            out[c + 4 * d] = value
    return out


def swap_matrix(size):
    src = iota((1, size), 1)
    swapped = (src & -256) | ((src & 15) << 4) | ((src >> 4) & 15)
    return one_hot(iota((size, size), 0) == swapped)


def pack_kernel(
    facets,
    cap,
    facet_hbm,
    slot_hbm,
    seen_hbm,
    send_hbm,
    dest_ref,
    facet_ref,
    slot_ref,
    seen_ref,
    send_ref,
    sems,
):
    tiles, width = seen_ref.shape
    total = facets * cap
    loads = [
        pltpu.make_async_copy(src, dst, sems.at[i])
        for i, (src, dst) in enumerate(
            ((facet_hbm, facet_ref), (slot_hbm, slot_ref), (seen_hbm, seen_ref))
        )
    ]
    for load in loads:
        load.start()
    before = one_hot(iota((tiles, tiles), 0) < iota((tiles, tiles), 1))
    loads[0].wait()
    facet = facet_ref[...]
    member = iota((facets, tiles), 0) == facet
    member_f = jnp.where(member, 1.0, 0.0)
    ranks = mm(member_f.astype(BF16), before)
    rank = jnp.sum(member_f * ranks, axis=0, keepdims=True).astype(jnp.int32)
    dest = facet * cap + rank
    dest_ref[...] = dest
    loads[1].wait()
    code = slot_ref[...] + 1
    lane = iota((LANES, tiles), 0)
    slots = mm(
        (member_f * (code >> 4).astype(F32)).astype(BF16), one_hot(lane == rank), ((1,), (1,))
    ) + mm(
        (member_f * (code & 15).astype(F32)).astype(BF16),
        one_hot(lane - LANES // 2 == rank),
        ((1,), (1,)),
    )
    parts = width // LANES
    groups = 4
    here = facets // groups
    loads[2].wait()
    saves = []
    for g in range(groups):
        placing = one_hot(iota((total // groups, tiles), 0) + g * (total // groups) == dest)
        packed = mm(placing, seen_ref[...]).astype(BF16)
        for i in range(here):
            d = g * here + i
            for part in range(parts):
                send_ref[d, part * cap : (part + 1) * cap, :] = packed[
                    i * cap : (i + 1) * cap, part * LANES : (part + 1) * LANES
                ]
            send_ref[d, parts * cap : parts * cap + 8, :] = jnp.broadcast_to(
                slots[d : d + 1, :], (8, LANES)
            ).astype(BF16)
        span = pl.ds(g * here, here)
        save = pltpu.make_async_copy(send_ref.at[span], send_hbm.at[span], sems.at[3 + g])
        save.start()
        saves.append(save)
    for save in saves:
        save.wait()


def forward_kernel(
    sky_ref,
    beam_ref,
    row_ref,
    twist_ref,
    mat_ref,
    first_ref,
    bias_ref,
    second_ref,
    dest_ref,
    high_ref,
    low_ref,
    one_ref,
    two_ref,
    place_ref,
    edge_one_ref,
    edge_two_ref,
    part_ref,
):
    spots = iota(place_ref.shape[::-1], 0)
    place_ref[...] = jnp.where(spots == dest_ref[...], 1.0, 0.0).T.astype(BF16)
    prepare(first_ref, bias_ref, second_ref, one_ref, two_ref)
    pair, narrow = edge_one_ref.shape
    height, depth = one_ref.shape
    even = (lax.axis_index("facet") & 1) == 0
    table = jnp.where(
        even, one_ref[:pair, :].astype(F32), one_ref[height - pair :, :].astype(F32)
    ).astype(BF16)
    lane = iota((depth, narrow), 1)
    column = (lane >> 3) * (BAND + 2) + (lane & 7)
    column = column + jnp.where(even | (lane >= narrow - 8), 0, BAND - 6)
    edge_one_ref[...] = mm(table, one_hot(iota((depth, narrow), 0) == column)).astype(BF16)
    edge_two_ref[...] = jnp.where(
        even, two_ref[:, :pair].astype(F32), two_ref[:, height - pair :].astype(F32)
    ).astype(BF16)
    rows, cols = sky_ref.shape
    outer = cols // LANES
    weighted = sky_ref[...] * beam_ref[...]
    w_high, w_low = split(weighted)
    mid = mm(row_ref[...], jnp.concatenate([w_high, w_low, w_high], axis=0))
    lines = [
        (
            mid[:rows, i * LANES : (i + 1) * LANES],
            mid[rows:, i * LANES : (i + 1) * LANES],
        )
        for i in range(outer)
    ]
    spread = dft16(lines, -1)
    blocks = []
    for w in range(outer):
        re, im = spread[w]
        tr, ti = twist_ref[0, w : w + 1, :], twist_ref[1, w : w + 1, :]
        blocks.append(jnp.concatenate([re * tr - im * ti, re * ti + im * tr], axis=1))
    high, low = split(jnp.concatenate(blocks, axis=0))
    mat_high, mat_low = mat_ref[0], mat_ref[1]
    model = mm(high, mat_high) + mm(low, mat_high) + mm(high, mat_low)
    for w in range(outer):
        for r in range(rows // S):
            for e in range(2):
                piece = model[
                    w * rows + r * S : w * rows + (r + 1) * S, e * LANES : (e + 1) * LANES
                ]
                piece_high, piece_low = split(piece)
                at = (pl.ds(e * 256 + w * S, S), pl.ds(r * LANES, LANES))
                part_ref[(0,) + at] = piece_high
                part_ref[(1,) + at] = piece_low
    swap = swap_matrix(high_ref.shape[0])
    high_ref[...] = mm(swap, part_ref[0]).astype(BF16)
    low_ref[...] = mm(swap, part_ref[1]).astype(BF16)


def residual_kernel(facets, cap, got_ref, high_ref, low_ref, res_hbm, sel_ref, own_ref, sems):
    slots = high_ref.shape[1]
    parts = high_ref.shape[0] // LANES
    pieces = sems.shape[0]
    here = facets // pieces
    count = here * cap
    contract = ((1,), (1,))
    lane = iota((count, LANES), 1)
    rank = iota((count, LANES), 0) % cap
    mine = (lane & (LANES // 2 - 1)) == rank
    digit = jnp.where(iota((LANES, LANES), 0) < LANES // 2, 16.0, 1.0).astype(BF16)
    saves = []
    for i in range(pieces):
        group = slice(i * here, (i + 1) * here)
        at = slice(i * count, (i + 1) * count)
        code = got_ref[group, parts * cap : parts * cap + 8, :].astype(F32)
        code = jnp.broadcast_to(code[:, 0:1, :], (here, cap, LANES)).reshape(count, LANES)
        slot = mm(jnp.where(mine, code, 0.0).astype(BF16), digit).astype(jnp.int32) - 1
        sel = jnp.concatenate(
            [one_hot(slot == lane + r * LANES) for r in range(slots // LANES)], axis=1
        )
        sel_ref[at, :] = sel
        predicted = mm(sel, high_ref[...], contract) + mm(sel, low_ref[...], contract)
        for part in range(parts):
            cols = slice(part * LANES, (part + 1) * LANES)
            seen = got_ref[group, part * cap : (part + 1) * cap, :]
            seen = seen.astype(F32).reshape(count, LANES)
            own_ref[at, cols] = (predicted[:, cols] - seen).astype(BF16)
        save = pltpu.make_async_copy(own_ref.at[at, :], res_hbm.at[at, :], sems.at[i])
        save.start()
        saves.append(save)
    for save in saves:
        save.wait()


def window(index, count, cols):
    part = cols // count
    width = min(cols, part + (LANES if count == 2 else 2 * LANES))
    return jnp.clip(index * part - LANES, 0, cols - width), width


def inverse_kernel(
    count,
    res_ref,
    sel_ref,
    row_ref,
    twist_ref,
    mat_ref,
    sky_hbm,
    beam_hbm,
    keep_ref,
    *rest,
):
    send_refs = rest[: count - 1]
    sky_ref, beam_ref, lines_ref, shift_ref, grid_ref, sems = rest[count - 1 :]
    rows, cols = beam_ref.shape
    outer = cols // LANES
    me = lax.axis_index("freq")
    start, width = window(me, count, cols)
    sky_part = sky_hbm.at[:, pl.ds(pl.multiple_of(start, LANES), width)]
    loads = [
        pltpu.make_async_copy(beam_hbm, beam_ref, sems.at[0]),
        pltpu.make_async_copy(sky_part, sky_ref, sems.at[1]),
    ]
    for load in loads:
        load.start()
    grid = mm(res_ref[...], sel_ref[...], ((0,), (0,)))
    for r in range(rows // S):
        grid_ref[r] = grid[:, r * LANES : (r + 1) * LANES]
    blocks = []
    for w in range(outer):
        blocks.append(
            jnp.concatenate(
                [
                    jnp.concatenate(
                        [
                            grid_ref[r, pl.ds(e * S * S + w, S, stride=S), :]
                            for e in range(2)
                        ],
                        axis=1,
                    )
                    for r in range(rows // S)
                ],
                axis=0,
            )
        )
    cells = jnp.concatenate(blocks, axis=0).astype(BF16)
    mid = mm(jnp.concatenate([cells, cells], axis=1), mat_ref[...].reshape(4 * LANES, 2 * LANES))
    lines = []
    for w in range(outer):
        re = mid[w * rows : (w + 1) * rows, :LANES]
        im = mid[w * rows : (w + 1) * rows, LANES:]
        tr, ti = twist_ref[0, w : w + 1, :], twist_ref[1, w : w + 1, :]
        lines.append((re * tr - im * ti, re * ti + im * tr))
    spread = dft16(lines, 1)
    for i, pair in enumerate(spread):
        for e in range(2):
            line = pair[e].astype(BF16)
            lines_ref[e * rows : (e + 1) * rows, i * LANES : (i + 1) * LANES] = line
            lines_ref[(2 + e) * rows : (3 + e) * rows, i * LANES : (i + 1) * LANES] = line
    back = mm(row_ref[...], lines_ref[...])
    for load in loads:
        load.wait()
    shift_ref[...] = back * beam_ref[...] * (-STEP)
    for d in range(count):
        start, width = window(lax.rem(me + d, count), count, cols)
        at = pl.ds(pl.multiple_of(start, LANES), width)
        if d == 0:
            keep_ref[...] = shift_ref[:, at] + sky_ref[...]
        else:
            send_refs[d - 1][...] = shift_ref[:, at].astype(BF16)


def sum_kernel(keep_ref, *refs):
    main_ref, near_ref, far_ref = refs[-3:]
    rows = keep_ref.shape[0]
    main = keep_ref[...]
    for ref in refs[:-3]:
        main = main + ref[...].astype(F32)
    main_ref[...] = main
    even = (lax.axis_index("facet") & 1) == 0
    top, bottom = main[0:2], main[rows - 2 : rows]
    near_ref[...] = jnp.where(even, bottom, top)
    far_ref[...] = jnp.where(even, top, bottom)


def prepare(first_ref, bias_ref, second_ref, one_ref, two_ref):
    hidden = first_ref.shape[2]
    depth = one_ref.shape[1]
    full = (BAND + 2) * 9
    bias_high, bias_low = split(bias_ref[...])
    line = iota((8, depth), 0)
    lane = iota((8, depth), 1)
    group = lane * 2731 >> 16
    term = group * 86 >> 8
    col = group - term * 3
    taps = one_hot(((line == col) & (term < 2)) | ((line - 3 == col) & (term == 2)))
    ends = one_hot(((line == 6) & (lane == full)) | ((line == 7) & (lane == full + 1)))
    values = []
    for a in range(3):
        high, low = split(first_ref[a])
        pieces = [high, low, bias_high, bias_low]
        weights = jnp.concatenate([p.astype(F32) for p in pieces], axis=0).astype(BF16)
        values.append(mm(weights, taps, ((0,), (0,))))
        if a == 0:
            offset = mm(weights, ends, ((0,), (0,)))
    lane = iota((hidden, depth), 1)
    yin = lane - (lane * 2731 >> 16) * (BAND + 2)
    for y in range(BAND):
        block = offset
        for a in range(3):
            block = block + jnp.where(yin == y + a, values[a], 0.0)
        one_ref[y * hidden : (y + 1) * hidden, :] = block.astype(BF16)

    wide = two_ref.shape[1]
    tall = BAND + 2
    expand = one_hot(iota((hidden, wide), 0) == (iota((hidden, wide), 1) & (hidden - 1)))
    pieces = [split(second_ref[a]) for a in range(3)]
    gap = iota((tall, wide), 1) // hidden + 2 - iota((tall, wide), 0)
    blocks = []
    for half in range(2):
        lines = [mm(pieces[a][half], expand) for a in range(3)]
        for b in range(3):
            total = jnp.zeros((tall, wide), F32)
            for a in range(3):
                total = jnp.where(gap == a, lines[a][b : b + 1, :], total)
            blocks.append(total)
    two_ref[...] = jnp.concatenate(blocks, axis=0).astype(BF16)


def moved(value):
    width = value.shape[1]
    lane = iota(value.shape, 1)
    return (
        jnp.where(lane == 0, 0.0, pltpu.roll(value, 1, 1)),
        jnp.where(lane == width - 1, 0.0, pltpu.roll(value, width - 1, 1)),
    )


def stack_of(band):
    ones = jnp.where(iota((8, band.shape[1]), 0) < 2, 1.0, 0.0)
    high = band.astype(BF16).astype(F32)
    shifted = []
    for value in (high, band - high):
        left, right = moved(value)
        shifted.append([left, value, right])
    return jnp.concatenate(shifted[0] + shifted[1] + shifted[0] + [ones], axis=0).astype(BF16)


def share_of(taps):
    tall = BAND + 2
    parts = [
        taps[b * tall : (b + 1) * tall] + taps[(3 + b) * tall : (4 + b) * tall] for b in range(3)
    ]
    return parts[1] + moved(parts[0])[0] + moved(parts[2])[1]


def prior_kernel(main_ref, near_ref, one_ref, two_ref, sum_ref, base_ref):
    rows, width = main_ref.shape
    tall = BAND + 2
    pair = 2 * one_ref.shape[0] // BAND
    main, near = main_ref[...], near_ref[...]
    even = (lax.axis_index("facet") & 1) == 0
    base_ref[8 : rows + 8, :] = main
    base_ref[6:8, :] = jnp.where(even, 0.0, near)
    base_ref[rows + 8 : rows + 10, :] = jnp.where(even, near, 0.0)
    sum_ref[0:8, :] = jnp.zeros((8, width), F32)
    sum_ref[8 : rows + 8, :] = main
    sum_ref[rows + 8 :, :] = jnp.zeros((8, width), F32)
    spots = [slice(k * BAND + 6, k * BAND + 6 + tall) for k in range((rows + 2) // BAND)]
    stack = jnp.concatenate([stack_of(base_ref[spot, :]) for spot in spots], axis=1)
    hidden = jnp.maximum(mm(one_ref[...], stack), 0.0)
    head, body, foot = hidden[:pair], hidden[pair:-pair], hidden[-pair:]
    head = jnp.concatenate([jnp.where(even, 0.0, head[:, :width]), head[:, width:]], axis=1)
    foot = jnp.concatenate([foot[:, :-width], jnp.where(even, foot[:, -width:], 0.0)], axis=1)
    hidden = jnp.concatenate([head, body, foot], axis=0).astype(BF16)
    taps = mm(two_ref[...], hidden)
    for k, spot in enumerate(spots):
        sum_ref[spot, :] = sum_ref[spot, :] + share_of(taps[:, k * width : (k + 1) * width])


def edge_kernel(
    count,
    part,
    sum_ref,
    main_ref,
    far_ref,
    one_ref,
    two_ref,
    place_ref,
    back_ref,
    out_hbm,
    tiles_hbm,
    base_ref,
    share_ref,
    last_ref,
    tiles_ref,
    sems,
):
    rows, width = main_ref.shape
    tall = BAND + 2
    inner = one_ref.shape[0] // 2
    place = lax.axis_index("facet")
    final = lax.axis_size("facet") - 1
    even = (place & 1) == 0
    me = lax.axis_index("freq")
    start, _ = window(me, count, part * count)
    at = pl.ds(pl.multiple_of(me * part - start, LANES), part)
    done = rows - 8
    first = pl.multiple_of(jnp.where(even, 8, 0), 8)
    early = pltpu.make_async_copy(
        sum_ref.at[pl.ds(pl.multiple_of(first + 8, 8), done), at],
        out_hbm.at[pl.ds(first, done), :],
        sems.at[0],
    )
    early.start()
    tiles_ref[...] = mm(place_ref[...], back_ref[...]).astype(BF16)
    tiles = pltpu.make_async_copy(tiles_ref, tiles_hbm, sems.at[2])
    tiles.start()
    far = far_ref[...]
    base_ref[0:2, :] = far
    base_ref[2:8, :] = main_ref[0:6, :]
    base_ref[8:14, :] = main_ref[rows - 6 : rows, :]
    base_ref[14:16, :] = far
    band = jnp.where(even, base_ref[0:8, :], base_ref[8:16, :])
    hidden = jnp.maximum(mm(one_ref[...], stack_of(band)), 0.0)
    hidden = jnp.concatenate(
        [
            jnp.where(place == 0, 0.0, hidden[:inner]),
            jnp.where(place == final, 0.0, hidden[inner:]),
        ],
        axis=0,
    )
    share_ref[0:8, :] = jnp.zeros((8, width), F32)
    share_ref[8 : tall + 8, :] = share_of(mm(two_ref[...], hidden.astype(BF16)))
    near_sum = jnp.where(even, sum_ref[8:16, :], sum_ref[rows : rows + 8, :])
    share = jnp.where(even, share_ref[10:18, :], share_ref[tall - 2 : tall + 6, :])
    last_ref[...] = near_sum + share
    late = pltpu.make_async_copy(
        last_ref.at[:, at],
        out_hbm.at[pl.ds(pl.multiple_of(jnp.where(even, 0, done), 8), 8), :],
        sems.at[1],
    )
    late.start()
    early.wait()
    tiles.wait()
    late.wait()


def shape(dims, dtype):
    return jax.ShapeDtypeStruct(dims, dtype)


def call(kernel, out_shape, flops, scratch=(), loaded=(), saved=(), limit=16):
    near = pl.BlockSpec(memory_space=pltpu.VMEM)
    far = pl.BlockSpec(memory_space=pltpu.HBM)

    def run(*args):
        return pl.pallas_call(
            kernel,
            out_shape=out_shape,
            in_specs=[far if i in loaded else near for i in range(len(args))],
            out_specs=[far if i in saved else near for i in range(len(out_shape))]
            if isinstance(out_shape, list)
            else near,
            scratch_shapes=scratch,
            compiler_params=pltpu.CompilerParams(vmem_limit_bytes=limit << 20),
            cost_estimate=pl.CostEstimate(flops=flops, bytes_accessed=4 << 20, transcendentals=0),
        )(*args)

    return run


def on_device(sky, beam, observed, facet_of, tile_slot, conv_first, bias_first, conv_second):
    rows, cols = sky.shape
    beam = beam.reshape(rows, cols)
    facets = lax.axis_size("facet")
    count = lax.axis_size("freq")
    tiles, width = observed.shape
    cap = 2 * tiles // facets
    total = facets * cap
    slots = (rows // S) * (cols // S)
    hidden = conv_first.shape[0]
    row_f, twist_f, mat_f = tables(rows, cols, -1)
    row_b, twist_b, mat_b = tables(rows, cols, 1)

    deep = (width // LANES) * cap + 8
    send, dest = call(
        functools.partial(pack_kernel, facets, cap),
        [shape((facets, deep, LANES), BF16), shape((1, tiles), jnp.int32)],
        1 << 28,
        scratch=[
            pltpu.VMEM((1, tiles), jnp.int32),
            pltpu.VMEM((1, tiles), jnp.int32),
            pltpu.VMEM((tiles, width), BF16),
            pltpu.VMEM((facets, deep, LANES), BF16),
            pltpu.SemaphoreType.DMA((7,)),
        ],
        loaded=(0, 1, 2),
        saved=(0,),
    )(
        *(
            pltpu.with_memory_space_constraint(value, pltpu.HBM)
            for value in (facet_of.reshape(1, tiles), tile_slot.reshape(1, tiles), observed)
        )
    )
    got = lax.all_to_all(send, "facet", split_axis=0, concat_axis=0, tiled=True)

    high, low, first, second, placed, edge_first, edge_second = call(
        forward_kernel,
        [
            shape((width, slots), BF16),
            shape((width, slots), BF16),
            shape((hidden * BAND, 9 * (BAND + 2) + 8), BF16),
            shape((6 * (BAND + 2), hidden * BAND), BF16),
            shape((tiles, total), BF16),
            shape((2 * hidden, 80), BF16),
            shape((6 * (BAND + 2), 2 * hidden), BF16),
        ],
        1 << 30,
        scratch=[pltpu.VMEM((2, width, slots), BF16)],
    )(
        sky,
        beam,
        row_f,
        twist_f,
        mat_f,
        conv_first.transpose(1, 2, 0),
        bias_first.reshape(1, hidden),
        conv_second.transpose(1, 2, 0),
        dest,
    )

    residual, select, own = call(
        functools.partial(residual_kernel, facets, cap),
        [shape((total, width), BF16), shape((total, slots), BF16), shape((total, width), BF16)],
        1 << 30,
        scratch=[pltpu.SemaphoreType.DMA((2,))],
        saved=(0,),
    )(got, *(pltpu.with_memory_space_constraint(value, pltpu.VMEM) for value in (high, low)))
    returned = lax.all_to_all(
        residual.reshape(facets, cap, width), "facet", split_axis=0, concat_axis=0, tiled=True
    ).reshape(total, width)

    _, wide = window(0, count, cols)
    keep, *sends = call(
        functools.partial(inverse_kernel, count),
        [shape((rows, wide), F32)] + [shape((rows, wide), BF16)] * (count - 1),
        1 << 30,
        scratch=[
            pltpu.VMEM((rows, wide), F32),
            pltpu.VMEM((rows, cols), F32),
            pltpu.VMEM((4 * rows, cols), BF16),
            pltpu.VMEM((rows, cols), F32),
            pltpu.VMEM((rows // S, width, LANES), F32),
            pltpu.SemaphoreType.DMA((2,)),
        ],
        loaded=(5, 6),
    )(
        own,
        select,
        row_b,
        twist_b,
        mat_b,
        *(pltpu.with_memory_space_constraint(value, pltpu.HBM) for value in (sky, beam)),
    )

    def beside(value, to):
        pairs = [(p, to(p)) for p in range(facets) if 0 <= to(p) < facets]
        return lax.ppermute(value, "facet", pairs)

    gots = [
        lax.ppermute(value, "freq", [(f, (f + d + 1) % count) for f in range(count)])
        for d, value in enumerate(sends)
    ]
    main, near, far = call(
        sum_kernel,
        [shape((rows, wide), F32), shape((2, wide), F32), shape((2, wide), F32)],
        1 << 24,
    )(keep, *gots)
    far = beside(far, lambda p: p + 1 if p & 1 else p - 1)
    near = beside(near, lambda p: p ^ 1)
    tall_rows = pltpu.VMEM((rows + 16, wide), F32)
    partial = call(
        prior_kernel, shape((rows + 16, wide), F32), 1 << 31, scratch=[tall_rows], limit=32
    )(main, near, first, second)
    image, tiles_out = call(
        functools.partial(edge_kernel, count, cols // count),
        [shape((rows, cols // count), F32), shape((tiles, width), BF16)],
        1 << 30,
        scratch=[
            pltpu.VMEM((16, wide), F32),
            pltpu.VMEM((BAND + 10, wide), F32),
            pltpu.VMEM((8, wide), F32),
            pltpu.VMEM((tiles, width), BF16),
            pltpu.SemaphoreType.DMA((3,)),
        ],
        saved=(0, 1),
    )(partial, main, far, edge_first, edge_second, placed, returned)
    return tiles_out, image


def solution(mesh):
    placed = (
        P("facet", None),
        P("freq", "facet", None),
        P(("freq", "facet"), None),
        P(("freq", "facet")),
        P(("freq", "facet")),
        P(),
        P(),
        P(),
    )

    return jax.shard_map(
        on_device,
        mesh=mesh,
        in_specs=placed,
        out_specs=(P(("freq", "facet"), None), P("facet", "freq")),
        check_vma=False,
    )
```

```python
import functools
import math

import jax
import jax.numpy as jnp
import numpy as np
from jax import lax
from jax.experimental import pallas as pl
from jax.experimental.pallas import tpu as pltpu
from jax.sharding import PartitionSpec as P


S = 16
LANES = 128
BAND = 22
STEP = 0.5
F32 = jnp.float32
BF16 = jnp.bfloat16


def iota(shape, dim):
    return lax.broadcasted_iota(jnp.int32, shape, dim)


def mm(a, b, dims=((1,), (0,))):
    return lax.dot_general(a, b, (dims, ((), ())), preferred_element_type=F32)


def one_hot(cond):
    return jnp.where(cond, 1.0, 0.0).astype(BF16)


def split(x):
    high = x.astype(BF16)
    return high, (x - high.astype(F32)).astype(BF16)


def np_split(x):
    x = np.asarray(x, np.float32)
    high = x.astype(BF16)
    return high, (x - high.astype(np.float32)).astype(BF16)


def tables(rows, cols, sign):
    outer = cols // LANES
    scale = 1.0 / math.sqrt(rows * cols)
    k = np.arange(rows)
    angle = sign * 2.0 * np.pi * ((k[:, None] * k[None, :]) % rows) / rows
    cos_r, sin_r = np.cos(angle) * scale, np.sin(angle) * scale
    if sign < 0:
        row_high, row_low = np_split(np.concatenate([cos_r, sin_r], 0))
        row = np.concatenate([row_high, row_high, row_low], 1)
    else:
        row = np.concatenate(np_split(np.concatenate([cos_r, -sin_r], 1)), 1)
    i2 = np.arange(LANES)
    w = np.arange(outer)
    twist = sign * 2.0 * np.pi * ((w[:, None] * i2[None, :]) % cols) / cols
    inner = sign * 2.0 * np.pi * ((i2[:, None] * i2[None, :]) % LANES) / LANES
    c, s = np.cos(inner), np.sin(inner)
    mat_high, mat_low = np_split(np.block([[c, s], [-s, c]]))
    return (
        row,
        np.stack([np.cos(twist), np.sin(twist)]).astype(np.float32),
        np.stack([mat_high, mat_low]),
    )


def times_i(z, sign):
    re, im = z
    return (-im, re) if sign > 0 else (im, -re)


def add(a, b):
    return (a[0] + b[0], a[1] + b[1])


def sub(a, b):
    return (a[0] - b[0], a[1] - b[1])


def dft4(x, sign):
    s0, s1 = add(x[0], x[2]), sub(x[0], x[2])
    s2, s3 = add(x[1], x[3]), times_i(sub(x[1], x[3]), sign)
    return [add(s0, s2), add(s1, s3), sub(s0, s2), sub(s1, s3)]


def dft16(x, sign):
    mid = [dft4([x[4 * a + b] for a in range(4)], sign) for b in range(4)]
    out = [None] * 16
    for c in range(4):
        turned = []
        for b in range(4):
            re, im = mid[b][c]
            phase = (b * c) % 16
            if phase == 0:
                turned.append((re, im))
            elif phase == 4:
                turned.append(times_i((re, im), sign))
            else:
                wr = math.cos(2.0 * math.pi * phase / 16)
                wi = sign * math.sin(2.0 * math.pi * phase / 16)
                turned.append((re * wr - im * wi, re * wi + im * wr))
        for d, value in enumerate(dft4(turned, sign)):
            out[c + 4 * d] = value
    return out


def swap_matrix(size):
    src = iota((1, size), 1)
    swapped = (src & -256) | ((src & 15) << 4) | ((src >> 4) & 15)
    return one_hot(iota((size, size), 0) == swapped)


def pack_kernel(
    facets,
    cap,
    facet_hbm,
    slot_hbm,
    seen_hbm,
    send_hbm,
    dest_ref,
    facet_ref,
    slot_ref,
    seen_ref,
    send_ref,
    sems,
):
    tiles, width = seen_ref.shape
    total = facets * cap
    loads = [
        pltpu.make_async_copy(src, dst, sems.at[i])
        for i, (src, dst) in enumerate(
            ((facet_hbm, facet_ref), (slot_hbm, slot_ref), (seen_hbm, seen_ref))
        )
    ]
    for load in loads:
        load.start()
    before = one_hot(iota((tiles, tiles), 0) < iota((tiles, tiles), 1))
    loads[0].wait()
    facet = facet_ref[...]
    member = iota((facets, tiles), 0) == facet
    member_f = jnp.where(member, 1.0, 0.0)
    ranks = mm(member_f.astype(BF16), before)
    rank = jnp.sum(member_f * ranks, axis=0, keepdims=True).astype(jnp.int32)
    dest = facet * cap + rank
    dest_ref[...] = dest
    loads[1].wait()
    code = slot_ref[...] + 1
    lane = iota((LANES, tiles), 0)
    slots = mm(
        (member_f * (code >> 4).astype(F32)).astype(BF16), one_hot(lane == rank), ((1,), (1,))
    ) + mm(
        (member_f * (code & 15).astype(F32)).astype(BF16),
        one_hot(lane - LANES // 2 == rank),
        ((1,), (1,)),
    )
    parts = width // LANES
    groups = 8
    here = facets // groups
    loads[2].wait()
    saves = []
    for g in range(groups):
        placing = one_hot(iota((total // groups, tiles), 0) + g * (total // groups) == dest)
        packed = mm(placing, seen_ref[...]).astype(BF16)
        for i in range(here):
            d = g * here + i
            for part in range(parts):
                send_ref[d, part * cap : (part + 1) * cap, :] = packed[
                    i * cap : (i + 1) * cap, part * LANES : (part + 1) * LANES
                ]
            send_ref[d, parts * cap : parts * cap + 8, :] = jnp.broadcast_to(
                slots[d : d + 1, :], (8, LANES)
            ).astype(BF16)
        span = pl.ds(g * here, here)
        save = pltpu.make_async_copy(send_ref.at[span], send_hbm.at[span], sems.at[3 + g])
        save.start()
        saves.append(save)
    for save in saves:
        save.wait()


def forward_kernel(
    sky_ref,
    beam_ref,
    row_ref,
    twist_ref,
    mat_ref,
    first_ref,
    bias_ref,
    second_ref,
    dest_ref,
    high_ref,
    low_ref,
    one_ref,
    two_ref,
    place_ref,
    edge_one_ref,
    edge_two_ref,
    part_ref,
):
    spots = iota(place_ref.shape[::-1], 0)
    place_ref[...] = jnp.where(spots == dest_ref[...], 1.0, 0.0).T.astype(BF16)
    prepare(first_ref, bias_ref, second_ref, one_ref, two_ref)
    pair, narrow = edge_one_ref.shape
    height, depth = one_ref.shape
    even = (lax.axis_index("facet") & 1) == 0
    table = jnp.where(
        even, one_ref[:pair, :].astype(F32), one_ref[height - pair :, :].astype(F32)
    ).astype(BF16)
    lane = iota((depth, narrow), 1)
    column = (lane >> 3) * (BAND + 2) + (lane & 7)
    column = column + jnp.where(even | (lane >= narrow - 8), 0, BAND - 6)
    edge_one_ref[...] = mm(table, one_hot(iota((depth, narrow), 0) == column)).astype(BF16)
    edge_two_ref[...] = jnp.where(
        even, two_ref[:, :pair].astype(F32), two_ref[:, height - pair :].astype(F32)
    ).astype(BF16)
    rows, cols = sky_ref.shape
    outer = cols // LANES
    weighted = sky_ref[...] * beam_ref[...]
    w_high, w_low = split(weighted)
    mid = mm(row_ref[...], jnp.concatenate([w_high, w_low, w_high], axis=0))
    lines = [
        (
            mid[:rows, i * LANES : (i + 1) * LANES],
            mid[rows:, i * LANES : (i + 1) * LANES],
        )
        for i in range(outer)
    ]
    spread = dft16(lines, -1)
    blocks = []
    for w in range(outer):
        re, im = spread[w]
        tr, ti = twist_ref[0, w : w + 1, :], twist_ref[1, w : w + 1, :]
        blocks.append(jnp.concatenate([re * tr - im * ti, re * ti + im * tr], axis=1))
    high, low = split(jnp.concatenate(blocks, axis=0))
    mat_high, mat_low = mat_ref[0], mat_ref[1]
    model = mm(high, mat_high) + mm(low, mat_high) + mm(high, mat_low)
    for w in range(outer):
        for r in range(rows // S):
            for e in range(2):
                piece = model[
                    w * rows + r * S : w * rows + (r + 1) * S, e * LANES : (e + 1) * LANES
                ]
                piece_high, piece_low = split(piece)
                at = (pl.ds(e * 256 + w * S, S), pl.ds(r * LANES, LANES))
                part_ref[(0,) + at] = piece_high
                part_ref[(1,) + at] = piece_low
    swap = swap_matrix(high_ref.shape[0])
    high_ref[...] = mm(swap, part_ref[0]).astype(BF16)
    low_ref[...] = mm(swap, part_ref[1]).astype(BF16)


def residual_kernel(facets, cap, got_ref, high_ref, low_ref, res_hbm, sel_ref, own_ref, sems):
    slots = high_ref.shape[1]
    parts = high_ref.shape[0] // LANES
    pieces = sems.shape[0]
    here = facets // pieces
    count = here * cap
    contract = ((1,), (1,))
    lane = iota((count, LANES), 1)
    rank = iota((count, LANES), 0) % cap
    mine = (lane & (LANES // 2 - 1)) == rank
    digit = jnp.where(iota((LANES, LANES), 0) < LANES // 2, 16.0, 1.0).astype(BF16)
    saves = []
    for i in range(pieces):
        group = slice(i * here, (i + 1) * here)
        at = slice(i * count, (i + 1) * count)
        code = got_ref[group, parts * cap : parts * cap + 8, :].astype(F32)
        code = jnp.broadcast_to(code[:, 0:1, :], (here, cap, LANES)).reshape(count, LANES)
        slot = mm(jnp.where(mine, code, 0.0).astype(BF16), digit).astype(jnp.int32) - 1
        sel = jnp.concatenate(
            [one_hot(slot == lane + r * LANES) for r in range(slots // LANES)], axis=1
        )
        sel_ref[at, :] = sel
        predicted = mm(sel, high_ref[...], contract) + mm(sel, low_ref[...], contract)
        for part in range(parts):
            cols = slice(part * LANES, (part + 1) * LANES)
            seen = got_ref[group, part * cap : (part + 1) * cap, :]
            seen = seen.astype(F32).reshape(count, LANES)
            own_ref[at, cols] = (predicted[:, cols] - seen).astype(BF16)
        save = pltpu.make_async_copy(own_ref.at[at, :], res_hbm.at[at, :], sems.at[i])
        save.start()
        saves.append(save)
    for save in saves:
        save.wait()


def window(index, count, cols):
    part = cols // count
    width = min(cols, part + (LANES if count == 2 else 2 * LANES))
    return jnp.clip(index * part - LANES, 0, cols - width), width


def inverse_kernel(
    count,
    res_ref,
    sel_ref,
    row_ref,
    twist_ref,
    mat_ref,
    sky_hbm,
    beam_hbm,
    keep_ref,
    *rest,
):
    send_refs = rest[: count - 1]
    sky_ref, beam_ref, lines_ref, shift_ref, grid_ref, sems = rest[count - 1 :]
    rows, cols = beam_ref.shape
    outer = cols // LANES
    me = lax.axis_index("freq")
    start, width = window(me, count, cols)
    sky_part = sky_hbm.at[:, pl.ds(pl.multiple_of(start, LANES), width)]
    loads = [
        pltpu.make_async_copy(beam_hbm, beam_ref, sems.at[0]),
        pltpu.make_async_copy(sky_part, sky_ref, sems.at[1]),
    ]
    for load in loads:
        load.start()
    grid = mm(res_ref[...], sel_ref[...], ((0,), (0,)))
    for r in range(rows // S):
        grid_ref[r] = grid[:, r * LANES : (r + 1) * LANES]
    blocks = []
    for w in range(outer):
        blocks.append(
            jnp.concatenate(
                [
                    jnp.concatenate(
                        [
                            grid_ref[r, pl.ds(e * S * S + w, S, stride=S), :]
                            for e in range(2)
                        ],
                        axis=1,
                    )
                    for r in range(rows // S)
                ],
                axis=0,
            )
        )
    cells = jnp.concatenate(blocks, axis=0).astype(BF16)
    mid = mm(jnp.concatenate([cells, cells], axis=1), mat_ref[...].reshape(4 * LANES, 2 * LANES))
    lines = []
    for w in range(outer):
        re = mid[w * rows : (w + 1) * rows, :LANES]
        im = mid[w * rows : (w + 1) * rows, LANES:]
        tr, ti = twist_ref[0, w : w + 1, :], twist_ref[1, w : w + 1, :]
        lines.append((re * tr - im * ti, re * ti + im * tr))
    spread = dft16(lines, 1)
    for i, pair in enumerate(spread):
        for e in range(2):
            line = pair[e].astype(BF16)
            lines_ref[e * rows : (e + 1) * rows, i * LANES : (i + 1) * LANES] = line
            lines_ref[(2 + e) * rows : (3 + e) * rows, i * LANES : (i + 1) * LANES] = line
    back = mm(row_ref[...], lines_ref[...])
    for load in loads:
        load.wait()
    shift_ref[...] = back * beam_ref[...] * (-STEP)
    for d in range(count):
        start, width = window(lax.rem(me + d, count), count, cols)
        at = pl.ds(pl.multiple_of(start, LANES), width)
        if d == 0:
            keep_ref[...] = shift_ref[:, at] + sky_ref[...]
        else:
            send_refs[d - 1][...] = shift_ref[:, at].astype(BF16)


def sum_kernel(keep_ref, *refs):
    main_ref, near_ref, far_ref = refs[-3:]
    rows = keep_ref.shape[0]
    main = keep_ref[...]
    for ref in refs[:-3]:
        main = main + ref[...].astype(F32)
    main_ref[...] = main
    even = (lax.axis_index("facet") & 1) == 0
    top, bottom = main[0:2], main[rows - 2 : rows]
    near_ref[...] = jnp.where(even, bottom, top)
    far_ref[...] = jnp.where(even, top, bottom)


def prepare(first_ref, bias_ref, second_ref, one_ref, two_ref):
    hidden = first_ref.shape[2]
    depth = one_ref.shape[1]
    full = (BAND + 2) * 9
    bias_high, bias_low = split(bias_ref[...])
    line = iota((8, depth), 0)
    lane = iota((8, depth), 1)
    group = lane * 2731 >> 16
    term = group * 86 >> 8
    col = group - term * 3
    taps = one_hot(((line == col) & (term < 2)) | ((line - 3 == col) & (term == 2)))
    ends = one_hot(((line == 6) & (lane == full)) | ((line == 7) & (lane == full + 1)))
    values = []
    for a in range(3):
        high, low = split(first_ref[a])
        pieces = [high, low, bias_high, bias_low]
        weights = jnp.concatenate([p.astype(F32) for p in pieces], axis=0).astype(BF16)
        values.append(mm(weights, taps, ((0,), (0,))))
        if a == 0:
            offset = mm(weights, ends, ((0,), (0,)))
    lane = iota((hidden, depth), 1)
    yin = lane - (lane * 2731 >> 16) * (BAND + 2)
    for y in range(BAND):
        block = offset
        for a in range(3):
            block = block + jnp.where(yin == y + a, values[a], 0.0)
        one_ref[y * hidden : (y + 1) * hidden, :] = block.astype(BF16)

    wide = two_ref.shape[1]
    tall = BAND + 2
    expand = one_hot(iota((hidden, wide), 0) == (iota((hidden, wide), 1) & (hidden - 1)))
    pieces = [split(second_ref[a]) for a in range(3)]
    gap = iota((tall, wide), 1) // hidden + 2 - iota((tall, wide), 0)
    blocks = []
    for half in range(2):
        lines = [mm(pieces[a][half], expand) for a in range(3)]
        for b in range(3):
            total = jnp.zeros((tall, wide), F32)
            for a in range(3):
                total = jnp.where(gap == a, lines[a][b : b + 1, :], total)
            blocks.append(total)
    two_ref[...] = jnp.concatenate(blocks, axis=0).astype(BF16)


def moved(value):
    width = value.shape[1]
    lane = iota(value.shape, 1)
    return (
        jnp.where(lane == 0, 0.0, pltpu.roll(value, 1, 1)),
        jnp.where(lane == width - 1, 0.0, pltpu.roll(value, width - 1, 1)),
    )


def stack_of(band):
    ones = jnp.where(iota((8, band.shape[1]), 0) < 2, 1.0, 0.0)
    high = band.astype(BF16).astype(F32)
    shifted = []
    for value in (high, band - high):
        left, right = moved(value)
        shifted.append([left, value, right])
    return jnp.concatenate(shifted[0] + shifted[1] + shifted[0] + [ones], axis=0).astype(BF16)


def share_of(taps):
    tall = BAND + 2
    parts = [
        taps[b * tall : (b + 1) * tall] + taps[(3 + b) * tall : (4 + b) * tall] for b in range(3)
    ]
    return parts[1] + moved(parts[0])[0] + moved(parts[2])[1]


def prior_kernel(main_ref, near_ref, one_ref, two_ref, sum_ref, base_ref):
    rows, width = main_ref.shape
    tall = BAND + 2
    pair = 2 * one_ref.shape[0] // BAND
    main, near = main_ref[...], near_ref[...]
    even = (lax.axis_index("facet") & 1) == 0
    base_ref[8 : rows + 8, :] = main
    base_ref[6:8, :] = jnp.where(even, 0.0, near)
    base_ref[rows + 8 : rows + 10, :] = jnp.where(even, near, 0.0)
    sum_ref[0:8, :] = jnp.zeros((8, width), F32)
    sum_ref[8 : rows + 8, :] = main
    sum_ref[rows + 8 :, :] = jnp.zeros((8, width), F32)
    spots = [slice(k * BAND + 6, k * BAND + 6 + tall) for k in range((rows + 2) // BAND)]
    stack = jnp.concatenate([stack_of(base_ref[spot, :]) for spot in spots], axis=1)
    hidden = jnp.maximum(mm(one_ref[...], stack), 0.0)
    head, body, foot = hidden[:pair], hidden[pair:-pair], hidden[-pair:]
    head = jnp.concatenate([jnp.where(even, 0.0, head[:, :width]), head[:, width:]], axis=1)
    foot = jnp.concatenate([foot[:, :-width], jnp.where(even, foot[:, -width:], 0.0)], axis=1)
    hidden = jnp.concatenate([head, body, foot], axis=0).astype(BF16)
    taps = mm(two_ref[...], hidden)
    for k, spot in enumerate(spots):
        sum_ref[spot, :] = sum_ref[spot, :] + share_of(taps[:, k * width : (k + 1) * width])


def edge_kernel(
    count,
    part,
    sum_ref,
    main_ref,
    far_ref,
    one_ref,
    two_ref,
    place_ref,
    back_ref,
    out_hbm,
    tiles_hbm,
    base_ref,
    share_ref,
    last_ref,
    tiles_ref,
    sems,
):
    rows, width = main_ref.shape
    tall = BAND + 2
    inner = one_ref.shape[0] // 2
    place = lax.axis_index("facet")
    final = lax.axis_size("facet") - 1
    even = (place & 1) == 0
    me = lax.axis_index("freq")
    start, _ = window(me, count, part * count)
    at = pl.ds(pl.multiple_of(me * part - start, LANES), part)
    done = rows - 8
    first = pl.multiple_of(jnp.where(even, 8, 0), 8)
    early = pltpu.make_async_copy(
        sum_ref.at[pl.ds(pl.multiple_of(first + 8, 8), done), at],
        out_hbm.at[pl.ds(first, done), :],
        sems.at[0],
    )
    early.start()
    half = tiles_ref.shape[0] // 2
    tiles = []
    for i in range(2):
        here = slice(i * half, (i + 1) * half)
        tiles_ref[here, :] = mm(place_ref[here, :], back_ref[...]).astype(BF16)
        save = pltpu.make_async_copy(tiles_ref.at[here, :], tiles_hbm.at[here, :], sems.at[2 + i])
        save.start()
        tiles.append(save)
    far = far_ref[...]
    base_ref[0:2, :] = far
    base_ref[2:8, :] = main_ref[0:6, :]
    base_ref[8:14, :] = main_ref[rows - 6 : rows, :]
    base_ref[14:16, :] = far
    band = jnp.where(even, base_ref[0:8, :], base_ref[8:16, :])
    hidden = jnp.maximum(mm(one_ref[...], stack_of(band)), 0.0)
    hidden = jnp.concatenate(
        [
            jnp.where(place == 0, 0.0, hidden[:inner]),
            jnp.where(place == final, 0.0, hidden[inner:]),
        ],
        axis=0,
    )
    share_ref[0:8, :] = jnp.zeros((8, width), F32)
    share_ref[8 : tall + 8, :] = share_of(mm(two_ref[...], hidden.astype(BF16)))
    near_sum = jnp.where(even, sum_ref[8:16, :], sum_ref[rows : rows + 8, :])
    share = jnp.where(even, share_ref[10:18, :], share_ref[tall - 2 : tall + 6, :])
    last_ref[...] = near_sum + share
    late = pltpu.make_async_copy(
        last_ref.at[:, at],
        out_hbm.at[pl.ds(pl.multiple_of(jnp.where(even, 0, done), 8), 8), :],
        sems.at[1],
    )
    late.start()
    early.wait()
    for save in tiles:
        save.wait()
    late.wait()


def shape(dims, dtype):
    return jax.ShapeDtypeStruct(dims, dtype)


def call(kernel, out_shape, flops, scratch=(), loaded=(), saved=(), limit=16):
    near = pl.BlockSpec(memory_space=pltpu.VMEM)
    far = pl.BlockSpec(memory_space=pltpu.HBM)

    def run(*args):
        return pl.pallas_call(
            kernel,
            out_shape=out_shape,
            in_specs=[far if i in loaded else near for i in range(len(args))],
            out_specs=[far if i in saved else near for i in range(len(out_shape))]
            if isinstance(out_shape, list)
            else near,
            scratch_shapes=scratch,
            compiler_params=pltpu.CompilerParams(vmem_limit_bytes=limit << 20),
            cost_estimate=pl.CostEstimate(flops=flops, bytes_accessed=4 << 20, transcendentals=0),
        )(*args)

    return run


def on_device(sky, beam, observed, facet_of, tile_slot, conv_first, bias_first, conv_second):
    rows, cols = sky.shape
    beam = beam.reshape(rows, cols)
    facets = lax.axis_size("facet")
    count = lax.axis_size("freq")
    tiles, width = observed.shape
    cap = 2 * tiles // facets
    total = facets * cap
    slots = (rows // S) * (cols // S)
    hidden = conv_first.shape[0]
    row_f, twist_f, mat_f = tables(rows, cols, -1)
    row_b, twist_b, mat_b = tables(rows, cols, 1)

    deep = (width // LANES) * cap + 8
    send, dest = call(
        functools.partial(pack_kernel, facets, cap),
        [shape((facets, deep, LANES), BF16), shape((1, tiles), jnp.int32)],
        1 << 28,
        scratch=[
            pltpu.VMEM((1, tiles), jnp.int32),
            pltpu.VMEM((1, tiles), jnp.int32),
            pltpu.VMEM((tiles, width), BF16),
            pltpu.VMEM((facets, deep, LANES), BF16),
            pltpu.SemaphoreType.DMA((11,)),
        ],
        loaded=(0, 1, 2),
        saved=(0,),
    )(
        *(
            pltpu.with_memory_space_constraint(value, pltpu.HBM)
            for value in (facet_of.reshape(1, tiles), tile_slot.reshape(1, tiles), observed)
        )
    )
    got = lax.all_to_all(send, "facet", split_axis=0, concat_axis=0, tiled=True)

    high, low, first, second, placed, edge_first, edge_second = call(
        forward_kernel,
        [
            shape((width, slots), BF16),
            shape((width, slots), BF16),
            shape((hidden * BAND, 9 * (BAND + 2) + 8), BF16),
            shape((6 * (BAND + 2), hidden * BAND), BF16),
            shape((tiles, total), BF16),
            shape((2 * hidden, 80), BF16),
            shape((6 * (BAND + 2), 2 * hidden), BF16),
        ],
        1 << 30,
        scratch=[pltpu.VMEM((2, width, slots), BF16)],
    )(
        sky,
        beam,
        row_f,
        twist_f,
        mat_f,
        conv_first.transpose(1, 2, 0),
        bias_first.reshape(1, hidden),
        conv_second.transpose(1, 2, 0),
        dest,
    )

    residual, select, own = call(
        functools.partial(residual_kernel, facets, cap),
        [shape((total, width), BF16), shape((total, slots), BF16), shape((total, width), BF16)],
        1 << 30,
        scratch=[pltpu.SemaphoreType.DMA((2,))],
        saved=(0,),
    )(got, *(pltpu.with_memory_space_constraint(value, pltpu.VMEM) for value in (high, low)))
    returned = lax.all_to_all(
        residual.reshape(facets, cap, width), "facet", split_axis=0, concat_axis=0, tiled=True
    ).reshape(total, width)

    _, wide = window(0, count, cols)
    keep, *sends = call(
        functools.partial(inverse_kernel, count),
        [shape((rows, wide), F32)] + [shape((rows, wide), BF16)] * (count - 1),
        1 << 30,
        scratch=[
            pltpu.VMEM((rows, wide), F32),
            pltpu.VMEM((rows, cols), F32),
            pltpu.VMEM((4 * rows, cols), BF16),
            pltpu.VMEM((rows, cols), F32),
            pltpu.VMEM((rows // S, width, LANES), F32),
            pltpu.SemaphoreType.DMA((2,)),
        ],
        loaded=(5, 6),
    )(
        own,
        select,
        row_b,
        twist_b,
        mat_b,
        *(pltpu.with_memory_space_constraint(value, pltpu.HBM) for value in (sky, beam)),
    )

    def beside(value, to):
        pairs = [(p, to(p)) for p in range(facets) if 0 <= to(p) < facets]
        return lax.ppermute(value, "facet", pairs)

    gots = [
        lax.ppermute(value, "freq", [(f, (f + d + 1) % count) for f in range(count)])
        for d, value in enumerate(sends)
    ]
    main, near, far = call(
        sum_kernel,
        [shape((rows, wide), F32), shape((2, wide), F32), shape((2, wide), F32)],
        1 << 24,
    )(keep, *gots)
    far = beside(far, lambda p: p + 1 if p & 1 else p - 1)
    near = beside(near, lambda p: p ^ 1)
    tall_rows = pltpu.VMEM((rows + 16, wide), F32)
    partial = call(
        prior_kernel, shape((rows + 16, wide), F32), 1 << 31, scratch=[tall_rows], limit=32
    )(main, near, first, second)
    image, tiles_out = call(
        functools.partial(edge_kernel, count, cols // count),
        [shape((rows, cols // count), F32), shape((tiles, width), BF16)],
        1 << 30,
        scratch=[
            pltpu.VMEM((16, wide), F32),
            pltpu.VMEM((BAND + 10, wide), F32),
            pltpu.VMEM((8, wide), F32),
            pltpu.VMEM((tiles, width), BF16),
            pltpu.SemaphoreType.DMA((4,)),
        ],
        saved=(0, 1),
    )(partial, main, far, edge_first, edge_second, placed, returned)
    return tiles_out, image


def solution(mesh):
    placed = (
        P("facet", None),
        P("freq", "facet", None),
        P(("freq", "facet"), None),
        P(("freq", "facet")),
        P(("freq", "facet")),
        P(),
        P(),
        P(),
    )

    return jax.shard_map(
        on_device,
        mesh=mesh,
        in_specs=placed,
        out_specs=(P(("freq", "facet"), None), P("facet", "freq")),
        check_vma=False,
    )
```
